256 devices in a mesh: row: 4 (over x), col: 16 (over y_hi, z), pair: 4 (over y_lo, core).
Axes of the slice: x: 4, y: 4 (y_hi: 2, y_lo: 2; y = y_hi * 2 + y_lo), z: 8, core: 2. Of those that a mesh axis runs over, the one named last changes fastest.
Arguments:
- frames: bfloat16 [4, 2, 64, 512, 256], P('pair', None, 'row', 'col'), may hold values from -6 to 6
- offsets: int32 [4, 2, 16, 2], P('pair'), may hold values from -8 to 8, as said below
- weight: bfloat16 [3, 3, 256, 256], replicated, may hold values from -0.125 to 0.125
- bias: float32 [256], replicated, may hold values from -3 to 3
- cotangent: bfloat16 [4, 81, 64, 512], P('pair', None, 'row', 'col'), may hold values from -0.023925781 to 0.023925781
Outputs:
- corr: bfloat16 [4, 81, 64, 512], P('pair', None, 'row', 'col')
- grad_weight: float32 [3, 3, 256, 256], replicated
- grad_bias: float32 [256], replicated
The draws below stay inside these ranges and needn't reach their ends.
Inputs may be any that keep to these rules, and one draw needn't show every extreme that they name: `offsets`: entry [.., 0] shifts rows and [.., 1] columns of one 32 x 32 block; both ends of the range occur in every draw.
All inputs are finite; a program needn't handle non-finite values.
Results may differ from the reference program's by a relative error of at most 0.0046.
Values may be sent and summed in bfloat16 or wider, within the bound.
No kernel may reach another device: no remote copies, remote signals or barrier semaphores. Data moves between devices by JAX's collectives and lax.ppermute only.
A program may use at most 64 MiB of HBM per device.

```python
import jax
import jax.numpy as jnp
from jax import lax

CH = 256
BLK = 32
RAD = 4
MAXOFF = 8
DISP = 81
PAIRS = 4
H = 64
WD = 512


def draw_offsets(key, part):
    key_values = jax.random.fold_in(key, 11)
    key_first = jax.random.fold_in(key, 23)
    key_second = jax.random.fold_in(key, 37)
    blocks = H // BLK * (WD // BLK)
    drawn = jax.random.randint(key_values, (PAIRS, blocks, 2), -MAXOFF, MAXOFF + 1, dtype=jnp.int32)
    first_spot = jax.random.randint(key_first, (), 0, blocks, dtype=jnp.int32)
    second_spot = (first_spot + 1 + jax.random.randint(key_second, (), 0, blocks - 1, dtype=jnp.int32)) % blocks
    drawn = drawn.at[0, first_spot].set(jnp.array([-MAXOFF, MAXOFF], dtype=jnp.int32))
    drawn = drawn.at[0, second_spot].set(jnp.array([MAXOFF, -MAXOFF], dtype=jnp.int32))
    return drawn.reshape(PAIRS, H // BLK, WD // BLK, 2)


def steps_of(stream_key, dims, cuts, least, high):
    def one(dim, parts):
        steps = jax.random.uniform(jax.random.fold_in(jax.random.fold_in(stream_key, 6), dim), (parts,), jnp.float32, least / len(cuts), high / len(cuts))
        return jnp.repeat(jnp.exp(steps), dims[dim] // parts).reshape((-1,) + (1,) * (len(dims) - dim - 1))

    loudness = one(*cuts[0])
    for cut in cuts[1:]:
        loudness = loudness * one(*cut)
    return loudness


def scatter_about(own_key, extent, scale, most, split=(), held_as=jnp.bfloat16):
    entries = scale * jax.random.normal(own_key, extent, jnp.float32)
    if split:
        entries = entries * steps_of(own_key, extent, split, -0.22, 0.18)
    return jnp.clip(entries, -most, most).astype(held_as)


def setup_inputs(seed: int = 0) -> dict:
    seeds = jax.random.split(jax.random.key(seed), 6)
    return {
        "frames": scatter_about(seeds[0], (PAIRS, 2, H, WD, CH), 1.0, 6.0, ((0, 4), (2, 4), (3, 16))),
        "offsets": draw_offsets(jax.random.fold_in(seeds[5], 71), 0),
        "weight": scatter_about(seeds[2], (3, 3, CH, CH), (9 * CH) ** -0.5, 0.125),
        "bias": scatter_about(seeds[3], (CH,), 0.5, 3.0, (), jnp.float32),
        "cotangent": scatter_about(seeds[4], (PAIRS, DISP, H, WD), 0.004, 0.023925781, ((0, 4), (2, 4), (3, 16))),
    }


def band_take(scores):
    row_count, col_count, patch_width = scores.shape
    widened = jnp.pad(scores, ((0, 0), (0, 0), (0, 1)))
    flattened = widened.reshape(row_count, col_count * (patch_width + 1))
    flattened = jnp.pad(flattened, ((0, 0), (0, col_count)))
    return flattened.reshape(row_count, col_count, patch_width + 2)[:, :, :2 * RAD + 1]


def band_spread(bands, patch_width):
    row_count, col_count, window_size = bands.shape
    widened = jnp.pad(bands, ((0, 0), (0, 0), (0, patch_width + 2 - window_size)))
    flattened = widened.reshape(row_count, col_count * (patch_width + 2))[:, :col_count * (patch_width + 1)]
    return flattened.reshape(row_count, col_count, patch_width + 1)[:, :, :patch_width]


def block_scores(block_one, window_two):
    row_count, col_count = block_one.shape[0], block_one.shape[1]
    window_size = 2 * RAD + 1
    score_list = []
    for row_shift in range(window_size):
        scores = jnp.einsum("yxc,yzc->yxz", block_one.astype(jnp.float32), window_two[row_shift:row_shift + row_count].astype(jnp.float32), precision=lax.Precision.HIGHEST)
        score_list.append(band_take(scores))
    stacked = jnp.stack(score_list)
    return jnp.transpose(stacked, (0, 3, 1, 2)).reshape(window_size * window_size, row_count, col_count)


def block_grads(cot_block, block_one, window_two):
    row_count, col_count, channels = block_one.shape
    window_size = 2 * RAD + 1
    patch_width = col_count + 2 * RAD
    cot_grid = jnp.transpose(cot_block.reshape(window_size, window_size, row_count, col_count), (0, 2, 3, 1))
    grad_block = jnp.zeros((row_count, col_count, channels), jnp.float32)
    grad_window = jnp.zeros((row_count + 2 * RAD, patch_width, channels), jnp.float32)
    for row_shift in range(window_size):
        spread = band_spread(cot_grid[row_shift], patch_width).astype(jnp.float32)
        grad_block = grad_block + jnp.einsum("yxz,yzc->yxc", spread, window_two[row_shift:row_shift + row_count].astype(jnp.float32), precision=lax.Precision.HIGHEST)
        patch_term = jnp.einsum("yxz,yxc->yzc", spread, block_one.astype(jnp.float32), precision=lax.Precision.HIGHEST)
        grad_window = grad_window.at[row_shift:row_shift + row_count].add(patch_term)
    return grad_block, grad_window


def encode(image, weight, bias):
    conv_out = lax.conv_general_dilated(image[None], weight, (1, 1), "SAME", dimension_numbers=("NHWC", "HWIO", "NHWC"), preferred_element_type=jnp.float32)[0]
    return conv_out + bias


def weight_terms(image, delta):
    padded = jnp.pad(image, ((1, 1), (1, 1), (0, 0))).astype(jnp.float32)
    tap_list = []
    for tap_row in range(3):
        for tap_col in range(3):
            window = padded[tap_row:tap_row + H, tap_col:tap_col + WD]
            tap_list.append(jnp.einsum("yxc,yxd->cd", window, delta.astype(jnp.float32), precision=lax.Precision.HIGHEST))
    return jnp.stack(tap_list).reshape(3, 3, CH, CH)


def per_pair(inputs, weight, bias):
    frames_one, offsets_one, cotangent_first = inputs
    pre_one = encode(frames_one[0], weight, bias)
    pre_two = encode(frames_one[1], weight, bias)
    feat_one = jnp.maximum(pre_one, 0.0).astype(jnp.bfloat16)
    feat_two = jnp.maximum(pre_two, 0.0).astype(jnp.bfloat16)
    border_width = MAXOFF + RAD
    padded_two = jnp.pad(feat_two, ((border_width, border_width), (border_width, border_width), (0, 0)))
    block_cols = WD // BLK
    inv_root = CH ** -0.5

    def block_step(carried, block_index):
        grad_one, grad_two = carried
        block_row = block_index // block_cols
        block_col = block_index % block_cols
        shift_row = offsets_one[block_row, block_col, 0].astype(jnp.int32)
        shift_col = offsets_one[block_row, block_col, 1].astype(jnp.int32)
        block_top = (block_row * BLK).astype(jnp.int32)
        block_left = (block_col * BLK).astype(jnp.int32)
        zero_index = jnp.zeros((), jnp.int32)
        block_one = lax.dynamic_slice(feat_one, (block_top, block_left, zero_index), (BLK, BLK, CH))
        start = (block_top + shift_row + MAXOFF, block_left + shift_col + MAXOFF, zero_index)
        window_two = lax.dynamic_slice(padded_two, start, (BLK + 2 * RAD, BLK + 2 * RAD, CH))
        scores = block_scores(block_one, window_two) * inv_root
        cot_block = lax.dynamic_slice(cotangent_first, (zero_index, block_top, block_left), (DISP, BLK, BLK))
        grad_block, grad_window = block_grads(cot_block, block_one, window_two)
        grad_one = lax.dynamic_update_slice(grad_one, grad_block * inv_root, (block_top, block_left, zero_index))
        previous = lax.dynamic_slice(grad_two, start, grad_window.shape)
        grad_two = lax.dynamic_update_slice(grad_two, previous + grad_window * inv_root, start)
        return (grad_one, grad_two), scores.astype(jnp.bfloat16)

    carried = (jnp.zeros((H, WD, CH), jnp.float32), jnp.zeros((H + 2 * border_width, WD + 2 * border_width, CH), jnp.float32))
    blocks_all = (H // BLK) * block_cols
    (grad_one, gradient_second_padded), corr_blocks = lax.scan(block_step, carried, jnp.arange(blocks_all, dtype=jnp.int32))
    corr_one = jnp.transpose(corr_blocks.reshape(H // BLK, block_cols, DISP, BLK, BLK), (2, 0, 3, 1, 4)).reshape(DISP, H, WD)
    grad_two = gradient_second_padded[border_width:border_width + H, border_width:border_width + WD]
    delta_one = jnp.where(pre_one > 0, grad_one, 0.0).astype(jnp.bfloat16)
    delta_two = jnp.where(pre_two > 0, grad_two, 0.0)
    grad_w = weight_terms(frames_one[0], delta_one) + weight_terms(frames_one[1], delta_two)
    grad_b = jnp.sum(delta_one.astype(jnp.float32), axis=(0, 1)) + jnp.sum(delta_two, axis=(0, 1))
    return corr_one, grad_w, grad_b


def reference(frames, offsets, weight, bias, cotangent):
    corr, grad_w, grad_b = lax.map(lambda inputs: per_pair(inputs, weight, bias), (frames, offsets, cotangent))
    return corr, jnp.sum(grad_w, axis=0), jnp.sum(grad_b, axis=0)
```

```python
import functools

import jax
import jax.numpy as jnp
import numpy as np
from jax import lax
from jax.experimental import pallas as pl
from jax.experimental.pallas import tpu as pltpu
from jax.sharding import Mesh
from jax.sharding import PartitionSpec as P

BLK = 32
RAD = 4
MAXOFF = 8
WIN = 2 * RAD + 1
HALO = MAXOFF + RAD + 1
PITCH = 48
WROWS = 24
WCOLS = 40
GROUP = 4
GROWS = GROUP + WIN - 1
BF = jnp.bfloat16
F32 = jnp.float32


def vmem(n):
    return [pl.BlockSpec(memory_space=pltpu.VMEM)] * n


def params():
    return pltpu.CompilerParams(vmem_limit_bytes=48 * 1024 * 1024)


def pack_kernel(frames, up, down, left, right, ul, ur, dl, dr):
    rows, cols = frames.shape[1], frames.shape[2]
    up[0:HALO] = frames[1, 0:HALO]
    up[HALO] = frames[0, 0]
    down[0:HALO] = frames[1, rows - HALO : rows]
    down[HALO] = frames[0, rows - 1]
    col = lax.broadcasted_iota(jnp.int32, (rows, 16, frames.shape[3]), 1)
    first = frames[0, :, 0:16].astype(F32)[:, 0:1]
    last = frames[0, :, cols - 16 : cols].astype(F32)[:, 15:16]
    a = jnp.where(col == 15, first, frames[1, :, 0:16].astype(F32)).astype(BF)
    b = jnp.where(col == 0, last, frames[1, :, cols - 16 : cols].astype(F32)).astype(BF)
    left[...] = a
    right[...] = b
    ul[...] = a[0:HALO]
    dl[...] = a[rows - HALO :]
    ur[...] = b[0:HALO]
    dr[...] = b[rows - HALO :]


def pack(frames):
    rows, cols, ch = frames.shape[1:]
    row = jax.ShapeDtypeStruct((HALO + 1, cols, ch), BF)
    col = jax.ShapeDtypeStruct((rows, 16, ch), BF)
    corner = jax.ShapeDtypeStruct((HALO, 16, ch), BF)
    return pl.pallas_call(
        pack_kernel,
        out_shape=(row, row, col, col, corner, corner, corner, corner),
        in_specs=vmem(1),
        out_specs=tuple(vmem(8)),
        compiler_params=params(),
        name="pack",
    )(frames)


def band_kernel(cot, bt, b):
    lanes = GROUP * BLK
    lane = lax.broadcasted_iota(jnp.int32, (PITCH, lanes), 1)
    wcol = lax.broadcasted_iota(jnp.int32, (PITCH, lanes), 0)
    gap = wcol - lane % BLK
    own = lax.broadcasted_iota(jnp.int32, (16, lanes), 1) // BLK
    for g in range(bt.shape[0]):
        for r in range(GROWS):
            pick = jnp.zeros((16, lanes), F32)
            for yy in range(GROUP):
                a = r - yy
                if 0 <= a < WIN:
                    part = cot[a * 16 : (a + 1) * 16, g * lanes : (g + 1) * lanes].astype(F32)
                    pick = jnp.where(own == yy, part, pick)
            block = jnp.zeros((PITCH, lanes), F32)
            for d in range(WIN):
                block = jnp.where(gap == d, pick[d : d + 1], block)
            bt[g, r * PITCH : (r + 1) * PITCH] = block.astype(BF)
        b[g] = bt[g].astype(F32).T.astype(BF)


def band(cot):
    groups = cot.shape[1] // (GROUP * BLK)
    return pl.pallas_call(
        band_kernel,
        out_shape=(
            jax.ShapeDtypeStruct((groups, GROWS * PITCH, GROUP * BLK), BF),
            jax.ShapeDtypeStruct((groups, GROUP * BLK, GROWS * PITCH), BF),
        ),
        in_specs=vmem(1),
        out_specs=tuple(vmem(2)),
        compiler_params=params(),
        name="band",
    )(cot)


def main_kernel(
    height, width, pieces,
    pos, frames, up, down, left, right, ul, ur, dl, dr, weight, bias, bt, b,
    out, f1, f2,
    ext2, ext1, xc2, xc1, pre2, pre1, gwin, dsh2, dsh1, dc2, dc1, ft2, ft1, total,
):
    rows, cols, ch = frames.shape[1:]
    inv_root = ch ** (-0.5)
    r0, c0, gy0, gx0 = pos[0], pos[1], pos[2], pos[3]
    lo, hi = HALO, HALO + rows
    ext2[lo:hi, 16 : 16 + cols] = frames[1].astype(F32)
    ext2[0:lo, 16 : 16 + cols] = up[0:HALO].astype(F32)
    ext2[hi:, 16 : 16 + cols] = down[0:HALO].astype(F32)
    vl = left[...].astype(F32)
    vr = right[...].astype(F32)
    ext2[lo:hi, 0:16] = vl
    ext2[lo:hi, 16 + cols : 32 + cols] = vr
    vul, vur = ul[...].astype(F32), ur[...].astype(F32)
    vdl, vdr = dl[...].astype(F32), dr[...].astype(F32)
    ext2[0:lo, 0:16] = vul
    ext2[0:lo, 16 + cols : 32 + cols] = vur
    ext2[hi:, 0:16] = vdl
    ext2[hi:, 16 + cols : 32 + cols] = vdr
    ext2[:, 32 + cols :] = jnp.zeros((ext2.shape[0], ext2.shape[1] - 32 - cols, ch), F32)
    ext1[...] = jnp.zeros(ext1.shape, F32)
    ext1[1 : rows + 1, 8 : 8 + cols] = frames[0].astype(F32)
    ext1[0:1, 8 : 8 + cols] = up[HALO : HALO + 1].astype(F32)
    ext1[rows + 1 : rows + 2, 8 : 8 + cols] = down[HALO : HALO + 1].astype(F32)
    ext1[1 : rows + 1, 7:8] = vl[:, 0:1]
    ext1[1 : rows + 1, 8 + cols : 9 + cols] = vr[:, 15:16]
    ext1[0:1, 7:8] = vul[HALO - 1 :, 0:1]
    ext1[0:1, 8 + cols : 9 + cols] = vur[HALO - 1 :, 15:16]
    ext1[rows + 1 : rows + 2, 7:8] = vdl[0:1, 0:1]
    ext1[rows + 1 : rows + 2, 8 + cols : 9 + cols] = vdr[0:1, 15:16]

    span = PITCH + 8
    base = pl.multiple_of((c0 // 8) * 8, 8)
    turn = span - c0 % 8

    def gather(r, carry):
        row = pltpu.roll(ext2[r0 + r, pl.ds(base, span), :], turn, 0)
        for j in range(3):
            xc2[r, :, j * ch : (j + 1) * ch] = row[j : j + PITCH].astype(BF)
        return carry

    lax.fori_loop(0, WROWS + 2, gather, 0)
    for j in range(3):
        xc1[:, :, j * ch : (j + 1) * ch] = ext1[:, 7 + j : 7 + j + cols].astype(BF)

    shift = bias[...]
    step = 8

    def conv_two(n, carry):
        acc = jnp.zeros((step * PITCH, ch), F32)
        for i in range(3):
            x = xc2[pl.ds(n * step + i, step)].reshape(step * PITCH, 3 * ch)
            acc = acc + jnp.dot(x, weight[i], preferred_element_type=F32)
        acc = (acc + shift).reshape(step, PITCH, ch)
        y = lax.broadcasted_iota(jnp.int32, acc.shape, 0) + n * step + gy0
        c = lax.broadcasted_iota(jnp.int32, acc.shape, 1)
        x = c + gx0
        ok = (y >= 0) & (y < height) & (x >= 0) & (x < width) & (c < WCOLS)
        acc = jnp.maximum(jnp.where(ok, acc, 0.0), 0.0).reshape(step * PITCH, ch)
        pre2[pl.ds(n * step * PITCH, step * PITCH)] = acc
        f2[pl.ds(n * step * PITCH, step * PITCH)] = acc.astype(BF)
        return carry

    lax.fori_loop(0, WROWS // step, conv_two, 0)

    def conv_one(n, carry):
        acc = jnp.zeros((step * cols, ch), F32)
        for i in range(3):
            x = xc1[pl.ds(n * step + i, step)].reshape(step * cols, 3 * ch)
            acc = acc + jnp.dot(x, weight[i], preferred_element_type=F32)
        acc = jnp.maximum(acc + shift, 0.0)
        pre1[pl.ds(n * step * cols, step * cols)] = acc
        f1[pl.ds(n * step * cols, step * cols)] = acc.astype(BF)
        return carry

    lax.fori_loop(0, rows // step, conv_one, 0)

    ft2[...] = xc2[:, :, 0:ch].reshape((WROWS + 2) * PITCH, ch).T
    ft1[...] = ext1[:, 7 : 7 + PITCH].astype(BF).reshape((rows + 2) * PITCH, ch).T

    gwin[...] = jnp.zeros(gwin.shape, F32)
    dsh1[...] = jnp.zeros(dsh1.shape, F32)
    lanes = GROUP * cols
    bsum = jnp.zeros((1, ch), F32)
    for g in range(rows // GROUP):
        at = slice(g * GROUP * PITCH, (g * GROUP + GROWS) * PITCH)
        px = slice(g * lanes, (g + 1) * lanes)
        gwin[at] += jnp.dot(bt[g], f1[px], preferred_element_type=F32)
        one = jnp.dot(b[g], f2[at], preferred_element_type=F32) * inv_root
        one = jnp.where(pre1[px] > 0, one, 0.0).astype(BF).astype(F32)
        bsum = bsum + jnp.sum(one, axis=0, keepdims=True)
        dsh1[g * GROUP : (g + 1) * GROUP, 8 : 8 + cols] = one.reshape(GROUP, cols, ch)
    two = jnp.where(pre2[...] > 0, gwin[...] * inv_root, 0.0)
    bsum = bsum + jnp.sum(two, axis=0, keepdims=True)
    dsh2[:, 0:8] = jnp.zeros((WROWS, 8, ch), F32)
    dsh2[:, 8 : 8 + PITCH] = two.reshape(WROWS, PITCH, ch)
    for ref, src, n in ((dc2, dsh2, WROWS), (dc1, dsh1, rows)):
        ref[0:2] = jnp.zeros((2,) + ref.shape[1:], BF)
        ref[n + 2 : n + 4] = jnp.zeros((2,) + ref.shape[1:], BF)
        for j in range(3):
            ref[2 : n + 2, :, j * ch : (j + 1) * ch] = src[:, 8 - j : 8 - j + PITCH].astype(BF)
    for i in range(3):
        n2, n1 = WROWS + 2, rows + 2
        acc = jnp.dot(
            ft2[...], dc2[2 - i : 2 - i + n2].reshape(n2 * PITCH, 3 * ch), preferred_element_type=F32
        )
        acc = acc + jnp.dot(
            ft1[...], dc1[2 - i : 2 - i + n1].reshape(n1 * PITCH, 3 * ch), preferred_element_type=F32
        )
        for j in range(3):
            total[(3 * i + j) * ch : (3 * i + j + 1) * ch] = acc[:, j * ch : (j + 1) * ch]
    size = 9 * ch // pieces
    for p in range(pieces):
        tail = bias_rows(bsum) if p == 0 else jnp.zeros((8, ch), F32)
        out[p] = jnp.concatenate([total[p * size : (p + 1) * size], tail], axis=0).astype(BF)


def bias_rows(value):
    high = value.astype(BF).astype(F32)
    row = lax.broadcasted_iota(jnp.int32, (8, value.shape[1]), 0)
    return jnp.where(row == 0, high, jnp.where(row == 1, value - high, 0.0))


def main(pos, frames, halo, weight, bias, bt, b, height, width, pieces):
    rows, cols, ch = frames.shape[1:]
    wpx, n2, n1 = WROWS * PITCH, WROWS + 2, rows + 2
    return pl.pallas_call(
        functools.partial(main_kernel, height, width, pieces),
        out_shape=(
            jax.ShapeDtypeStruct((pieces, 9 * ch // pieces + 8, ch), BF),
            jax.ShapeDtypeStruct((rows * cols, ch), BF),
            jax.ShapeDtypeStruct((wpx, ch), BF),
        ),
        in_specs=[pl.BlockSpec(memory_space=pltpu.SMEM)] + vmem(13),
        out_specs=tuple(vmem(3)),
        scratch_shapes=[
            pltpu.VMEM((rows + 2 * HALO, cols + 48, ch), F32),
            pltpu.VMEM((n1, 56, ch), F32),
            pltpu.VMEM((n2, PITCH, 3 * ch), BF),
            pltpu.VMEM((n1, cols, 3 * ch), BF),
            pltpu.VMEM((wpx, ch), F32),
            pltpu.VMEM((rows * cols, ch), F32),
            pltpu.VMEM((wpx, ch), F32),
            pltpu.VMEM((WROWS, 64, ch), F32),
            pltpu.VMEM((rows, 64, ch), F32),
            pltpu.VMEM((WROWS + 4, PITCH, 3 * ch), BF),
            pltpu.VMEM((rows + 4, PITCH, 3 * ch), BF),
            pltpu.VMEM((ch, n2 * PITCH), BF),
            pltpu.VMEM((ch, n1 * PITCH), BF),
            pltpu.VMEM((9 * ch, ch), F32),
        ],
        compiler_params=params(),
        cost_estimate=pl.CostEstimate(flops=5_000_000_000, bytes_accessed=8_000_000, transcendentals=0),
        name="main",
    )(pos, frames, *halo, weight, bias, bt, b)


def corr_kernel(f1, f2, out):
    lanes = GROUP * BLK
    inv_root = f1.shape[1] ** (-0.5)
    lane = lax.broadcasted_iota(jnp.int32, (PITCH, lanes), 1)
    gap = lax.broadcasted_iota(jnp.int32, (PITCH, lanes), 0) - lane % BLK
    own = lane // BLK
    for g in range(f1.shape[0] // lanes):
        at = slice(g * GROUP * PITCH, (g * GROUP + GROWS) * PITCH)
        scores = lax.dot_general(
            f2[at], f1[g * lanes : (g + 1) * lanes], (((1,), (1,)), ((), ())),
            preferred_element_type=F32,
        )
        for a in range(WIN):
            pick = scores[a * PITCH : (a + 1) * PITCH]
            for yy in range(1, GROUP):
                pick = jnp.where(own == yy, scores[(a + yy) * PITCH : (a + yy + 1) * PITCH], pick)
            for d in range(WIN):
                line = jnp.sum(jnp.where(gap == d, pick, 0.0), axis=0, keepdims=True) * inv_root
                out[a * WIN + d : a * WIN + d + 1, g * lanes : (g + 1) * lanes] = line


def correlate(f1, f2):
    return pl.pallas_call(
        corr_kernel,
        out_shape=jax.ShapeDtypeStruct((WIN * WIN, f1.shape[0]), F32),
        in_specs=vmem(2),
        out_specs=vmem(1)[0],
        compiler_params=params(),
        cost_estimate=pl.CostEstimate(flops=300_000_000, bytes_accessed=1_000_000, transcendentals=0),
        name="corr",
    )(f1, f2)


def sum_kernel(parts, out):
    copies = out.shape[0]
    size, ch = parts.shape[1:]
    step = 8
    for s in range(0, size - 16, 16):
        out_rows = parts[0, s : s + 16].astype(F32)
        for n in range(1, parts.shape[0]):
            out_rows = out_rows + parts[n, s : s + 16].astype(F32)
        for k in range(copies):
            out[k, s : s + 16] = out_rows.astype(BF)
    s = size - 16
    last = parts[0, s:size].astype(F32)
    for n in range(1, parts.shape[0]):
        last = last + parts[n, s:size].astype(F32)
    tail = bias_rows(last[step : step + 1] + last[step + 1 : step + 2])
    last = jnp.concatenate([last[0:step], tail], axis=0).astype(BF)
    for k in range(copies):
        out[k, s:size] = last


def sum_and_copy(parts, copies):
    return pl.pallas_call(
        sum_kernel,
        out_shape=jax.ShapeDtypeStruct((copies,) + parts.shape[1:], BF),
        in_specs=vmem(1),
        out_specs=vmem(1)[0],
        compiler_params=params(),
        name="sum",
    )(parts)


def unpack_kernel(parts, grad, bias):
    size = parts.shape[1] - 8
    for p in range(parts.shape[0]):
        value = parts[p].astype(F32)
        grad[p * size : (p + 1) * size] = value[0:size]
        if p == 0:
            bias[...] = value[size : size + 1] + value[size + 1 : size + 2]


def unpack(parts):
    pieces, size, ch = parts.shape
    return pl.pallas_call(
        unpack_kernel,
        out_shape=(
            jax.ShapeDtypeStruct((pieces * (size - 8), ch), F32),
            jax.ShapeDtypeStruct((1, ch), F32),
        ),
        in_specs=vmem(1),
        out_specs=tuple(vmem(2)),
        compiler_params=params(),
        name="unpack",
    )(parts)


def exchange(pieces, axes, row_count, col_count):
    moves = ((-1, 0), (1, 0), (0, -1), (0, 1), (-1, -1), (-1, 1), (1, -1), (1, 1))
    got = {}
    for k in (4, 5, 6, 7, 0, 1, 2, 3):
        dy, dx = moves[k]
        pairs = []
        for r in range(row_count):
            for c in range(col_count):
                if 0 <= r + dy < row_count and 0 <= c + dx < col_count:
                    pairs.append((r * col_count + c, (r + dy) * col_count + c + dx))
        got[(-dy, -dx)] = lax.ppermute(pieces[k], axes, pairs)
    return [got[m] for m in moves]


def shards(row_count, col_count, space, group, frames, offsets, weight, bias, cotangent):
    rows, cols, ch = frames.shape[2:]
    height, width = row_count * rows, col_count * cols
    row_start = lax.axis_index("row") * rows
    col_start = lax.axis_index(space[1:]) * cols
    shift = offsets[0, row_start // BLK, col_start // BLK]
    pos = jnp.stack(
        [
            shift[0] + MAXOFF,
            shift[1] + 16 - RAD - 1,
            row_start + shift[0] - RAD,
            col_start + shift[1] - RAD,
        ]
    ).astype(jnp.int32)
    halo = exchange(pack(frames[0]), space, row_count, col_count)
    cot = jnp.pad(cotangent[0].reshape(WIN, WIN, rows * cols), ((0, 0), (0, 16 - WIN), (0, 0)))
    bt, b = band(cot.reshape(WIN * 16, rows * cols))
    pieces = int(np.prod([lax.axis_size(a) for a in group]))
    parts, f1, f2 = main(
        pos, frames[0], halo, weight.reshape(3, 3 * ch, ch), bias.reshape(1, ch), bt, b, height, width, pieces
    )
    parts = lax.all_to_all(parts, group, 0, 0, tiled=True)
    corr = correlate(f1, f2)
    corr = corr.reshape(1, WIN * WIN, rows, cols).astype(BF)
    parts = sum_and_copy(parts, lax.axis_size("z"))
    parts = lax.all_to_all(parts, "z", 0, 0, tiled=True)
    parts = sum_and_copy(parts, pieces)
    parts = lax.all_to_all(parts, group, 0, 0, tiled=True)
    grad_w, grad_b = unpack(parts)
    return corr, grad_w.reshape(3, 3, ch, ch), grad_b.reshape(ch)


def solution(mesh):
    row_count, col_count, pair_count = (mesh.shape[a] for a in ("row", "col", "pair"))
    high = 2 if col_count == 16 else 1
    fine = Mesh(
        mesh.devices.reshape(row_count, high, col_count // high, pair_count), ("row", "high", "z", "pair")
    )
    col = ("high", "z")
    return jax.shard_map(
        functools.partial(shards, row_count, col_count, ("row",) + col, ("row", "high", "pair")),
        mesh=fine,
        in_specs=(
            P("pair", None, "row", col, None),
            P("pair", None, None, None),
            P(),
            P(),
            P("pair", None, "row", col),
        ),
        out_specs=(P("pair", None, "row", col), P(), P()),
        check_vma=False,
    )
```

```python
import functools

import jax
import jax.numpy as jnp
import numpy as np
from jax import lax
from jax.experimental import pallas as pl
from jax.experimental.pallas import tpu as pltpu
from jax.sharding import Mesh
from jax.sharding import PartitionSpec as P

BLK = 32
RAD = 4
MAXOFF = 8
WIN = 2 * RAD + 1
HALO = MAXOFF + RAD + 1
PITCH = 48
WROWS = 24
WCOLS = 40
GROUP = 4
GROWS = GROUP + WIN - 1
BF = jnp.bfloat16
F32 = jnp.float32


def vmem(n):
    return [pl.BlockSpec(memory_space=pltpu.VMEM)] * n


def params():
    return pltpu.CompilerParams(vmem_limit_bytes=48 * 1024 * 1024)


def even(index):
    return lax.rem(index, 2) == 0


def rows_kernel(pos, frames, first, second):
    rows = frames.shape[1]
    below = even(pos[0])
    for ref, low in ((first, below), (second, jnp.logical_not(below))):
        ref[0:HALO] = frames[1, pl.ds(jnp.where(low, rows - HALO, 0), HALO)]
        ref[HALO] = frames[0, jnp.where(low, rows - 1, 0)]


def row_pieces(pos, frames):
    cols, ch = frames.shape[2:]
    piece = jax.ShapeDtypeStruct((HALO + 1, cols, ch), BF)
    return pl.pallas_call(
        rows_kernel,
        out_shape=(piece, piece),
        in_specs=[pl.BlockSpec(memory_space=pltpu.SMEM)] + vmem(1),
        out_specs=tuple(vmem(2)),
        compiler_params=params(),
        name="row_pieces",
    )(pos, frames)


def cols_kernel(pos, offs, frames, got_first, got_second, first, second, center, one, ext):
    rows, cols, ch = frames.shape[1:]
    below = even(pos[0])
    block = pos[0] * rows // BLK
    last = pos[2] - 1
    ext[HALO : HALO + rows] = frames[1]
    one[1 : rows + 1] = frames[0]
    for ref, low in ((got_first, below), (got_second, jnp.logical_not(below))):
        ext[pl.ds(jnp.where(low, HALO + rows, 0), HALO)] = ref[0:HALO]
        one[jnp.where(low, rows + 1, 0)] = ref[HALO]
    center[...] = ext[pl.ds(offs[block, 2 * pos[1]] + MAXOFF, WROWS + 2)]
    right = even(pos[1])
    col = lax.broadcasted_iota(jnp.int32, (rows + 2, 16, ch), 1)
    for ref, side in ((first, right), (second, jnp.logical_not(right))):
        other = jnp.clip(jnp.where(side, pos[1] + 1, pos[1] - 1), 0, last)
        start = offs[block, 2 * other] + MAXOFF
        at = pl.multiple_of(jnp.where(side, cols - 16, 0), 16)
        ref[...] = ext[pl.ds(start, WROWS + 2), pl.ds(at, 16)]
        border = one[:, pl.ds(at, 16)].astype(F32)
        border = jnp.where(side, border[:, 15:16], border[:, 0:1])
        spare = jnp.where(side, 0, 15)
        ref[0 : rows + 2] = jnp.where(col == spare, border, ref[0 : rows + 2].astype(F32)).astype(BF)


def col_pieces(pos, offs, frames, got):
    rows, cols, ch = frames.shape[1:]
    piece = jax.ShapeDtypeStruct((WROWS + 2, 16, ch), BF)
    return pl.pallas_call(
        cols_kernel,
        out_shape=(
            piece,
            piece,
            jax.ShapeDtypeStruct((WROWS + 2, cols, ch), BF),
            jax.ShapeDtypeStruct((rows + 2, cols, ch), BF),
        ),
        in_specs=[pl.BlockSpec(memory_space=pltpu.SMEM)] * 2 + vmem(3),
        out_specs=tuple(vmem(4)),
        scratch_shapes=[pltpu.VMEM((rows + 2 * HALO, cols, ch), BF)],
        compiler_params=params(),
        name="col_pieces",
    )(pos, offs, frames, *got)


def swap(pieces, axes, count):
    got = []
    for piece, start in zip(pieces, (0, 1)):
        pairs = []
        for i in range(start, count - 1, 2):
            pairs += [(i, i + 1), (i + 1, i)]
        got.append(lax.ppermute(piece, axes, pairs))
    return got


def band_kernel(cot, bt, b, lines):
    count, rows, cols = cot.shape
    lanes = GROUP * BLK

    def iota(shape, axis):
        return lax.broadcasted_iota(jnp.int32, shape, axis)

    copy = (iota((cols, lanes), 1) % cols == iota((cols, lanes), 0)).astype(F32).astype(BF)
    wide = jnp.dot(cot[...].reshape(count * rows, cols), copy, preferred_element_type=F32)
    shape = (WIN * 16, count * rows)
    q, d = iota(shape, 0), iota(shape, 1) // rows
    pickd = ((q // 16 * WIN + q % 16 == d) & (q % 16 < WIN)).astype(F32).astype(BF)
    line = iota((count * rows, lanes), 0) % rows
    want = iota((count * rows, lanes), 1) // cols
    gap = iota((PITCH, lanes), 0) - iota((PITCH, lanes), 1) % BLK
    own = iota((16, lanes), 1) // BLK
    for g in range(bt.shape[0]):
        mine = jnp.where(line == want + g * GROUP, wide, 0.0).astype(BF)
        lines[...] = jnp.dot(pickd, mine, preferred_element_type=F32)
        for r in range(GROWS):
            pick = jnp.zeros((16, lanes), F32)
            for yy in range(GROUP):
                a = r - yy
                if 0 <= a < WIN:
                    pick = jnp.where(own == yy, lines[a * 16 : (a + 1) * 16], pick)
            block = jnp.zeros((PITCH, lanes), F32)
            for k in range(WIN):
                block = jnp.where(gap == k, pick[k : k + 1], block)
            bt[g, r * PITCH : (r + 1) * PITCH] = block.astype(BF)
        b[g] = bt[g].astype(F32).T.astype(BF)


def band(cot):
    groups = cot.shape[1] // GROUP
    return pl.pallas_call(
        band_kernel,
        out_shape=(
            jax.ShapeDtypeStruct((groups, GROWS * PITCH, GROUP * BLK), BF),
            jax.ShapeDtypeStruct((groups, GROUP * BLK, GROWS * PITCH), BF),
        ),
        in_specs=vmem(1),
        out_specs=tuple(vmem(2)),
        scratch_shapes=[pltpu.VMEM((WIN * 16, GROUP * BLK), F32)],
        compiler_params=params(),
        cost_estimate=pl.CostEstimate(flops=2_000_000_000, bytes_accessed=1_000_000, transcendentals=0),
        name="band",
    )(cot)


def main_kernel(
    row_count, col_count, pieces,
    pos, offs, center, one, got_first, got_second, weight, bias, bt, b,
    out, f1, f2,
    ext2, ext1, xc2, xc1, pre2, pre1, gwin, dsh2, dsh1, dc2, dc1, ft2, ft1, total,
):
    rows, cols, ch = one.shape[0] - 2, one.shape[1], one.shape[2]
    height, width = row_count * rows, col_count * cols
    inv_root = ch ** (-0.5)
    block = pos[0] * rows // BLK
    oy, ox = offs[block, 2 * pos[1]], offs[block, 2 * pos[1] + 1]
    c0, gy0, gx0 = ox + 16 - RAD - 1, pos[0] * rows + oy - RAD, pos[1] * cols + ox - RAD
    right = even(pos[1])
    ext2[:, 16 : 16 + cols] = center[...].astype(F32)
    v_first, v_second = got_first[...].astype(F32), got_second[...].astype(F32)
    for value, side in ((v_first, right), (v_second, jnp.logical_not(right))):
        ext2[:, pl.ds(pl.multiple_of(jnp.where(side, 16 + cols, 0), 16), 16)] = value
    ext2[:, 32 + cols :] = jnp.zeros((WROWS + 2, ext2.shape[1] - 32 - cols, ch), F32)
    ext1[:, 0:8] = jnp.zeros((rows + 2, 8, ch), F32)
    ext1[:, 8 + cols :] = jnp.zeros((rows + 2, ext1.shape[1] - 8 - cols, ch), F32)
    ext1[:, 8 : 8 + cols] = one[...].astype(F32)
    ext1[:, 7:8] = jnp.where(right, v_second[0 : rows + 2, 0:1], v_first[0 : rows + 2, 0:1])
    ext1[:, 8 + cols : 9 + cols] = jnp.where(right, v_first[0 : rows + 2, 15:16], v_second[0 : rows + 2, 15:16])

    span = PITCH + 8
    base = pl.multiple_of((c0 // 8) * 8, 8)
    turn = span - c0 % 8

    def gather(r, carry):
        row = pltpu.roll(ext2[r, pl.ds(base, span), :], turn, 0)
        for j in range(3):
            xc2[r, :, j * ch : (j + 1) * ch] = row[j : j + PITCH].astype(BF)
        return carry

    lax.fori_loop(0, WROWS + 2, gather, 0)
    for j in range(3):
        xc1[:, :, j * ch : (j + 1) * ch] = ext1[:, 7 + j : 7 + j + cols].astype(BF)

    shift = bias[...]
    step = 8

    def conv_two(n, carry):
        acc = jnp.zeros((step * PITCH, ch), F32)
        for i in range(3):
            x = xc2[pl.ds(n * step + i, step)].reshape(step * PITCH, 3 * ch)
            acc = acc + jnp.dot(x, weight[i], preferred_element_type=F32)
        acc = (acc + shift).reshape(step, PITCH, ch)
        y = lax.broadcasted_iota(jnp.int32, acc.shape, 0) + n * step + gy0
        c = lax.broadcasted_iota(jnp.int32, acc.shape, 1)
        x = c + gx0
        ok = (y >= 0) & (y < height) & (x >= 0) & (x < width) & (c < WCOLS)
        acc = jnp.maximum(jnp.where(ok, acc, 0.0), 0.0).reshape(step * PITCH, ch)
        pre2[pl.ds(n * step * PITCH, step * PITCH)] = acc
        f2[pl.ds(n * step * PITCH, step * PITCH)] = acc.astype(BF)
        return carry

    lax.fori_loop(0, WROWS // step, conv_two, 0)

    def conv_one(n, carry):
        acc = jnp.zeros((step * cols, ch), F32)
        for i in range(3):
            x = xc1[pl.ds(n * step + i, step)].reshape(step * cols, 3 * ch)
            acc = acc + jnp.dot(x, weight[i], preferred_element_type=F32)
        acc = jnp.maximum(acc + shift, 0.0)
        pre1[pl.ds(n * step * cols, step * cols)] = acc
        f1[pl.ds(n * step * cols, step * cols)] = acc.astype(BF)
        return carry

    lax.fori_loop(0, rows // step, conv_one, 0)

    ft2[...] = xc2[:, :, 0:ch].reshape((WROWS + 2) * PITCH, ch).T
    ft1[...] = ext1[:, 7 : 7 + PITCH].astype(BF).reshape((rows + 2) * PITCH, ch).T

    gwin[...] = jnp.zeros(gwin.shape, F32)
    dsh1[...] = jnp.zeros(dsh1.shape, F32)
    lanes = GROUP * cols
    bsum = jnp.zeros((1, ch), F32)
    for g in range(rows // GROUP):
        at = slice(g * GROUP * PITCH, (g * GROUP + GROWS) * PITCH)
        px = slice(g * lanes, (g + 1) * lanes)
        gwin[at] += jnp.dot(bt[g], f1[px], preferred_element_type=F32)
        one = jnp.dot(b[g], f2[at], preferred_element_type=F32) * inv_root
        one = jnp.where(pre1[px] > 0, one, 0.0).astype(BF).astype(F32)
        bsum = bsum + jnp.sum(one, axis=0, keepdims=True)
        dsh1[g * GROUP : (g + 1) * GROUP, 8 : 8 + cols] = one.reshape(GROUP, cols, ch)
    two = jnp.where(pre2[...] > 0, gwin[...] * inv_root, 0.0)
    bsum = bsum + jnp.sum(two, axis=0, keepdims=True)
    dsh2[:, 0:8] = jnp.zeros((WROWS, 8, ch), F32)
    dsh2[:, 8 : 8 + PITCH] = two.reshape(WROWS, PITCH, ch)
    for ref, src, n in ((dc2, dsh2, WROWS), (dc1, dsh1, rows)):
        ref[0:2] = jnp.zeros((2,) + ref.shape[1:], BF)
        ref[n + 2 : n + 4] = jnp.zeros((2,) + ref.shape[1:], BF)
        for j in range(3):
            ref[2 : n + 2, :, j * ch : (j + 1) * ch] = src[:, 8 - j : 8 - j + PITCH].astype(BF)
    for i in range(3):
        n2, n1 = WROWS + 2, rows + 2
        acc = jnp.dot(
            ft2[...], dc2[2 - i : 2 - i + n2].reshape(n2 * PITCH, 3 * ch), preferred_element_type=F32
        )
        acc = acc + jnp.dot(
            ft1[...], dc1[2 - i : 2 - i + n1].reshape(n1 * PITCH, 3 * ch), preferred_element_type=F32
        )
        for j in range(3):
            total[(3 * i + j) * ch : (3 * i + j + 1) * ch] = acc[:, j * ch : (j + 1) * ch]
    size = 9 * ch // pieces
    for p in range(pieces):
        tail = bias_rows(bsum) if p == 0 else jnp.zeros((8, ch), F32)
        out[p] = jnp.concatenate([total[p * size : (p + 1) * size], tail], axis=0).astype(BF)


def bias_rows(value):
    high = value.astype(BF).astype(F32)
    row = lax.broadcasted_iota(jnp.int32, (8, value.shape[1]), 0)
    return jnp.where(row == 0, high, jnp.where(row == 1, value - high, 0.0))


def main(pos, offs, center, one, got, weight, bias, bt, b, row_count, col_count, pieces):
    rows, cols, ch = one.shape[0] - 2, one.shape[1], one.shape[2]
    wpx, n2, n1 = WROWS * PITCH, WROWS + 2, rows + 2
    return pl.pallas_call(
        functools.partial(main_kernel, row_count, col_count, pieces),
        out_shape=(
            jax.ShapeDtypeStruct((pieces, 9 * ch // pieces + 8, ch), BF),
            jax.ShapeDtypeStruct((rows * cols, ch), BF),
            jax.ShapeDtypeStruct((wpx, ch), BF),
        ),
        in_specs=[pl.BlockSpec(memory_space=pltpu.SMEM)] * 2 + vmem(8),
        out_specs=tuple(vmem(3)),
        scratch_shapes=[
            pltpu.VMEM((n2, cols + 48, ch), F32),
            pltpu.VMEM((n1, 56, ch), F32),
            pltpu.VMEM((n2, PITCH, 3 * ch), BF),
            pltpu.VMEM((n1, cols, 3 * ch), BF),
            pltpu.VMEM((wpx, ch), F32),
            pltpu.VMEM((rows * cols, ch), F32),
            pltpu.VMEM((wpx, ch), F32),
            pltpu.VMEM((WROWS, 64, ch), F32),
            pltpu.VMEM((rows, 64, ch), F32),
            pltpu.VMEM((WROWS + 4, PITCH, 3 * ch), BF),
            pltpu.VMEM((rows + 4, PITCH, 3 * ch), BF),
            pltpu.VMEM((ch, n2 * PITCH), BF),
            pltpu.VMEM((ch, n1 * PITCH), BF),
            pltpu.VMEM((9 * ch, ch), F32),
        ],
        compiler_params=params(),
        cost_estimate=pl.CostEstimate(flops=5_000_000_000, bytes_accessed=8_000_000, transcendentals=0),
        name="main",
    )(pos, offs, center, one, *got, weight, bias, bt, b)


def corr_kernel(f1, f2, out):
    lanes = GROUP * BLK
    inv_root = f1.shape[1] ** (-0.5)
    lane = lax.broadcasted_iota(jnp.int32, (PITCH, lanes), 1)
    gap = lax.broadcasted_iota(jnp.int32, (PITCH, lanes), 0) - lane % BLK
    own = lane // BLK
    for g in range(f1.shape[0] // lanes):
        at = slice(g * GROUP * PITCH, (g * GROUP + GROWS) * PITCH)
        scores = lax.dot_general(
            f2[at], f1[g * lanes : (g + 1) * lanes], (((1,), (1,)), ((), ())),
            preferred_element_type=F32,
        )
        for a in range(WIN):
            pick = scores[a * PITCH : (a + 1) * PITCH]
            for yy in range(1, GROUP):
                pick = jnp.where(own == yy, scores[(a + yy) * PITCH : (a + yy + 1) * PITCH], pick)
            for d in range(WIN):
                line = jnp.sum(jnp.where(gap == d, pick, 0.0), axis=0, keepdims=True) * inv_root
                out[a * WIN + d : a * WIN + d + 1, g * lanes : (g + 1) * lanes] = line


def correlate(f1, f2):
    return pl.pallas_call(
        corr_kernel,
        out_shape=jax.ShapeDtypeStruct((WIN * WIN, f1.shape[0]), F32),
        in_specs=vmem(2),
        out_specs=vmem(1)[0],
        compiler_params=params(),
        cost_estimate=pl.CostEstimate(flops=300_000_000, bytes_accessed=1_000_000, transcendentals=0),
        name="corr",
    )(f1, f2)


def sum_kernel(parts, out):
    copies = out.shape[0]
    size, ch = parts.shape[1:]
    step = 8
    for s in range(0, size - 16, 16):
        out_rows = parts[0, s : s + 16].astype(F32)
        for n in range(1, parts.shape[0]):
            out_rows = out_rows + parts[n, s : s + 16].astype(F32)
        for k in range(copies):
            out[k, s : s + 16] = out_rows.astype(BF)
    s = size - 16
    last = parts[0, s:size].astype(F32)
    for n in range(1, parts.shape[0]):
        last = last + parts[n, s:size].astype(F32)
    tail = bias_rows(last[step : step + 1] + last[step + 1 : step + 2])
    last = jnp.concatenate([last[0:step], tail], axis=0).astype(BF)
    for k in range(copies):
        out[k, s:size] = last


def sum_and_copy(parts, copies):
    return pl.pallas_call(
        sum_kernel,
        out_shape=jax.ShapeDtypeStruct((copies,) + parts.shape[1:], BF),
        in_specs=vmem(1),
        out_specs=vmem(1)[0],
        compiler_params=params(),
        name="sum",
    )(parts)


def unpack_kernel(parts, grad, bias):
    size = parts.shape[1] - 8
    for p in range(parts.shape[0]):
        value = parts[p].astype(F32)
        grad[p * size : (p + 1) * size] = value[0:size]
        if p == 0:
            bias[...] = value[size : size + 1] + value[size + 1 : size + 2]


def unpack(parts):
    pieces, size, ch = parts.shape
    return pl.pallas_call(
        unpack_kernel,
        out_shape=(
            jax.ShapeDtypeStruct((pieces * (size - 8), ch), F32),
            jax.ShapeDtypeStruct((1, ch), F32),
        ),
        in_specs=vmem(1),
        out_specs=tuple(vmem(2)),
        compiler_params=params(),
        name="unpack",
    )(parts)


def shards(row_count, col_count, space, group, frames, offsets, weight, bias, cotangent):
    rows, cols, ch = frames.shape[2:]
    pos = jnp.stack([lax.axis_index("row"), lax.axis_index(space), jnp.int32(col_count)]).astype(jnp.int32)
    offs = offsets[0].reshape(offsets.shape[1], -1)
    got = swap(row_pieces(pos, frames[0]), "row", row_count)
    bt, b = band(cotangent[0])
    first, second, center, one = col_pieces(pos, offs, frames[0], got)
    got = swap((first, second), space, col_count)
    pieces = int(np.prod([lax.axis_size(a) for a in group]))
    parts, f1, f2 = main(
        pos, offs, center, one, got, weight.reshape(3, 3 * ch, ch), bias.reshape(1, ch), bt, b,
        row_count, col_count, pieces,
    )
    parts = lax.all_to_all(parts, group, 0, 0, tiled=True)
    corr = correlate(f1, f2)
    corr = corr.reshape(1, WIN * WIN, rows, cols).astype(BF)
    parts = sum_and_copy(parts, lax.axis_size("z"))
    parts = lax.all_to_all(parts, "z", 0, 0, tiled=True)
    parts = sum_and_copy(parts, pieces)
    parts = lax.all_to_all(parts, group, 0, 0, tiled=True)
    grad_w, grad_b = unpack(parts)
    return corr, grad_w.reshape(3, 3, ch, ch), grad_b.reshape(ch)


def solution(mesh):
    row_count, col_count, pair_count = (mesh.shape[a] for a in ("row", "col", "pair"))
    high = 2 if col_count == 16 else 1
    fine = Mesh(
        mesh.devices.reshape(row_count, high, col_count // high, pair_count), ("row", "high", "z", "pair")
    )
    col = ("high", "z")
    return jax.shard_map(
        functools.partial(shards, row_count, col_count, col, ("row", "high", "pair")),
        mesh=fine,
        in_specs=(
            P("pair", None, "row", col, None),
            P("pair", None, None, None),
            P(),
            P(),
            P("pair", None, "row", col),
        ),
        out_specs=(P("pair", None, "row", col), P(), P()),
        check_vma=False,
    )
```

```python
import functools

import jax
import jax.numpy as jnp
import numpy as np
from jax import lax
from jax.experimental import pallas as pl
from jax.experimental.pallas import tpu as pltpu
from jax.sharding import Mesh
from jax.sharding import PartitionSpec as P

BLK = 32
RAD = 4
MAXOFF = 8
WIN = 2 * RAD + 1
HALO = MAXOFF + RAD + 1
PITCH = 48
WROWS = 24
WCOLS = 40
GROUP = 4
GROWS = GROUP + WIN - 1
BF = jnp.bfloat16
F32 = jnp.float32


def vmem(n):
    return [pl.BlockSpec(memory_space=pltpu.VMEM)] * n


def params():
    return pltpu.CompilerParams(vmem_limit_bytes=48 * 1024 * 1024)


def even(index):
    return lax.rem(index, 2) == 0


def rows_kernel(pos, frames, first, second, kept):
    rows = frames.shape[1]
    below = even(pos[0])
    for ref, low in ((first, below), (second, jnp.logical_not(below))):
        ref[0:HALO] = frames[1, pl.ds(jnp.where(low, rows - HALO, 0), HALO)]
        ref[HALO] = frames[0, jnp.where(low, rows - 1, 0)]
    kept[...] = frames[...]


def row_pieces(pos, frames):
    cols, ch = frames.shape[2:]
    piece = jax.ShapeDtypeStruct((HALO + 1, cols, ch), BF)
    return pl.pallas_call(
        rows_kernel,
        out_shape=(piece, piece, jax.ShapeDtypeStruct(frames.shape, BF)),
        in_specs=[pl.BlockSpec(memory_space=pltpu.SMEM)] + vmem(1),
        out_specs=tuple(vmem(3)),
        compiler_params=params(),
        name="row_pieces",
    )(pos, frames)


def cols_kernel(pos, offs, frames, got_first, got_second, first, second, center, one, ext):
    rows, cols, ch = frames.shape[1:]
    below = even(pos[0])
    block = pos[0] * rows // BLK
    last = pos[2] - 1
    ext[HALO : HALO + rows] = frames[1]
    one[1 : rows + 1] = frames[0]
    for ref, low in ((got_first, below), (got_second, jnp.logical_not(below))):
        ext[pl.ds(jnp.where(low, HALO + rows, 0), HALO)] = ref[0:HALO]
        one[jnp.where(low, rows + 1, 0)] = ref[HALO]
    center[...] = ext[pl.ds(offs[block * pos[2] + pos[1], 0] + MAXOFF, WROWS + 2)]
    right = even(pos[1])
    col = lax.broadcasted_iota(jnp.int32, (rows + 2, 16, ch), 1)
    for ref, side in ((first, right), (second, jnp.logical_not(right))):
        other = jnp.clip(jnp.where(side, pos[1] + 1, pos[1] - 1), 0, last)
        start = offs[block * pos[2] + other, 0] + MAXOFF
        at = pl.multiple_of(jnp.where(side, cols - 16, 0), 16)
        ref[...] = ext[pl.ds(start, WROWS + 2), pl.ds(at, 16)]
        border = one[:, pl.ds(at, 16)].astype(F32)
        border = jnp.where(side, border[:, 15:16], border[:, 0:1])
        spare = jnp.where(side, 0, 15)
        ref[0 : rows + 2] = jnp.where(col == spare, border, ref[0 : rows + 2].astype(F32)).astype(BF)


def col_pieces(pos, offs, frames, got):
    rows, cols, ch = frames.shape[1:]
    piece = jax.ShapeDtypeStruct((WROWS + 2, 16, ch), BF)
    return pl.pallas_call(
        cols_kernel,
        out_shape=(
            piece,
            piece,
            jax.ShapeDtypeStruct((WROWS + 2, cols, ch), BF),
            jax.ShapeDtypeStruct((rows + 2, cols, ch), BF),
        ),
        in_specs=[pl.BlockSpec(memory_space=pltpu.SMEM)] * 2 + vmem(3),
        out_specs=tuple(vmem(4)),
        scratch_shapes=[pltpu.VMEM((rows + 2 * HALO, cols, ch), BF)],
        compiler_params=params(),
        name="col_pieces",
    )(pos, offs, frames, *got)


def swap(pieces, axes, count):
    got = []
    for piece, start in zip(pieces, (0, 1)):
        pairs = []
        for i in range(start, count - 1, 2):
            pairs += [(i, i + 1), (i + 1, i)]
        got.append(lax.ppermute(piece, axes, pairs))
    return got


def band_kernel(cot, bt, b, lines):
    count, rows, cols = cot.shape
    lanes = GROUP * BLK

    def iota(shape, axis):
        return lax.broadcasted_iota(jnp.int32, shape, axis)

    copy = (iota((cols, lanes), 1) % cols == iota((cols, lanes), 0)).astype(F32).astype(BF)
    wide = jnp.dot(cot[...].reshape(count * rows, cols), copy, preferred_element_type=F32)
    shape = (WIN * 16, count * rows)
    q, d = iota(shape, 0), iota(shape, 1) // rows
    pickd = ((q // 16 * WIN + q % 16 == d) & (q % 16 < WIN)).astype(F32).astype(BF)
    line = iota((count * rows, lanes), 0) % rows
    want = iota((count * rows, lanes), 1) // cols
    gap = iota((PITCH, lanes), 0) - iota((PITCH, lanes), 1) % BLK
    own = iota((16, lanes), 1) // BLK
    for g in range(bt.shape[0]):
        mine = jnp.where(line == want + g * GROUP, wide, 0.0).astype(BF)
        lines[...] = jnp.dot(pickd, mine, preferred_element_type=F32)
        for r in range(GROWS):
            pick = jnp.zeros((16, lanes), F32)
            for yy in range(GROUP):
                a = r - yy
                if 0 <= a < WIN:
                    pick = jnp.where(own == yy, lines[a * 16 : (a + 1) * 16], pick)
            block = jnp.zeros((PITCH, lanes), F32)
            for k in range(WIN):
                block = jnp.where(gap == k, pick[k : k + 1], block)
            bt[g, r * PITCH : (r + 1) * PITCH] = block.astype(BF)
        b[g] = bt[g].astype(F32).T.astype(BF)


def band(cot):
    groups = cot.shape[1] // GROUP
    return pl.pallas_call(
        band_kernel,
        out_shape=(
            jax.ShapeDtypeStruct((groups, GROWS * PITCH, GROUP * BLK), BF),
            jax.ShapeDtypeStruct((groups, GROUP * BLK, GROWS * PITCH), BF),
        ),
        in_specs=vmem(1),
        out_specs=tuple(vmem(2)),
        scratch_shapes=[pltpu.VMEM((WIN * 16, GROUP * BLK), F32)],
        compiler_params=params(),
        cost_estimate=pl.CostEstimate(flops=2_000_000_000, bytes_accessed=1_000_000, transcendentals=0),
        name="band",
    )(cot)


def main_kernel(
    row_count, col_count, pieces,
    pos, offs, center, one, got_first, got_second, weight, bias, bt, b,
    keep, send, f1, f2,
    ext2, ext1, xc2, xc1, pre2, pre1, gwin, dsh2, dsh1, dc2, dc1, ft2, ft1, total,
):
    rows, cols, ch = one.shape[0] - 2, one.shape[1], one.shape[2]
    height, width = row_count * rows, col_count * cols
    inv_root = ch ** (-0.5)
    block = pos[0] * rows // BLK
    oy, ox = offs[block * pos[2] + pos[1], 0], offs[block * pos[2] + pos[1], 1]
    c0, gy0, gx0 = ox + 16 - RAD - 1, pos[0] * rows + oy - RAD, pos[1] * cols + ox - RAD
    right = even(pos[1])
    ext2[:, 16 : 16 + cols] = center[...].astype(F32)
    v_first, v_second = got_first[...].astype(F32), got_second[...].astype(F32)
    for value, side in ((v_first, right), (v_second, jnp.logical_not(right))):
        ext2[:, pl.ds(pl.multiple_of(jnp.where(side, 16 + cols, 0), 16), 16)] = value
    ext2[:, 32 + cols :] = jnp.zeros((WROWS + 2, ext2.shape[1] - 32 - cols, ch), F32)
    ext1[:, 0:8] = jnp.zeros((rows + 2, 8, ch), F32)
    ext1[:, 8 + cols :] = jnp.zeros((rows + 2, ext1.shape[1] - 8 - cols, ch), F32)
    ext1[:, 8 : 8 + cols] = one[...].astype(F32)
    ext1[:, 7:8] = jnp.where(right, v_second[0 : rows + 2, 0:1], v_first[0 : rows + 2, 0:1])
    ext1[:, 8 + cols : 9 + cols] = jnp.where(right, v_first[0 : rows + 2, 15:16], v_second[0 : rows + 2, 15:16])

    span = PITCH + 8
    base = pl.multiple_of((c0 // 8) * 8, 8)
    turn = span - c0 % 8

    def gather(r, carry):
        row = pltpu.roll(ext2[r, pl.ds(base, span), :], turn, 0)
        for j in range(3):
            xc2[r, :, j * ch : (j + 1) * ch] = row[j : j + PITCH].astype(BF)
        return carry

    lax.fori_loop(0, WROWS + 2, gather, 0)
    for j in range(3):
        xc1[:, :, j * ch : (j + 1) * ch] = ext1[:, 7 + j : 7 + j + cols].astype(BF)

    shift = bias[...]
    step = 8

    def conv_two(n, carry):
        acc = jnp.zeros((step * PITCH, ch), F32)
        for i in range(3):
            x = xc2[pl.ds(n * step + i, step)].reshape(step * PITCH, 3 * ch)
            acc = acc + jnp.dot(x, weight[i], preferred_element_type=F32)
        acc = (acc + shift).reshape(step, PITCH, ch)
        y = lax.broadcasted_iota(jnp.int32, acc.shape, 0) + n * step + gy0
        c = lax.broadcasted_iota(jnp.int32, acc.shape, 1)
        x = c + gx0
        ok = (y >= 0) & (y < height) & (x >= 0) & (x < width) & (c < WCOLS)
        acc = jnp.maximum(jnp.where(ok, acc, 0.0), 0.0).reshape(step * PITCH, ch)
        pre2[pl.ds(n * step * PITCH, step * PITCH)] = acc
        f2[pl.ds(n * step * PITCH, step * PITCH)] = acc.astype(BF)
        return carry

    lax.fori_loop(0, WROWS // step, conv_two, 0)

    def conv_one(n, carry):
        acc = jnp.zeros((step * cols, ch), F32)
        for i in range(3):
            x = xc1[pl.ds(n * step + i, step)].reshape(step * cols, 3 * ch)
            acc = acc + jnp.dot(x, weight[i], preferred_element_type=F32)
        acc = jnp.maximum(acc + shift, 0.0)
        pre1[pl.ds(n * step * cols, step * cols)] = acc
        f1[pl.ds(n * step * cols, step * cols)] = acc.astype(BF)
        return carry

    lax.fori_loop(0, rows // step, conv_one, 0)

    ft2[...] = xc2[:, :, 0:ch].reshape((WROWS + 2) * PITCH, ch).T
    ft1[...] = ext1[:, 7 : 7 + PITCH].astype(BF).reshape((rows + 2) * PITCH, ch).T

    gwin[...] = jnp.zeros(gwin.shape, F32)
    dsh1[...] = jnp.zeros(dsh1.shape, F32)
    lanes = GROUP * cols
    bsum = jnp.zeros((1, ch), F32)
    for g in range(rows // GROUP):
        at = slice(g * GROUP * PITCH, (g * GROUP + GROWS) * PITCH)
        px = slice(g * lanes, (g + 1) * lanes)
        gwin[at] += jnp.dot(bt[g], f1[px], preferred_element_type=F32)
        one = jnp.dot(b[g], f2[at], preferred_element_type=F32) * inv_root
        one = jnp.where(pre1[px] > 0, one, 0.0).astype(BF).astype(F32)
        bsum = bsum + jnp.sum(one, axis=0, keepdims=True)
        dsh1[g * GROUP : (g + 1) * GROUP, 8 : 8 + cols] = one.reshape(GROUP, cols, ch)
    two = jnp.where(pre2[...] > 0, gwin[...] * inv_root, 0.0)
    bsum = bsum + jnp.sum(two, axis=0, keepdims=True)
    dsh2[:, 0:8] = jnp.zeros((WROWS, 8, ch), F32)
    dsh2[:, 8 : 8 + PITCH] = two.reshape(WROWS, PITCH, ch)
    for ref, src, n in ((dc2, dsh2, WROWS), (dc1, dsh1, rows)):
        ref[0:2] = jnp.zeros((2,) + ref.shape[1:], BF)
        ref[n + 2 : n + 4] = jnp.zeros((2,) + ref.shape[1:], BF)
        for j in range(3):
            ref[2 : n + 2, :, j * ch : (j + 1) * ch] = src[:, 8 - j : 8 - j + PITCH].astype(BF)
    for i in range(3):
        n2, n1 = WROWS + 2, rows + 2
        acc = jnp.dot(
            ft2[...], dc2[2 - i : 2 - i + n2].reshape(n2 * PITCH, 3 * ch), preferred_element_type=F32
        )
        acc = acc + jnp.dot(
            ft1[...], dc1[2 - i : 2 - i + n1].reshape(n1 * PITCH, 3 * ch), preferred_element_type=F32
        )
        for j in range(3):
            total[(3 * i + j) * ch : (3 * i + j + 1) * ch] = acc[:, j * ch : (j + 1) * ch]
    size = 9 * ch // pieces
    half = 9 * ch // 2
    tail = bias_rows(bsum)
    for p in range(pieces // 2):
        for ref, which in ((keep, pos[3]), (send, 1 - pos[3])):
            at = pl.multiple_of(which * half + p * size, 8)
            last = tail if p == 0 else jnp.zeros((8, ch), F32)
            ref[p] = jnp.concatenate([total[pl.ds(at, size)], last], axis=0).astype(ref.dtype)


def bias_rows(value):
    high = value.astype(BF).astype(F32)
    row = lax.broadcasted_iota(jnp.int32, (8, value.shape[1]), 0)
    return jnp.where(row == 0, high, jnp.where(row == 1, value - high, 0.0))


def main(pos, offs, center, one, got, weight, bias, bt, b, row_count, col_count, pieces):
    rows, cols, ch = one.shape[0] - 2, one.shape[1], one.shape[2]
    wpx, n2, n1 = WROWS * PITCH, WROWS + 2, rows + 2
    size = 9 * ch // pieces + 8
    return pl.pallas_call(
        functools.partial(main_kernel, row_count, col_count, pieces),
        out_shape=(
            jax.ShapeDtypeStruct((pieces // 2, size, ch), F32),
            jax.ShapeDtypeStruct((pieces // 2, size, ch), BF),
            jax.ShapeDtypeStruct((rows * cols, ch), BF),
            jax.ShapeDtypeStruct((wpx, ch), BF),
        ),
        in_specs=[pl.BlockSpec(memory_space=pltpu.SMEM)] * 2 + vmem(8),
        out_specs=tuple(vmem(4)),
        scratch_shapes=[
            pltpu.VMEM((n2, cols + 48, ch), F32),
            pltpu.VMEM((n1, 56, ch), F32),
            pltpu.VMEM((n2, PITCH, 3 * ch), BF),
            pltpu.VMEM((n1, cols, 3 * ch), BF),
            pltpu.VMEM((wpx, ch), F32),
            pltpu.VMEM((rows * cols, ch), F32),
            pltpu.VMEM((wpx, ch), F32),
            pltpu.VMEM((WROWS, 64, ch), F32),
            pltpu.VMEM((rows, 64, ch), F32),
            pltpu.VMEM((WROWS + 4, PITCH, 3 * ch), BF),
            pltpu.VMEM((rows + 4, PITCH, 3 * ch), BF),
            pltpu.VMEM((ch, n2 * PITCH), BF),
            pltpu.VMEM((ch, n1 * PITCH), BF),
            pltpu.VMEM((9 * ch, ch), F32),
        ],
        compiler_params=params(),
        cost_estimate=pl.CostEstimate(flops=5_000_000_000, bytes_accessed=8_000_000, transcendentals=0),
        name="main",
    )(pos, offs, center, one, *got, weight, bias, bt, b)


def corr_kernel(f1, f2, out):
    lanes = GROUP * BLK
    inv_root = f1.shape[1] ** (-0.5)
    lane = lax.broadcasted_iota(jnp.int32, (PITCH, lanes), 1)
    gap = lax.broadcasted_iota(jnp.int32, (PITCH, lanes), 0) - lane % BLK
    own = lane // BLK
    for g in range(f1.shape[0] // lanes):
        at = slice(g * GROUP * PITCH, (g * GROUP + GROWS) * PITCH)
        scores = lax.dot_general(
            f2[at], f1[g * lanes : (g + 1) * lanes], (((1,), (1,)), ((), ())),
            preferred_element_type=F32,
        )
        for a in range(WIN):
            pick = scores[a * PITCH : (a + 1) * PITCH]
            for yy in range(1, GROUP):
                pick = jnp.where(own == yy, scores[(a + yy) * PITCH : (a + yy + 1) * PITCH], pick)
            for d in range(WIN):
                line = jnp.sum(jnp.where(gap == d, pick, 0.0), axis=0, keepdims=True) * inv_root
                out[a * WIN + d : a * WIN + d + 1, g * lanes : (g + 1) * lanes] = line


def correlate(f1, f2):
    return pl.pallas_call(
        corr_kernel,
        out_shape=jax.ShapeDtypeStruct((WIN * WIN, f1.shape[0]), F32),
        in_specs=vmem(2),
        out_specs=vmem(1)[0],
        compiler_params=params(),
        cost_estimate=pl.CostEstimate(flops=300_000_000, bytes_accessed=1_000_000, transcendentals=0),
        name="corr",
    )(f1, f2)


def sum_kernel(parts, out):
    size = parts.shape[1]
    for s in range(0, size, 8):
        value = parts[0, s : s + 8].astype(F32)
        for n in range(1, parts.shape[0]):
            value = value + parts[n, s : s + 8].astype(F32)
        if s == size - 8:
            value = bias_rows(value[0:1] + value[1:2])
        value = value.astype(BF)
        for k in range(out.shape[0]):
            out[k, s : s + 8] = value


def sum_and_copy(parts, copies):
    return pl.pallas_call(
        sum_kernel,
        out_shape=jax.ShapeDtypeStruct((copies,) + parts.shape[1:], BF),
        in_specs=vmem(1),
        out_specs=vmem(1)[0],
        compiler_params=params(),
        name="sum",
    )(parts)


def merge_kernel(kept, got, out):
    size = kept.shape[1]
    for p in range(kept.shape[0]):
        value = kept[p] + got[p].astype(F32)
        if p == 0:
            tail = value[size - 8 :]
            value = jnp.concatenate([value[0 : size - 8], bias_rows(tail[0:1] + tail[1:2])], axis=0)
        out[p] = value.astype(BF)


def merge(kept, got):
    return pl.pallas_call(
        merge_kernel,
        out_shape=jax.ShapeDtypeStruct(got.shape, BF),
        in_specs=vmem(2),
        out_specs=vmem(1)[0],
        compiler_params=params(),
        name="merge",
    )(kept, got)


def unpack_kernel(pos, own, other, grad, bias):
    size = own.shape[1] - 8
    half = own.shape[0] * size
    for ref, which in ((own, pos[3]), (other, 1 - pos[3])):
        for p in range(own.shape[0]):
            grad[pl.ds(pl.multiple_of(which * half + p * size, 8), size)] = ref[p, 0:size].astype(F32)
    first = jnp.where(pos[3] == 0, own[0, size:].astype(F32), other[0, size:].astype(F32))
    bias[...] = first[0:1] + first[1:2]


def unpack(pos, own, other):
    pieces, size, ch = own.shape
    return pl.pallas_call(
        unpack_kernel,
        out_shape=(
            jax.ShapeDtypeStruct((2 * pieces * (size - 8), ch), F32),
            jax.ShapeDtypeStruct((1, ch), F32),
        ),
        in_specs=[pl.BlockSpec(memory_space=pltpu.SMEM)] + vmem(2),
        out_specs=tuple(vmem(2)),
        compiler_params=params(),
        name="unpack",
    )(pos, own, other)


def shards(row_count, col_count, space, group, frames, offsets, weight, bias, cotangent):
    rows, cols, ch = frames.shape[2:]
    pos = jnp.stack(
        [lax.axis_index("row"), lax.axis_index(space), jnp.int32(col_count), lax.axis_index("core")]
    ).astype(jnp.int32)
    offs = offsets.reshape(-1, 2)
    *sent, kept = row_pieces(pos, frames[0])
    got = swap(sent, "row", row_count)
    bt, b = band(cotangent[0])
    first, second, center, one = col_pieces(pos, offs, kept, got)
    got = swap((first, second), space, col_count)
    count = int(np.prod([lax.axis_size(a) for a in group]))
    kept, sent, f1, f2 = main(
        pos, offs, center, one, got, weight.reshape(3, 3 * ch, ch), bias.reshape(1, ch), bt, b,
        row_count, col_count, 2 * count,
    )
    cores = [(0, 1), (1, 0)]
    parts = merge(kept, lax.ppermute(sent, "core", cores))
    parts = lax.all_to_all(parts, group, 0, 0, tiled=True)
    corr = correlate(f1, f2)
    corr = corr.reshape(1, WIN * WIN, rows, cols).astype(BF)
    parts = lax.all_to_all(sum_and_copy(parts, lax.axis_size("z")), "z", 0, 0, tiled=True)
    parts = lax.all_to_all(sum_and_copy(parts, count), group, 0, 0, tiled=True)
    grad_w, grad_b = unpack(pos, parts, lax.ppermute(parts, "core", cores))
    return corr, grad_w.reshape(3, 3, ch, ch), grad_b.reshape(ch)


def solution(mesh):
    row_count, col_count, pair_count = (mesh.shape[a] for a in ("row", "col", "pair"))
    high = 2 if col_count == 16 else 1
    fine = Mesh(
        mesh.devices.reshape(row_count, high, col_count // high, pair_count // 2, 2),
        ("row", "high", "z", "low", "core"),
    )
    col, pair = ("high", "z"), ("low", "core")
    return jax.shard_map(
        functools.partial(shards, row_count, col_count, col, ("row", "high", "low")),
        mesh=fine,
        in_specs=(
            P(pair, None, "row", col, None),
            P(pair, None, None, None),
            P(),
            P(),
            P(pair, None, "row", col),
        ),
        out_specs=(P(pair, None, "row", col), P(), P()),
        check_vma=False,
    )
```

```python
import functools

import jax
import jax.numpy as jnp
import numpy as np
from jax import lax
from jax.experimental import pallas as pl
from jax.experimental.pallas import tpu as pltpu
from jax.sharding import Mesh
from jax.sharding import PartitionSpec as P

BLK = 32
RAD = 4
MAXOFF = 8
WIN = 2 * RAD + 1
HALO = MAXOFF + RAD + 1
PITCH = 40
WROWS = 24
GROUP = 4
GROWS = GROUP + WIN - 1
BF = jnp.bfloat16
F32 = jnp.float32


def vmem(n):
    return [pl.BlockSpec(memory_space=pltpu.VMEM)] * n


def params(mib=16):
    return pltpu.CompilerParams(vmem_limit_bytes=mib * 1024 * 1024)


def smem(n):
    return [pl.BlockSpec(memory_space=pltpu.SMEM)] * n


def even(index):
    return lax.rem(index, 2) == 0


def rows_kernel(pos, frames, first, second, kept, sems):
    rows = frames.shape[1]
    below = even(pos[0])
    copies = []
    for ref, low in ((first, below), (second, jnp.logical_not(below))):
        copies.append((frames.at[1, pl.ds(jnp.where(low, rows - HALO, 0), HALO)], ref.at[0:HALO]))
        copies.append((frames.at[0, pl.ds(jnp.where(low, rows - 1, 0), 1)], ref.at[HALO : HALO + 1]))
    copies.append((frames, kept))
    copies = [pltpu.make_async_copy(src, dst, sems.at[n]) for n, (src, dst) in enumerate(copies)]
    for copy in copies:
        copy.start()
    for copy in copies:
        copy.wait()


def row_pieces(pos, frames):
    cols, ch = frames.shape[2:]
    piece = jax.ShapeDtypeStruct((HALO + 1, cols, ch), BF)
    return pl.pallas_call(
        rows_kernel,
        out_shape=(piece, piece, jax.ShapeDtypeStruct(frames.shape, BF)),
        in_specs=smem(1) + [pl.BlockSpec(memory_space=pltpu.HBM)],
        out_specs=tuple(vmem(3)),
        scratch_shapes=[pltpu.SemaphoreType.DMA((5,))],
        compiler_params=params(),
        name="row_pieces",
    )(pos, frames)


def cols_kernel(pos, offs, frames, got_first, got_second, first, second, center, one, ext):
    rows, cols, ch = frames.shape[1:]
    below = even(pos[0])
    block = pos[0] * rows // BLK
    last = pos[2] - 1
    ext[HALO : HALO + rows] = frames[1]
    one[1 : rows + 1] = frames[0]
    for ref, low in ((got_first, below), (got_second, jnp.logical_not(below))):
        ext[pl.ds(jnp.where(low, HALO + rows, 0), HALO)] = ref[0:HALO]
        one[jnp.where(low, rows + 1, 0)] = ref[HALO]
    center[...] = ext[pl.ds(offs[block * pos[2] + pos[1], 0] + MAXOFF, WROWS + 2)]
    right = even(pos[1])
    col = lax.broadcasted_iota(jnp.int32, (rows + 2, 16, ch), 1)
    for ref, side in ((first, right), (second, jnp.logical_not(right))):
        other = jnp.clip(jnp.where(side, pos[1] + 1, pos[1] - 1), 0, last)
        start = offs[block * pos[2] + other, 0] + MAXOFF
        at = pl.multiple_of(jnp.where(side, cols - 16, 0), 16)
        ref[...] = ext[pl.ds(start, WROWS + 2), pl.ds(at, 16)]
        border = one[:, pl.ds(at, 16)].astype(F32)
        border = jnp.where(side, border[:, 15:16], border[:, 0:1])
        spare = jnp.where(side, 0, 15)
        ref[0 : rows + 2] = jnp.where(col == spare, border, ref[0 : rows + 2].astype(F32)).astype(BF)


def col_pieces(pos, offs, frames, got):
    rows, cols, ch = frames.shape[1:]
    piece = jax.ShapeDtypeStruct((WROWS + 2, 16, ch), BF)
    return pl.pallas_call(
        cols_kernel,
        out_shape=(
            piece,
            piece,
            jax.ShapeDtypeStruct((WROWS + 2, cols, ch), BF),
            jax.ShapeDtypeStruct((rows + 2, cols, ch), BF),
        ),
        in_specs=[pl.BlockSpec(memory_space=pltpu.SMEM)] * 2 + vmem(3),
        out_specs=tuple(vmem(4)),
        scratch_shapes=[pltpu.VMEM((rows + 2 * HALO, cols, ch), BF)],
        compiler_params=params(),
        name="col_pieces",
    )(pos, offs, frames, *got)


def swap(pieces, axes, count):
    got = []
    for piece, start in ((pieces[1], 1), (pieces[0], 0)):
        pairs = []
        for i in range(start, count - 1, 2):
            pairs += [(i, i + 1), (i + 1, i)]
        got.append(lax.ppermute(piece, axes, pairs))
    return got[::-1]


def band_kernel(cot, bt, b, lines):
    count, rows, cols = cot.shape
    lanes = GROUP * BLK

    def iota(shape, axis):
        return lax.broadcasted_iota(jnp.int32, shape, axis)

    copy = (iota((cols, lanes), 1) % cols == iota((cols, lanes), 0)).astype(F32).astype(BF)
    wide = jnp.dot(cot[...].reshape(count * rows, cols), copy, preferred_element_type=F32)
    shape = (WIN * 16, count * rows)
    q, d = iota(shape, 0), iota(shape, 1) // rows
    pickd = ((q // 16 * WIN + q % 16 == d) & (q % 16 < WIN)).astype(F32).astype(BF)
    line = iota((count * rows, lanes), 0) % rows
    want = iota((count * rows, lanes), 1) // cols
    gap = iota((PITCH, lanes), 0) - iota((PITCH, lanes), 1) % BLK
    own = iota((16, lanes), 1) // BLK
    for g in range(bt.shape[0]):
        mine = jnp.where(line == want + g * GROUP, wide, 0.0).astype(BF)
        lines[...] = jnp.dot(pickd, mine, preferred_element_type=F32)
        for r in range(GROWS):
            pick = jnp.zeros((16, lanes), F32)
            for yy in range(GROUP):
                a = r - yy
                if 0 <= a < WIN:
                    pick = jnp.where(own == yy, lines[a * 16 : (a + 1) * 16], pick)
            block = jnp.zeros((PITCH, lanes), F32)
            for k in range(WIN):
                block = jnp.where(gap == k, pick[k : k + 1], block)
            bt[g, r * PITCH : (r + 1) * PITCH] = block.astype(BF)
        b[g] = bt[g].astype(F32).T.astype(BF)


def band(cot):
    groups = cot.shape[1] // GROUP
    return pl.pallas_call(
        band_kernel,
        out_shape=(
            jax.ShapeDtypeStruct((groups, GROWS * PITCH, GROUP * BLK), BF),
            jax.ShapeDtypeStruct((groups, GROUP * BLK, GROWS * PITCH), BF),
        ),
        in_specs=vmem(1),
        out_specs=tuple(vmem(2)),
        scratch_shapes=[pltpu.VMEM((WIN * 16, GROUP * BLK), F32)],
        compiler_params=params(),
        cost_estimate=pl.CostEstimate(flops=2_000_000_000, bytes_accessed=1_000_000, transcendentals=0),
        name="band",
    )(cot)


def main_kernel(
    row_count, col_count,
    pos, offs, center, one, got_first, got_second, weight, bias, bt, b,
    keep, send, f1, f2,
    ext2, ext1, xc2, xc1, pre2, pre1, gwin, d1, total,
):
    rows, cols, ch = one.shape[0] - 2, one.shape[1], one.shape[2]
    height, width = row_count * rows, col_count * cols
    inv_root = ch ** (-0.5)
    block = pos[0] * rows // BLK
    oy, ox = offs[block * pos[2] + pos[1], 0], offs[block * pos[2] + pos[1], 1]
    c0, gy0, gx0 = ox + 16 - RAD - 1, pos[0] * rows + oy - RAD, pos[1] * cols + ox - RAD
    right = even(pos[1])
    ext2[:, 16 : 16 + cols] = center[...].astype(F32)
    v_first, v_second = got_first[...].astype(F32), got_second[...].astype(F32)
    for value, side in ((v_first, right), (v_second, jnp.logical_not(right))):
        ext2[:, pl.ds(pl.multiple_of(jnp.where(side, 16 + cols, 0), 16), 16)] = value
    ext2[:, 32 + cols :] = jnp.zeros((WROWS + 2, ext2.shape[1] - 32 - cols, ch), F32)
    ext1[:, 0:8] = jnp.zeros((rows + 2, 8, ch), F32)
    ext1[:, 8 + cols :] = jnp.zeros((rows + 2, ext1.shape[1] - 8 - cols, ch), F32)
    ext1[:, 8 : 8 + cols] = one[...].astype(F32)
    ext1[:, 7:8] = jnp.where(right, v_second[0 : rows + 2, 0:1], v_first[0 : rows + 2, 0:1])
    ext1[:, 8 + cols : 9 + cols] = jnp.where(right, v_first[0 : rows + 2, 15:16], v_second[0 : rows + 2, 15:16])

    span = PITCH + 16
    base = pl.multiple_of((c0 // 8) * 8, 8)
    turn = span - c0 % 8

    def gather(r, carry):
        row = pltpu.roll(ext2[r, pl.ds(base, span), :], turn, 0)
        for j in range(3):
            xc2[r, :, j * ch : (j + 1) * ch] = row[j : j + PITCH].astype(BF)
        return carry

    lax.fori_loop(0, WROWS + 2, gather, 0)
    for j in range(3):
        xc1[:, :, j * ch : (j + 1) * ch] = ext1[:, 7 + j : 7 + j + cols].astype(BF)

    shift = bias[...]
    step = 8

    def conv_two(n, carry):
        acc = jnp.zeros((step * PITCH, ch), F32)
        for i in range(3):
            x = xc2[pl.ds(n * step + i, step)].reshape(step * PITCH, 3 * ch)
            acc = acc + jnp.dot(x, weight[i], preferred_element_type=F32)
        acc = (acc + shift).reshape(step, PITCH, ch)
        y = lax.broadcasted_iota(jnp.int32, acc.shape, 0) + n * step + gy0
        x = lax.broadcasted_iota(jnp.int32, acc.shape, 1) + gx0
        ok = (y >= 0) & (y < height) & (x >= 0) & (x < width)
        acc = jnp.maximum(jnp.where(ok, acc, 0.0), 0.0).reshape(step * PITCH, ch)
        pre2[pl.ds(n * step * PITCH, step * PITCH)] = acc
        f2[pl.ds(n * step * PITCH, step * PITCH)] = acc.astype(BF)
        return carry

    lax.fori_loop(0, WROWS // step, conv_two, 0)

    def conv_one(n, carry):
        acc = jnp.zeros((step * cols, ch), F32)
        for i in range(3):
            x = xc1[pl.ds(n * step + i, step)].reshape(step * cols, 3 * ch)
            acc = acc + jnp.dot(x, weight[i], preferred_element_type=F32)
        acc = jnp.maximum(acc + shift, 0.0)
        pre1[pl.ds(n * step * cols, step * cols)] = acc
        f1[pl.ds(n * step * cols, step * cols)] = acc.astype(BF)
        return carry

    lax.fori_loop(0, rows // step, conv_one, 0)

    gwin[...] = jnp.zeros(gwin.shape, F32)
    lanes = GROUP * cols
    bsum = jnp.zeros((1, ch), F32)
    for g in range(rows // GROUP):
        at = slice(g * GROUP * PITCH, (g * GROUP + GROWS) * PITCH)
        px = slice(g * lanes, (g + 1) * lanes)
        gwin[at] += jnp.dot(bt[g], f1[px], preferred_element_type=F32)
        delta = jnp.dot(b[g], f2[at], preferred_element_type=F32) * inv_root
        delta = jnp.where(pre1[px] > 0, delta, 0.0).astype(BF)
        d1[px] = delta
        bsum = bsum + jnp.sum(delta.astype(F32), axis=0, keepdims=True)
    delta = jnp.where(pre2[...] > 0, gwin[...] * inv_root, 0.0)
    bsum = bsum + jnp.sum(delta, axis=0, keepdims=True)
    d2t, d1t = delta.astype(BF).T, d1[...].T
    for i in range(3):
        x2 = xc2[i : i + WROWS].reshape(WROWS * PITCH, 3 * ch)
        x1 = xc1[i : i + rows].reshape(rows * cols, 3 * ch)
        total[i] = jnp.dot(d2t, x2, preferred_element_type=F32) + jnp.dot(
            d1t, x1, preferred_element_type=F32
        )
    half = ch // 2
    for ref, which in ((keep, pos[3]), (send, 1 - pos[3])):
        at = pl.ds(pl.multiple_of(which * half, half), half)
        for t in range(9):
            ref[t * half : (t + 1) * half] = total[t // 3, at, t % 3 * ch : (t % 3 + 1) * ch].astype(ref.dtype)
        ref[9 * half : 9 * half + 8] = bias_rows(bsum).astype(ref.dtype)
        ref[9 * half + 8 :] = jnp.zeros((ref.shape[0] - 9 * half - 8, ch), ref.dtype)


def bias_rows(value):
    high = value.astype(BF).astype(F32)
    row = lax.broadcasted_iota(jnp.int32, (8, value.shape[1]), 0)
    return jnp.where(row == 0, high, jnp.where(row == 1, value - high, 0.0))


def main(pos, offs, center, one, got, weight, bias, bt, b, row_count, col_count, flat):
    rows, cols, ch = one.shape[0] - 2, one.shape[1], one.shape[2]
    wpx, n2, n1 = WROWS * PITCH, WROWS + 2, rows + 2
    return pl.pallas_call(
        functools.partial(main_kernel, row_count, col_count),
        out_shape=(
            jax.ShapeDtypeStruct((flat, ch), F32),
            jax.ShapeDtypeStruct((flat, ch), BF),
            jax.ShapeDtypeStruct((rows * cols, ch), BF),
            jax.ShapeDtypeStruct((wpx, ch), BF),
        ),
        in_specs=smem(2) + vmem(8),
        out_specs=tuple(vmem(4)),
        scratch_shapes=[
            pltpu.VMEM((n2, cols + 48, ch), F32),
            pltpu.VMEM((n1, 56, ch), F32),
            pltpu.VMEM((n2, PITCH, 3 * ch), BF),
            pltpu.VMEM((n1, cols, 3 * ch), BF),
            pltpu.VMEM((wpx, ch), F32),
            pltpu.VMEM((rows * cols, ch), F32),
            pltpu.VMEM((wpx, ch), F32),
            pltpu.VMEM((rows * cols, ch), BF),
            pltpu.VMEM((3, ch, 3 * ch), F32),
        ],
        compiler_params=params(28),
        cost_estimate=pl.CostEstimate(flops=5_000_000_000, bytes_accessed=8_000_000, transcendentals=0),
        name="main",
    )(pos, offs, center, one, *got, weight, bias, bt, b)


def corr_kernel(f1, f2, out):
    lanes = GROUP * BLK
    inv_root = f1.shape[1] ** (-0.5)
    lane = lax.broadcasted_iota(jnp.int32, (PITCH, lanes), 1)
    gap = lax.broadcasted_iota(jnp.int32, (PITCH, lanes), 0) - lane % BLK
    own = lane // BLK
    for g in range(f1.shape[0] // lanes):
        at = slice(g * GROUP * PITCH, (g * GROUP + GROWS) * PITCH)
        scores = lax.dot_general(
            f2[at], f1[g * lanes : (g + 1) * lanes], (((1,), (1,)), ((), ())),
            preferred_element_type=F32,
        )
        for a in range(WIN):
            pick = scores[a * PITCH : (a + 1) * PITCH]
            for yy in range(1, GROUP):
                pick = jnp.where(own == yy, scores[(a + yy) * PITCH : (a + yy + 1) * PITCH], pick)
            for d in range(WIN):
                line = jnp.sum(jnp.where(gap == d, pick, 0.0), axis=0, keepdims=True) * inv_root
                out[a * WIN + d : a * WIN + d + 1, g * lanes : (g + 1) * lanes] = line


def correlate(f1, f2):
    return pl.pallas_call(
        corr_kernel,
        out_shape=jax.ShapeDtypeStruct((WIN * WIN, f1.shape[0]), F32),
        in_specs=vmem(2),
        out_specs=vmem(1)[0],
        compiler_params=params(),
        cost_estimate=pl.CostEstimate(flops=300_000_000, bytes_accessed=1_000_000, transcendentals=0),
        name="corr",
    )(f1, f2)


def sum_kernel(rows, pos, parts, out):
    size = parts.shape[1]
    for s in range(0, size, 8):
        value = parts[0, s : s + 8].astype(F32)
        for n in range(1, parts.shape[0]):
            value = value + parts[n, s : s + 8].astype(F32)
        if s == rows % size:
            value = jnp.where(pos[4] == rows // size, bias_rows(value[0:1] + value[1:2]), value)
        value = value.astype(BF)
        for k in range(out.shape[0]):
            out[k, s : s + 8] = value


def sum_and_copy(pos, parts, copies, rows):
    return pl.pallas_call(
        functools.partial(sum_kernel, rows),
        out_shape=jax.ShapeDtypeStruct((copies,) + parts.shape[1:], BF),
        in_specs=smem(1) + vmem(1),
        out_specs=vmem(1)[0],
        compiler_params=params(),
        name="sum",
    )(pos, parts)


def merge_kernel(rows, kept, got, out):
    out[...] = (kept[...] + got[...].astype(F32)).astype(BF)
    tail = kept[rows : rows + 8] + got[rows : rows + 8].astype(F32)
    out[rows : rows + 8] = bias_rows(tail[0:1] + tail[1:2]).astype(BF)


def merge(kept, got, rows):
    return pl.pallas_call(
        functools.partial(merge_kernel, rows),
        out_shape=jax.ShapeDtypeStruct(got.shape, BF),
        in_specs=vmem(2),
        out_specs=vmem(1)[0],
        compiler_params=params(),
        name="merge",
    )(kept, got)


def unpack_kernel(pos, own, other, grad, bias):
    ch = own.shape[1]
    half = ch // 2
    for ref, which in ((own, pos[3]), (other, 1 - pos[3])):
        at = pl.ds(pl.multiple_of(which * half, half), half)
        for t in range(9):
            grad[t * ch : (t + 1) * ch, at] = ref[t * half : (t + 1) * half].astype(F32).T
    rows = slice(9 * half, 9 * half + 8)
    first = jnp.where(pos[3] == 0, own[rows].astype(F32), other[rows].astype(F32))
    bias[...] = first[0:1] + first[1:2]


def unpack(pos, own, other):
    ch = own.shape[1]
    return pl.pallas_call(
        unpack_kernel,
        out_shape=(
            jax.ShapeDtypeStruct((9 * ch, ch), F32),
            jax.ShapeDtypeStruct((1, ch), F32),
        ),
        in_specs=smem(1) + vmem(2),
        out_specs=tuple(vmem(2)),
        compiler_params=params(),
        name="unpack",
    )(pos, own, other)


def shards(row_count, col_count, space, group, frames, offsets, weight, bias, cotangent):
    rows, cols, ch = frames.shape[2:]
    pos = jnp.stack(
        [
            lax.axis_index("row"),
            lax.axis_index(space),
            jnp.int32(col_count),
            lax.axis_index("core"),
            lax.axis_index(group),
        ]
    ).astype(jnp.int32)
    offs = offsets.reshape(-1, 2)
    *sent, kept = row_pieces(pos, frames[0])
    got = swap(sent, "row", row_count)
    bt, b = band(cotangent[0])
    first, second, center, one = col_pieces(pos, offs, kept, got)
    got = swap((first, second), space, col_count)
    count = int(np.prod([lax.axis_size(a) for a in group]))
    depth = lax.axis_size("z")
    half = 9 * ch // 2
    size = (half + 8 + 8 * count - 1) // (8 * count) * 8
    kept, sent, f1, f2 = main(
        pos, offs, center, one, got, weight.reshape(3, 3 * ch, ch), bias.reshape(1, ch), bt, b,
        row_count, col_count, size * count,
    )
    cores = [(0, 1), (1, 0)]
    parts = merge(kept, lax.ppermute(sent, "core", cores), half)
    parts = lax.all_to_all(parts.reshape(count, size, ch), group, 0, 0, tiled=True)
    corr = correlate(f1, f2)
    corr = corr.reshape(1, WIN * WIN, rows, cols).astype(BF)
    parts = lax.all_to_all(sum_and_copy(pos, parts, depth, half), "z", 0, 0, tiled=True)
    parts = lax.all_to_all(sum_and_copy(pos, parts, count, half), group, 0, 0, tiled=True)
    parts = parts.reshape(count * size, ch)
    grad_w, grad_b = unpack(pos, parts, lax.ppermute(parts, "core", cores))
    return corr, grad_w.reshape(3, 3, ch, ch), grad_b.reshape(ch)


def solution(mesh):
    row_count, col_count, pair_count = (mesh.shape[a] for a in ("row", "col", "pair"))
    high = 2 if col_count == 16 else 1
    fine = Mesh(
        mesh.devices.reshape(row_count, high, col_count // high, pair_count // 2, 2),
        ("row", "high", "z", "low", "core"),
    )
    col, pair = ("high", "z"), ("low", "core")
    return jax.shard_map(
        functools.partial(shards, row_count, col_count, col, ("row", "high", "low")),
        mesh=fine,
        in_specs=(
            P(pair, None, "row", col, None),
            P(pair, None, None, None),
            P(),
            P(),
            P(pair, None, "row", col),
        ),
        out_specs=(P(pair, None, "row", col), P(), P()),
        check_vma=False,
    )
```

```python
import functools

import jax
import jax.numpy as jnp
import numpy as np
from jax import lax
from jax.experimental import pallas as pl
from jax.experimental.pallas import tpu as pltpu
from jax.sharding import Mesh
from jax.sharding import PartitionSpec as P

BLK = 32
RAD = 4
MAXOFF = 8
WIN = 2 * RAD + 1
HALO = MAXOFF + RAD + 1
PITCH = 40
WROWS = 24
GROUP = 4
GROWS = GROUP + WIN - 1
BF = jnp.bfloat16
F32 = jnp.float32


def vmem(n):
    return [pl.BlockSpec(memory_space=pltpu.VMEM)] * n


def params(mib=16):
    return pltpu.CompilerParams(vmem_limit_bytes=mib * 1024 * 1024)


def smem(n):
    return [pl.BlockSpec(memory_space=pltpu.SMEM)] * n


def even(index):
    return lax.rem(index, 2) == 0


def rows_kernel(pos, frames, first, second, kept):
    rows = frames.shape[1]
    below = even(pos[0])
    for ref, low in ((first, below), (second, jnp.logical_not(below))):
        ref[0:HALO] = frames[1, pl.ds(jnp.where(low, rows - HALO, 0), HALO)]
        ref[HALO] = frames[0, jnp.where(low, rows - 1, 0)]
    kept[...] = frames[...]


def row_pieces(pos, frames):
    cols, ch = frames.shape[2:]
    piece = jax.ShapeDtypeStruct((HALO + 1, cols, ch), BF)
    return pl.pallas_call(
        rows_kernel,
        out_shape=(piece, piece, jax.ShapeDtypeStruct(frames.shape, BF)),
        in_specs=smem(1) + vmem(1),
        out_specs=tuple(vmem(3)),
        compiler_params=params(),
        name="row_pieces",
    )(pos, frames)


def cols_kernel(pos, offs, frames, got_first, got_second, second, first, center, one, ext):
    rows, cols, ch = frames.shape[1:]
    below = even(pos[0])
    block = pos[0] * rows // BLK
    last = pos[2] - 1
    ext[HALO : HALO + rows] = frames[1]
    one[1 : rows + 1] = frames[0]
    for ref, low in ((got_first, below), (got_second, jnp.logical_not(below))):
        ext[pl.ds(jnp.where(low, HALO + rows, 0), HALO)] = ref[0:HALO]
        one[jnp.where(low, rows + 1, 0)] = ref[HALO]
    center[...] = ext[pl.ds(offs[block * pos[2] + pos[1], 0] + MAXOFF, WROWS + 2)]
    right = even(pos[1])
    col = lax.broadcasted_iota(jnp.int32, (rows + 2, 16, ch), 1)
    for ref, side in ((first, right), (second, jnp.logical_not(right))):
        other = jnp.clip(jnp.where(side, pos[1] + 1, pos[1] - 1), 0, last)
        start = offs[block * pos[2] + other, 0] + MAXOFF
        at = pl.multiple_of(jnp.where(side, cols - 16, 0), 16)
        ref[...] = ext[pl.ds(start, WROWS + 2), pl.ds(at, 16)]
        border = one[:, pl.ds(at, 16)].astype(F32)
        border = jnp.where(side, border[:, 15:16], border[:, 0:1])
        spare = jnp.where(side, 0, 15)
        ref[0 : rows + 2] = jnp.where(col == spare, border, ref[0 : rows + 2].astype(F32)).astype(BF)


def col_pieces(pos, offs, frames, got):
    rows, cols, ch = frames.shape[1:]
    piece = jax.ShapeDtypeStruct((WROWS + 2, 16, ch), BF)
    return pl.pallas_call(
        cols_kernel,
        out_shape=(
            piece,
            piece,
            jax.ShapeDtypeStruct((WROWS + 2, cols, ch), BF),
            jax.ShapeDtypeStruct((rows + 2, cols, ch), BF),
        ),
        in_specs=[pl.BlockSpec(memory_space=pltpu.SMEM)] * 2 + vmem(3),
        out_specs=tuple(vmem(4)),
        scratch_shapes=[pltpu.VMEM((rows + 2 * HALO, cols, ch), BF)],
        compiler_params=params(),
        name="col_pieces",
    )(pos, offs, frames, *got)


def swap(pieces, axes, count):
    got = []
    for piece, start in ((pieces[1], 1), (pieces[0], 0)):
        pairs = []
        for i in range(start, count - 1, 2):
            pairs += [(i, i + 1), (i + 1, i)]
        got.append(lax.ppermute(piece, axes, pairs))
    return got[::-1]


def band_kernel(cot, bt, b, lines):
    count, rows, cols = cot.shape
    lanes = GROUP * BLK

    def iota(shape, axis):
        return lax.broadcasted_iota(jnp.int32, shape, axis)

    copy = (iota((cols, lanes), 1) % cols == iota((cols, lanes), 0)).astype(F32).astype(BF)
    wide = jnp.dot(cot[...].reshape(count * rows, cols), copy, preferred_element_type=F32)
    shape = (WIN * 16, count * rows)
    q, d = iota(shape, 0), iota(shape, 1) // rows
    pickd = ((q // 16 * WIN + q % 16 == d) & (q % 16 < WIN)).astype(F32).astype(BF)
    line = iota((count * rows, lanes), 0) % rows
    want = iota((count * rows, lanes), 1) // cols
    gap = iota((PITCH, lanes), 0) - iota((PITCH, lanes), 1) % BLK
    own = iota((16, lanes), 1) // BLK
    for g in range(bt.shape[0]):
        mine = jnp.where(line == want + g * GROUP, wide, 0.0).astype(BF)
        lines[...] = jnp.dot(pickd, mine, preferred_element_type=F32)
        for r in range(GROWS):
            pick = jnp.zeros((16, lanes), F32)
            for yy in range(GROUP):
                a = r - yy
                if 0 <= a < WIN:
                    pick = jnp.where(own == yy, lines[a * 16 : (a + 1) * 16], pick)
            block = jnp.zeros((PITCH, lanes), F32)
            for k in range(WIN):
                block = jnp.where(gap == k, pick[k : k + 1], block)
            bt[g, r * PITCH : (r + 1) * PITCH] = block.astype(BF)
        b[g] = bt[g].astype(F32).T.astype(BF)


def band(cot):
    groups = cot.shape[1] // GROUP
    return pl.pallas_call(
        band_kernel,
        out_shape=(
            jax.ShapeDtypeStruct((groups, GROWS * PITCH, GROUP * BLK), BF),
            jax.ShapeDtypeStruct((groups, GROUP * BLK, GROWS * PITCH), BF),
        ),
        in_specs=vmem(1),
        out_specs=tuple(vmem(2)),
        scratch_shapes=[pltpu.VMEM((WIN * 16, GROUP * BLK), F32)],
        compiler_params=params(),
        cost_estimate=pl.CostEstimate(flops=2_000_000_000, bytes_accessed=1_000_000, transcendentals=0),
        name="band",
    )(cot)


def main_kernel(
    row_count, col_count,
    pos, offs, center, one, got_first, got_second, weight, bias, bt, b,
    keep, send, f1, f2,
    ext2, ext1, xc2, xc1, pre2, pre1, gwin, d1, total,
):
    rows, cols, ch = one.shape[0] - 2, one.shape[1], one.shape[2]
    height, width = row_count * rows, col_count * cols
    inv_root = ch ** (-0.5)
    block = pos[0] * rows // BLK
    oy, ox = offs[block * pos[2] + pos[1], 0], offs[block * pos[2] + pos[1], 1]
    c0, gy0, gx0 = ox + 16 - RAD - 1, pos[0] * rows + oy - RAD, pos[1] * cols + ox - RAD
    right = even(pos[1])
    ext2[:, 16 : 16 + cols] = center[...].astype(F32)
    v_first, v_second = got_first[...].astype(F32), got_second[...].astype(F32)
    for value, side in ((v_first, right), (v_second, jnp.logical_not(right))):
        ext2[:, pl.ds(pl.multiple_of(jnp.where(side, 16 + cols, 0), 16), 16)] = value
    ext2[:, 32 + cols :] = jnp.zeros((WROWS + 2, ext2.shape[1] - 32 - cols, ch), F32)
    ext1[:, 0:8] = jnp.zeros((rows + 2, 8, ch), F32)
    ext1[:, 8 + cols :] = jnp.zeros((rows + 2, ext1.shape[1] - 8 - cols, ch), F32)
    ext1[:, 8 : 8 + cols] = one[...].astype(F32)
    ext1[:, 7:8] = jnp.where(right, v_second[0 : rows + 2, 0:1], v_first[0 : rows + 2, 0:1])
    ext1[:, 8 + cols : 9 + cols] = jnp.where(right, v_first[0 : rows + 2, 15:16], v_second[0 : rows + 2, 15:16])

    span = PITCH + 16
    base = pl.multiple_of((c0 // 8) * 8, 8)
    turn = span - c0 % 8

    def gather(r, carry):
        row = pltpu.roll(ext2[r, pl.ds(base, span), :], turn, 0)
        for j in range(3):
            xc2[r, :, j * ch : (j + 1) * ch] = row[j : j + PITCH].astype(BF)
        return carry

    lax.fori_loop(0, WROWS + 2, gather, 0)
    for j in range(3):
        xc1[:, :, j * ch : (j + 1) * ch] = ext1[:, 7 + j : 7 + j + cols].astype(BF)

    shift = bias[...]
    step = 8

    def conv_two(n, carry):
        acc = jnp.zeros((step * PITCH, ch), F32)
        for i in range(3):
            x = xc2[pl.ds(n * step + i, step)].reshape(step * PITCH, 3 * ch)
            acc = acc + jnp.dot(x, weight[i], preferred_element_type=F32)
        acc = (acc + shift).reshape(step, PITCH, ch)
        y = lax.broadcasted_iota(jnp.int32, acc.shape, 0) + n * step + gy0
        x = lax.broadcasted_iota(jnp.int32, acc.shape, 1) + gx0
        ok = (y >= 0) & (y < height) & (x >= 0) & (x < width)
        acc = jnp.maximum(jnp.where(ok, acc, 0.0), 0.0).reshape(step * PITCH, ch)
        pre2[pl.ds(n * step * PITCH, step * PITCH)] = acc
        f2[pl.ds(n * step * PITCH, step * PITCH)] = acc.astype(BF)
        return carry

    lax.fori_loop(0, WROWS // step, conv_two, 0)

    def conv_one(n, carry):
        acc = jnp.zeros((step * cols, ch), F32)
        for i in range(3):
            x = xc1[pl.ds(n * step + i, step)].reshape(step * cols, 3 * ch)
            acc = acc + jnp.dot(x, weight[i], preferred_element_type=F32)
        acc = jnp.maximum(acc + shift, 0.0)
        pre1[pl.ds(n * step * cols, step * cols)] = acc
        f1[pl.ds(n * step * cols, step * cols)] = acc.astype(BF)
        return carry

    lax.fori_loop(0, rows // step, conv_one, 0)

    gwin[...] = jnp.zeros(gwin.shape, F32)
    lanes = GROUP * cols
    bsum = jnp.zeros((1, ch), F32)
    for g in range(rows // GROUP):
        at = slice(g * GROUP * PITCH, (g * GROUP + GROWS) * PITCH)
        px = slice(g * lanes, (g + 1) * lanes)
        gwin[at] += jnp.dot(bt[g], f1[px], preferred_element_type=F32)
        delta = jnp.dot(b[g], f2[at], preferred_element_type=F32) * inv_root
        delta = jnp.where(pre1[px] > 0, delta, 0.0).astype(BF)
        d1[px] = delta
        bsum = bsum + jnp.sum(delta.astype(F32), axis=0, keepdims=True)
    delta = jnp.where(pre2[...] > 0, gwin[...] * inv_root, 0.0)
    bsum = bsum + jnp.sum(delta, axis=0, keepdims=True)
    d2t, d1t = delta.astype(BF).T, d1[...].T
    for i in range(3):
        x2 = xc2[i : i + WROWS].reshape(WROWS * PITCH, 3 * ch)
        x1 = xc1[i : i + rows].reshape(rows * cols, 3 * ch)
        total[i] = jnp.dot(d2t, x2, preferred_element_type=F32) + jnp.dot(
            d1t, x1, preferred_element_type=F32
        )
    half = ch // 2
    for ref, which in ((keep, pos[3]), (send, 1 - pos[3])):
        at = pl.ds(pl.multiple_of(which * half, half), half)
        for t in range(9):
            ref[t * half : (t + 1) * half] = total[t // 3, at, t % 3 * ch : (t % 3 + 1) * ch].astype(ref.dtype)
        ref[9 * half : 9 * half + 8] = bias_rows(bsum).astype(ref.dtype)
        ref[9 * half + 8 :] = jnp.zeros((ref.shape[0] - 9 * half - 8, ch), ref.dtype)


def bias_rows(value):
    high = value.astype(BF).astype(F32)
    row = lax.broadcasted_iota(jnp.int32, (8, value.shape[1]), 0)
    return jnp.where(row == 0, high, jnp.where(row == 1, value - high, 0.0))


def main(pos, offs, center, one, got, weight, bias, bt, b, row_count, col_count, flat):
    rows, cols, ch = one.shape[0] - 2, one.shape[1], one.shape[2]
    wpx, n2, n1 = WROWS * PITCH, WROWS + 2, rows + 2
    return pl.pallas_call(
        functools.partial(main_kernel, row_count, col_count),
        out_shape=(
            jax.ShapeDtypeStruct((flat, ch), F32),
            jax.ShapeDtypeStruct((flat, ch), BF),
            jax.ShapeDtypeStruct((rows * cols, ch), BF),
            jax.ShapeDtypeStruct((wpx, ch), BF),
        ),
        in_specs=smem(2) + vmem(8),
        out_specs=tuple(vmem(4)),
        scratch_shapes=[
            pltpu.VMEM((n2, cols + 48, ch), F32),
            pltpu.VMEM((n1, 56, ch), F32),
            pltpu.VMEM((n2, PITCH, 3 * ch), BF),
            pltpu.VMEM((n1, cols, 3 * ch), BF),
            pltpu.VMEM((wpx, ch), F32),
            pltpu.VMEM((rows * cols, ch), F32),
            pltpu.VMEM((wpx, ch), F32),
            pltpu.VMEM((rows * cols, ch), BF),
            pltpu.VMEM((3, ch, 3 * ch), F32),
        ],
        compiler_params=params(28),
        cost_estimate=pl.CostEstimate(flops=5_000_000_000, bytes_accessed=8_000_000, transcendentals=0),
        name="main",
    )(pos, offs, center, one, *got, weight, bias, bt, b)


def corr_kernel(f1, f2, out):
    lanes = GROUP * BLK
    inv_root = f1.shape[1] ** (-0.5)
    lane = lax.broadcasted_iota(jnp.int32, (PITCH, lanes), 1)
    gap = lax.broadcasted_iota(jnp.int32, (PITCH, lanes), 0) - lane % BLK
    own = lane // BLK
    for g in range(f1.shape[0] // lanes):
        at = slice(g * GROUP * PITCH, (g * GROUP + GROWS) * PITCH)
        scores = lax.dot_general(
            f2[at], f1[g * lanes : (g + 1) * lanes], (((1,), (1,)), ((), ())),
            preferred_element_type=F32,
        )
        for a in range(WIN):
            pick = scores[a * PITCH : (a + 1) * PITCH]
            for yy in range(1, GROUP):
                pick = jnp.where(own == yy, scores[(a + yy) * PITCH : (a + yy + 1) * PITCH], pick)
            for d in range(WIN):
                line = jnp.sum(jnp.where(gap == d, pick, 0.0), axis=0, keepdims=True) * inv_root
                out[a * WIN + d : a * WIN + d + 1, g * lanes : (g + 1) * lanes] = line


def correlate(f1, f2):
    return pl.pallas_call(
        corr_kernel,
        out_shape=jax.ShapeDtypeStruct((WIN * WIN, f1.shape[0]), F32),
        in_specs=vmem(2),
        out_specs=vmem(1)[0],
        compiler_params=params(),
        cost_estimate=pl.CostEstimate(flops=300_000_000, bytes_accessed=1_000_000, transcendentals=0),
        name="corr",
    )(f1, f2)


def sum_kernel(rows, pos, parts, out):
    size = parts.shape[1]
    for s in range(0, size, 8):
        value = parts[0, s : s + 8].astype(F32)
        for n in range(1, parts.shape[0]):
            value = value + parts[n, s : s + 8].astype(F32)
        if s == rows % size:
            value = jnp.where(pos[4] == rows // size, bias_rows(value[0:1] + value[1:2]), value)
        value = value.astype(BF)
        for k in range(out.shape[0]):
            out[k, s : s + 8] = value


def sum_and_copy(pos, parts, copies, rows):
    return pl.pallas_call(
        functools.partial(sum_kernel, rows),
        out_shape=jax.ShapeDtypeStruct((copies,) + parts.shape[1:], BF),
        in_specs=smem(1) + vmem(1),
        out_specs=vmem(1)[0],
        compiler_params=params(),
        name="sum",
    )(pos, parts)


def merge_kernel(rows, kept, got, out):
    out[...] = (kept[...] + got[...].astype(F32)).astype(BF)
    tail = kept[rows : rows + 8] + got[rows : rows + 8].astype(F32)
    out[rows : rows + 8] = bias_rows(tail[0:1] + tail[1:2]).astype(BF)


def merge(kept, got, rows):
    return pl.pallas_call(
        functools.partial(merge_kernel, rows),
        out_shape=jax.ShapeDtypeStruct(got.shape, BF),
        in_specs=vmem(2),
        out_specs=vmem(1)[0],
        compiler_params=params(),
        name="merge",
    )(kept, got)


def unpack_kernel(pos, own, other, grad, bias):
    ch = own.shape[1]
    half = ch // 2
    for ref, which in ((own, pos[3]), (other, 1 - pos[3])):
        at = pl.ds(pl.multiple_of(which * half, half), half)
        for t in range(9):
            grad[t * ch : (t + 1) * ch, at] = ref[t * half : (t + 1) * half].astype(F32).T
    rows = slice(9 * half, 9 * half + 8)
    first = jnp.where(pos[3] == 0, own[rows].astype(F32), other[rows].astype(F32))
    bias[...] = first[0:1] + first[1:2]


def unpack(pos, own, other):
    ch = own.shape[1]
    return pl.pallas_call(
        unpack_kernel,
        out_shape=(
            jax.ShapeDtypeStruct((9 * ch, ch), F32),
            jax.ShapeDtypeStruct((1, ch), F32),
        ),
        in_specs=smem(1) + vmem(2),
        out_specs=tuple(vmem(2)),
        compiler_params=params(),
        name="unpack",
    )(pos, own, other)


def shards(row_count, col_count, space, group, frames, offsets, weight, bias, cotangent):
    rows, cols, ch = frames.shape[2:]
    pos = jnp.stack(
        [
            lax.axis_index("row"),
            lax.axis_index(space),
            jnp.int32(col_count),
            lax.axis_index("core"),
            lax.axis_index(group),
        ]
    ).astype(jnp.int32)
    offs = offsets.reshape(-1, 2)
    *sent, kept = row_pieces(pos, frames[0])
    got = swap(sent, "row", row_count)
    bt, b = band(cotangent[0])
    second, first, center, one = col_pieces(pos, offs, kept, got)
    got = swap((first, second), space, col_count)
    count = int(np.prod([lax.axis_size(a) for a in group]))
    depth = lax.axis_size("zh")
    half = 9 * ch // 2
    size = (half + 8 + 8 * count - 1) // (8 * count) * 8
    kept, sent, f1, f2 = main(
        pos, offs, center, one, got, weight.reshape(3, 3 * ch, ch), bias.reshape(1, ch), bt, b,
        row_count, col_count, size * count,
    )
    cores = [(0, 1), (1, 0)]
    parts = merge(kept, lax.ppermute(sent, "core", cores), half)
    parts = lax.all_to_all(parts.reshape(count, size, ch), group, 0, 0, tiled=True)
    corr = correlate(f1, f2)
    corr = corr.reshape(1, WIN * WIN, rows, cols).astype(BF)
    parts = lax.all_to_all(sum_and_copy(pos, parts, depth, half), "zh", 0, 0, tiled=True)
    parts = lax.all_to_all(sum_and_copy(pos, parts, count, half), group, 0, 0, tiled=True)
    parts = parts.reshape(count * size, ch)
    grad_w, grad_b = unpack(pos, parts, lax.ppermute(parts, "core", cores))
    return corr, grad_w.reshape(3, 3, ch, ch), grad_b.reshape(ch)


def solution(mesh):
    row_count, col_count, pair_count = (mesh.shape[a] for a in ("row", "col", "pair"))
    high = 2 if col_count == 16 else 1
    near = 2 if col_count // high >= 4 else 1
    fine = Mesh(
        mesh.devices.reshape(row_count, high, col_count // high // near, near, pair_count // 2, 2),
        ("row", "high", "zh", "zl", "low", "core"),
    )
    col, pair = ("high", "zh", "zl"), ("low", "core")
    return jax.shard_map(
        functools.partial(shards, row_count, col_count, col, ("row", "high", "zl", "low")),
        mesh=fine,
        in_specs=(
            P(pair, None, "row", col, None),
            P(pair, None, None, None),
            P(),
            P(),
            P(pair, None, "row", col),
        ),
        out_specs=(P(pair, None, "row", col), P(), P()),
        check_vma=False,
    )
```

```python
import functools

import jax
import jax.numpy as jnp
import numpy as np
from jax import lax
from jax.experimental import pallas as pl
from jax.experimental.pallas import tpu as pltpu
from jax.sharding import Mesh
from jax.sharding import PartitionSpec as P

BLK = 32
RAD = 4
MAXOFF = 8
WIN = 2 * RAD + 1
HALO = MAXOFF + RAD + 1
PITCH = 40
WROWS = 24
GROUP = 4
GROWS = GROUP + WIN - 1
BF = jnp.bfloat16
F32 = jnp.float32


def vmem(n):
    return [pl.BlockSpec(memory_space=pltpu.VMEM)] * n


def params(mib=16):
    return pltpu.CompilerParams(vmem_limit_bytes=mib * 1024 * 1024)


def smem(n):
    return [pl.BlockSpec(memory_space=pltpu.SMEM)] * n


def even(index):
    return lax.rem(index, 2) == 0


def rows_kernel(pos, frames, first, second, kept):
    rows = frames.shape[1]
    below = even(pos[0])
    for ref, low in ((first, below), (second, jnp.logical_not(below))):
        ref[0:HALO] = frames[1, pl.ds(jnp.where(low, rows - HALO, 0), HALO)]
        ref[HALO] = frames[0, jnp.where(low, rows - 1, 0)]
    kept[...] = frames[...]


def row_pieces(pos, frames):
    cols, ch = frames.shape[2:]
    piece = jax.ShapeDtypeStruct((HALO + 1, cols, ch), BF)
    return pl.pallas_call(
        rows_kernel,
        out_shape=(piece, piece, jax.ShapeDtypeStruct(frames.shape, BF)),
        in_specs=smem(1) + vmem(1),
        out_specs=tuple(vmem(3)),
        compiler_params=params(),
        name="row_pieces",
    )(pos, frames)


def cols_kernel(pos, offs, frames, got_first, got_second, second, first, center, one, ext):
    rows, cols, ch = frames.shape[1:]
    below = even(pos[0])
    block = pos[0] * rows // BLK
    last = pos[2] - 1
    ext[HALO : HALO + rows] = frames[1]
    one[1 : rows + 1] = frames[0]
    for ref, low in ((got_first, below), (got_second, jnp.logical_not(below))):
        ext[pl.ds(jnp.where(low, HALO + rows, 0), HALO)] = ref[0:HALO]
        one[jnp.where(low, rows + 1, 0)] = ref[HALO]
    center[...] = ext[pl.ds(offs[block * pos[2] + pos[1], 0] + MAXOFF, WROWS + 2)]
    right = even(pos[1])
    col = lax.broadcasted_iota(jnp.int32, (rows + 2, 16, ch), 1)
    for ref, side in ((first, right), (second, jnp.logical_not(right))):
        other = jnp.clip(jnp.where(side, pos[1] + 1, pos[1] - 1), 0, last)
        start = offs[block * pos[2] + other, 0] + MAXOFF
        at = pl.multiple_of(jnp.where(side, cols - 16, 0), 16)
        ref[...] = ext[pl.ds(start, WROWS + 2), pl.ds(at, 16)]
        border = one[:, pl.ds(at, 16)].astype(F32)
        border = jnp.where(side, border[:, 15:16], border[:, 0:1])
        spare = jnp.where(side, 0, 15)
        ref[0 : rows + 2] = jnp.where(col == spare, border, ref[0 : rows + 2].astype(F32)).astype(BF)


def col_pieces(pos, offs, frames, got):
    rows, cols, ch = frames.shape[1:]
    piece = jax.ShapeDtypeStruct((WROWS + 2, 16, ch), BF)
    return pl.pallas_call(
        cols_kernel,
        out_shape=(
            piece,
            piece,
            jax.ShapeDtypeStruct((WROWS + 2, cols, ch), BF),
            jax.ShapeDtypeStruct((rows + 2, cols, ch), BF),
        ),
        in_specs=[pl.BlockSpec(memory_space=pltpu.SMEM)] * 2 + vmem(3),
        out_specs=tuple(vmem(4)),
        scratch_shapes=[pltpu.VMEM((rows + 2 * HALO, cols, ch), BF)],
        compiler_params=params(),
        name="col_pieces",
    )(pos, offs, frames, *got)


def swap(pieces, axes, count):
    got = []
    for piece, start in ((pieces[1], 1), (pieces[0], 0)):
        pairs = []
        for i in range(start, count - 1, 2):
            pairs += [(i, i + 1), (i + 1, i)]
        got.append(lax.ppermute(piece, axes, pairs))
    return got[::-1]


def band_kernel(cot, bt, b, lines):
    count, rows, cols = cot.shape
    lanes = GROUP * BLK

    def iota(shape, axis):
        return lax.broadcasted_iota(jnp.int32, shape, axis)

    copy = (iota((cols, lanes), 1) % cols == iota((cols, lanes), 0)).astype(F32).astype(BF)
    wide = jnp.dot(cot[...].reshape(count * rows, cols), copy, preferred_element_type=F32)
    shape = (WIN * 16, count * rows)
    q, d = iota(shape, 0), iota(shape, 1) // rows
    pickd = ((q // 16 * WIN + q % 16 == d) & (q % 16 < WIN)).astype(F32).astype(BF)
    line = iota((count * rows, lanes), 0) % rows
    want = iota((count * rows, lanes), 1) // cols
    gap = iota((PITCH, lanes), 0) - iota((PITCH, lanes), 1) % BLK
    own = iota((16, lanes), 1) // BLK
    for g in range(bt.shape[0]):
        mine = jnp.where(line == want + g * GROUP, wide, 0.0).astype(BF)
        lines[...] = jnp.dot(pickd, mine, preferred_element_type=F32)
        for r in range(GROWS):
            pick = jnp.zeros((16, lanes), F32)
            for yy in range(GROUP):
                a = r - yy
                if 0 <= a < WIN:
                    pick = jnp.where(own == yy, lines[a * 16 : (a + 1) * 16], pick)
            block = jnp.zeros((PITCH, lanes), F32)
            for k in range(WIN):
                block = jnp.where(gap == k, pick[k : k + 1], block)
            bt[g, r * PITCH : (r + 1) * PITCH] = block.astype(BF)
        b[g] = bt[g].astype(F32).T.astype(BF)


def band(cot):
    groups = cot.shape[1] // GROUP
    return pl.pallas_call(
        band_kernel,
        out_shape=(
            jax.ShapeDtypeStruct((groups, GROWS * PITCH, GROUP * BLK), BF),
            jax.ShapeDtypeStruct((groups, GROUP * BLK, GROWS * PITCH), BF),
        ),
        in_specs=vmem(1),
        out_specs=tuple(vmem(2)),
        scratch_shapes=[pltpu.VMEM((WIN * 16, GROUP * BLK), F32)],
        compiler_params=params(),
        cost_estimate=pl.CostEstimate(flops=2_000_000_000, bytes_accessed=1_000_000, transcendentals=0),
        name="band",
    )(cot)


def one_kernel(one, weight, bias, xc1, acc1, ext):
    rows, cols, ch = one.shape[0] - 2, one.shape[1], one.shape[2]
    ext[:, 0:8] = jnp.zeros((rows + 2, 8, ch), F32)
    ext[:, 8 + cols :] = jnp.zeros((rows + 2, 8, ch), F32)
    ext[:, 8 : 8 + cols] = one[...].astype(F32)
    for j in range(3):
        xc1[:, :, j * ch : (j + 1) * ch] = ext[:, 7 + j : 7 + j + cols].astype(BF)
    step = 8

    def conv(n, carry):
        acc = jnp.zeros((step * cols, ch), F32) + bias[...]
        for i in range(3):
            x = xc1[pl.ds(n * step + i, step)].reshape(step * cols, 3 * ch)
            acc = acc + jnp.dot(x, weight[i], preferred_element_type=F32)
        acc1[pl.ds(n * step, step)] = acc.reshape(step, cols, ch)
        return carry

    lax.fori_loop(0, rows // step, conv, 0)


def convolve_one(one, weight, bias):
    rows, cols, ch = one.shape[0] - 2, one.shape[1], one.shape[2]
    return pl.pallas_call(
        one_kernel,
        out_shape=(
            jax.ShapeDtypeStruct((rows + 2, cols, 3 * ch), BF),
            jax.ShapeDtypeStruct((rows, cols, ch), F32),
        ),
        in_specs=vmem(3),
        out_specs=tuple(vmem(2)),
        scratch_shapes=[pltpu.VMEM((rows + 2, cols + 16, ch), F32)],
        compiler_params=params(),
        cost_estimate=pl.CostEstimate(flops=1_500_000_000, bytes_accessed=1_000_000, transcendentals=0),
        name="one",
    )(one, weight, bias)


def half_grad(which, d2t, d1t, xc2, xc1, out):
    ch, rows, cols = d2t.shape[0], xc1.shape[0] - 2, xc1.shape[1]
    for i, lanes, base in (
        (2 * which, pl.ds(0, 3 * ch), 0),
        (1, pl.ds(pl.multiple_of(which * (3 * ch // 2), 128), 3 * ch // 2), 6),
    ):
        width = lanes.size
        x2 = xc2[pl.ds(i, WROWS), :, lanes].reshape(WROWS * PITCH, width)
        x1 = xc1[pl.ds(i, rows), :, lanes].reshape(rows * cols, width)
        acc = jnp.dot(d2t[...], x2, preferred_element_type=F32)
        acc = acc + jnp.dot(d1t[...], x1, preferred_element_type=F32)
        for k in range(width // 128):
            out[(base + k) * ch : (base + k + 1) * ch] = acc[:, k * 128 : (k + 1) * 128].astype(out.dtype)


def main_kernel(
    row_count, col_count,
    pos, offs, center, xc1_in, acc1, got_second, got_first, weight, bias, bt, b,
    send, tail, f1, f2, xc2, xc1, d2t, d1t,
    ext2, pre2, pre1, gwin, d1,
):
    rows, cols, ch = acc1.shape
    height, width = row_count * rows, col_count * cols
    inv_root = ch ** (-0.5)
    block = pos[0] * rows // BLK
    oy, ox = offs[block * pos[2] + pos[1], 0], offs[block * pos[2] + pos[1], 1]
    c0, gy0, gx0 = ox + 16 - RAD - 1, pos[0] * rows + oy - RAD, pos[1] * cols + ox - RAD
    right = even(pos[1])
    ext2[:, 16 : 16 + cols] = center[...].astype(F32)
    v_first, v_second = got_first[...].astype(F32), got_second[...].astype(F32)
    for value, side in ((v_first, right), (v_second, jnp.logical_not(right))):
        ext2[:, pl.ds(pl.multiple_of(jnp.where(side, 16 + cols, 0), 16), 16)] = value
    ext2[:, 32 + cols :] = jnp.zeros((WROWS + 2, ext2.shape[1] - 32 - cols, ch), F32)
    xc1[...] = xc1_in[...]
    pre1[...] = acc1[...]
    col = lax.broadcasted_iota(jnp.int32, (rows + 2, 8, ch), 1)
    n1 = rows + 2
    for j, spot, at, value in (
        (0, 0, 0, jnp.where(right, v_second[0:n1, 0:8], v_first[0:n1, 0:8])),
        (2, 7, cols - 8, jnp.where(right, v_first[0:n1, 8:16], v_second[0:n1, 8:16])),
    ):
        value = jnp.where(col == spot, value, 0.0)
        lanes = slice(j * ch, (j + 1) * ch)
        xc1[:, at : at + 8, lanes] = (xc1_in[:, at : at + 8, lanes].astype(F32) + value).astype(BF)
        value = value.astype(BF)
        acc = jnp.zeros((rows * 8, ch), F32)
        for i in range(3):
            x = value[i : i + rows].reshape(rows * 8, ch)
            acc = acc + jnp.dot(x, weight[i, j * ch : (j + 1) * ch], preferred_element_type=F32)
        pre1[:, at : at + 8] = acc1[:, at : at + 8] + acc.reshape(rows, 8, ch)
    f1[...] = jnp.maximum(pre1[...], 0.0).reshape(rows * cols, ch).astype(BF)

    span = PITCH + 16
    base = pl.multiple_of((c0 // 8) * 8, 8)
    turn = span - c0 % 8

    def gather(r, carry):
        row = pltpu.roll(ext2[r, pl.ds(base, span), :], turn, 0)
        for j in range(3):
            xc2[r, :, j * ch : (j + 1) * ch] = row[j : j + PITCH].astype(BF)
        return carry

    lax.fori_loop(0, WROWS + 2, gather, 0, unroll=2)

    shift = bias[...]
    step = 8

    def conv_two(n, carry):
        acc = jnp.zeros((step * PITCH, ch), F32)
        for i in range(3):
            x = xc2[pl.ds(n * step + i, step)].reshape(step * PITCH, 3 * ch)
            acc = acc + jnp.dot(x, weight[i], preferred_element_type=F32)
        acc = (acc + shift).reshape(step, PITCH, ch)
        y = lax.broadcasted_iota(jnp.int32, acc.shape, 0) + n * step + gy0
        x = lax.broadcasted_iota(jnp.int32, acc.shape, 1) + gx0
        ok = (y >= 0) & (y < height) & (x >= 0) & (x < width)
        acc = jnp.maximum(jnp.where(ok, acc, 0.0), 0.0).reshape(step * PITCH, ch)
        pre2[pl.ds(n * step * PITCH, step * PITCH)] = acc
        f2[pl.ds(n * step * PITCH, step * PITCH)] = acc.astype(BF)
        return carry

    lax.fori_loop(0, WROWS // step, conv_two, 0)

    gwin[...] = jnp.zeros(gwin.shape, F32)
    lanes = GROUP * cols
    bsum = jnp.zeros((1, ch), F32)
    for g in range(rows // GROUP):
        at = slice(g * GROUP * PITCH, (g * GROUP + GROWS) * PITCH)
        px = slice(g * lanes, (g + 1) * lanes)
        gwin[at] += jnp.dot(bt[g], f1[px], preferred_element_type=F32)
        delta = jnp.dot(b[g], f2[at], preferred_element_type=F32) * inv_root
        mine = pre1[g * GROUP : (g + 1) * GROUP].reshape(lanes, ch)
        delta = jnp.where(mine > 0, delta, 0.0).astype(BF)
        d1[px] = delta
        bsum = bsum + jnp.sum(delta.astype(F32), axis=0, keepdims=True)
    delta = jnp.where(pre2[...] > 0, gwin[...] * inv_root, 0.0)
    bsum = bsum + jnp.sum(delta, axis=0, keepdims=True)
    d2t[...] = delta.astype(BF).T
    d1t[...] = d1[...].T
    half_grad(1 - pos[3], d2t, d1t, xc2, xc1, send)
    tail[...] = bias_tile(bsum[:, 0:128], bsum[:, 128:])
    send[9 * ch : 9 * ch + 8] = tail[...].astype(BF)
    send[9 * ch + 8 :] = jnp.zeros((send.shape[0] - 9 * ch - 8, 128), BF)


def bias_tile(low, high):
    row = lax.broadcasted_iota(jnp.int32, (8, 128), 0)
    out = jnp.zeros((8, 128), F32)
    for n, value in enumerate((low, high)):
        top = value.astype(BF).astype(F32)
        out = jnp.where(row == n, top, jnp.where(row == n + 2, value - top, out))
    return out


def bias_again(value):
    return bias_tile(value[0:1] + value[2:3], value[1:2] + value[3:4])


def main(pos, offs, center, xc1, acc1, got, weight, bias, bt, b, row_count, col_count, flat):
    rows, cols, ch = acc1.shape
    wpx, n2 = WROWS * PITCH, WROWS + 2
    return pl.pallas_call(
        functools.partial(main_kernel, row_count, col_count),
        out_shape=(
            jax.ShapeDtypeStruct((flat, 128), BF),
            jax.ShapeDtypeStruct((8, 128), F32),
            jax.ShapeDtypeStruct((rows * cols, ch), BF),
            jax.ShapeDtypeStruct((wpx, ch), BF),
            jax.ShapeDtypeStruct((n2, PITCH, 3 * ch), BF),
            jax.ShapeDtypeStruct(xc1.shape, BF),
            jax.ShapeDtypeStruct((ch, wpx), BF),
            jax.ShapeDtypeStruct((ch, rows * cols), BF),
        ),
        in_specs=smem(2) + vmem(9),
        out_specs=tuple(vmem(8)),
        scratch_shapes=[
            pltpu.VMEM((n2, cols + 48, ch), F32),
            pltpu.VMEM((wpx, ch), F32),
            pltpu.VMEM((rows, cols, ch), F32),
            pltpu.VMEM((wpx, ch), F32),
            pltpu.VMEM((rows * cols, ch), BF),
        ],
        compiler_params=params(20),
        cost_estimate=pl.CostEstimate(flops=5_000_000_000, bytes_accessed=8_000_000, transcendentals=0),
        name="main",
    )(pos, offs, center, xc1, acc1, got[1], got[0], weight, bias, bt, b)


def keep_kernel(pos, tail, xc2, xc1, d2t, d1t, keep):
    ch = d2t.shape[0]
    half_grad(pos[3], d2t, d1t, xc2, xc1, keep)
    keep[9 * ch : 9 * ch + 8] = tail[...]
    keep[9 * ch + 8 :] = jnp.zeros((keep.shape[0] - 9 * ch - 8, 128), F32)


def keep_half(pos, tail, xc2, xc1, d2t, d1t, flat):
    return pl.pallas_call(
        keep_kernel,
        out_shape=jax.ShapeDtypeStruct((flat, 128), F32),
        in_specs=smem(1) + vmem(5),
        out_specs=vmem(1)[0],
        compiler_params=params(),
        cost_estimate=pl.CostEstimate(flops=1_000_000_000, bytes_accessed=1_000_000, transcendentals=0),
        name="keep",
    )(pos, tail, xc2, xc1, d2t, d1t)


def corr_kernel(f1, f2, out, token, lines):
    lanes = GROUP * BLK
    inv_root = f1.shape[1] ** (-0.5)
    lane = lax.broadcasted_iota(jnp.int32, (PITCH, lanes), 1)
    gap = lax.broadcasted_iota(jnp.int32, (PITCH, lanes), 0) - lane % BLK
    own = lane // BLK
    token[...] = jnp.zeros(token.shape, F32)
    lines[WIN * WIN - 1 :] = jnp.zeros((128 - WIN * WIN + 1, lanes), F32)
    for g in range(f1.shape[0] // lanes):
        at = slice(g * GROUP * PITCH, (g * GROUP + GROWS) * PITCH)
        scores = lax.dot_general(
            f2[at], f1[g * lanes : (g + 1) * lanes], (((1,), (1,)), ((), ())),
            preferred_element_type=F32,
        )
        for a in range(WIN):
            pick = scores[a * PITCH : (a + 1) * PITCH]
            for yy in range(1, GROUP):
                pick = jnp.where(own == yy, scores[(a + yy) * PITCH : (a + yy + 1) * PITCH], pick)
            for d in range(WIN):
                line = jnp.sum(jnp.where(gap == d, pick, 0.0), axis=0, keepdims=True) * inv_root
                lines[a * WIN + d : a * WIN + d + 1] = line
        out[g * lanes : (g + 1) * lanes] = lines[...].T[:, : WIN * WIN].astype(BF)


def correlate(f1, f2):
    return pl.pallas_call(
        corr_kernel,
        out_shape=(jax.ShapeDtypeStruct((f1.shape[0], WIN * WIN), BF), jax.ShapeDtypeStruct((8, 128), F32)),
        in_specs=vmem(2),
        out_specs=tuple(vmem(2)),
        scratch_shapes=[pltpu.VMEM((128, GROUP * BLK), F32)],
        compiler_params=params(),
        cost_estimate=pl.CostEstimate(flops=300_000_000, bytes_accessed=1_000_000, transcendentals=0),
        name="corr",
    )(f1, f2)


def sum_kernel(rows, pos, parts, out):
    size = parts.shape[1]
    for s in range(0, size, 8):
        value = parts[0, s : s + 8].astype(F32)
        for n in range(1, parts.shape[0]):
            value = value + parts[n, s : s + 8].astype(F32)
        if s == rows % size:
            value = jnp.where(pos[4] == rows // size, bias_again(value), value)
        value = value.astype(BF)
        for k in range(out.shape[0]):
            out[k, s : s + 8] = value


def sum_and_copy(pos, parts, copies, rows):
    return pl.pallas_call(
        functools.partial(sum_kernel, rows),
        out_shape=jax.ShapeDtypeStruct((copies,) + parts.shape[1:], BF),
        in_specs=smem(1) + vmem(1),
        out_specs=vmem(1)[0],
        compiler_params=params(),
        name="sum",
    )(pos, parts)


def merge_kernel(rows, kept, got, after, out):
    out[...] = (kept[...] + got[...].astype(F32)).astype(BF)
    tail = kept[rows : rows + 8] + got[rows : rows + 8].astype(F32)
    out[rows : rows + 8] = bias_again(tail).astype(BF)


def merge(kept, got, after, rows):
    return pl.pallas_call(
        functools.partial(merge_kernel, rows),
        out_shape=jax.ShapeDtypeStruct(got.shape, BF),
        in_specs=vmem(3),
        out_specs=vmem(1)[0],
        compiler_params=params(),
        name="merge",
    )(kept, got, after)


def unpack_half(which, part, held, grad, sems):
    ch = held.shape[1]
    for k in range(9):
        held[k * 128 : (k + 1) * 128] = part[k * ch : (k + 1) * ch].astype(F32).T
    full = grad.at[pl.ds(pl.multiple_of(which * 6 * ch, 128), 768)]
    rest = grad.at[pl.ds(pl.multiple_of(3 * ch + which * (3 * ch // 2), 128), 384)]
    copies = [
        pltpu.make_async_copy(held.at[0:768], full, sems.at[0]),
        pltpu.make_async_copy(held.at[768:1152], rest, sems.at[1]),
    ]
    for copy in copies:
        copy.start()
    for copy in copies:
        copy.wait()


def own_kernel(pos, own, grad, held, sems):
    unpack_half(pos[3], own, held, grad, sems)


def other_kernel(pos, own, other, grad_in, grad, bias, held, sems):
    unpack_half(1 - pos[3], other, held, grad, sems)
    rows = slice(9 * bias.shape[1], 9 * bias.shape[1] + 8)
    first = jnp.where(pos[3] == 0, own[rows].astype(F32), other[rows].astype(F32))
    bias[:, 0:128] = first[0:1] + first[2:3]
    bias[:, 128:] = first[1:2] + first[3:4]


def unpack(pos, own, other, ch):
    grad = jax.ShapeDtypeStruct((9 * ch, ch), F32)
    scratch = [pltpu.VMEM((9 * ch // 2, ch), F32), pltpu.SemaphoreType.DMA((2,))]
    outside = [pl.BlockSpec(memory_space=pl.ANY)]
    part = pl.pallas_call(
        own_kernel,
        out_shape=grad,
        in_specs=smem(1) + vmem(1),
        out_specs=outside[0],
        scratch_shapes=scratch,
        compiler_params=params(),
        cost_estimate=pl.CostEstimate(flops=10_000_000, bytes_accessed=3_000_000, transcendentals=0),
        name="unpack_own",
    )(pos, own)
    return pl.pallas_call(
        other_kernel,
        out_shape=(grad, jax.ShapeDtypeStruct((1, ch), F32)),
        in_specs=smem(1) + vmem(2) + outside,
        out_specs=tuple(outside + vmem(1)),
        scratch_shapes=scratch,
        input_output_aliases={3: 0},
        compiler_params=params(),
        name="unpack_other",
    )(pos, own, other, part)


def shards(row_count, col_count, space, group, frames, offsets, weight, bias, cotangent):
    rows, cols, ch = frames.shape[2:]
    pos = jnp.stack(
        [
            lax.axis_index("row"),
            lax.axis_index(space),
            jnp.int32(col_count),
            lax.axis_index("core"),
            lax.axis_index(group),
        ]
    ).astype(jnp.int32)
    offs = offsets.reshape(-1, 2)
    *sent, kept = row_pieces(pos, frames[0])
    got = swap(sent, "row", row_count)
    bt, b = band(cotangent[0])
    second, first, center, one = col_pieces(pos, offs, kept, got)
    got = swap((first, second), space, col_count)
    taps, bias = weight.reshape(3, 3 * ch, ch), bias.reshape(1, ch)
    xc1, acc1 = convolve_one(one, taps, bias)
    count = int(np.prod([lax.axis_size(a) for a in group]))
    depth = lax.axis_size("zh")
    half = 9 * ch
    size = (half + 8 + 8 * count - 1) // (8 * count) * 8
    sent, tail, f1, f2, *rest = main(
        pos, offs, center, xc1, acc1, got, taps, bias, bt, b, row_count, col_count, size * count
    )
    cores = [(0, 1), (1, 0)]
    got = lax.ppermute(sent, "core", cores)
    corr, token = correlate(f1, f2)
    kept = keep_half(pos, tail, *rest, size * count)
    parts = merge(kept, got, token, half)
    parts = lax.all_to_all(parts.reshape(count, size, 128), group, 0, 0, tiled=True)
    parts = lax.all_to_all(sum_and_copy(pos, parts, depth, half), "zh", 0, 0, tiled=True)
    parts = lax.all_to_all(sum_and_copy(pos, parts, count, half), group, 0, 0, tiled=True)
    parts = parts.reshape(count * size, 128)
    grad_w, grad_b = unpack(pos, parts, lax.ppermute(parts, "core", cores), ch)
    corr = jnp.transpose(corr.reshape(1, rows, cols, WIN * WIN), (0, 3, 1, 2))
    return corr, grad_w.reshape(3, 3, ch, ch), grad_b.reshape(ch)


def solution(mesh):
    row_count, col_count, pair_count = (mesh.shape[a] for a in ("row", "col", "pair"))
    high = 2 if col_count == 16 else 1
    near = 2 if col_count // high >= 4 else 1
    fine = Mesh(
        mesh.devices.reshape(row_count, high, col_count // high // near, near, pair_count // 2, 2),
        ("row", "high", "zh", "zl", "low", "core"),
    )
    col, pair = ("high", "zh", "zl"), ("low", "core")
    return jax.shard_map(
        functools.partial(shards, row_count, col_count, col, ("row", "high", "zl", "low")),
        mesh=fine,
        in_specs=(
            P(pair, None, "row", col, None),
            P(pair, None, None, None),
            P(),
            P(),
            P(pair, None, "row", col),
        ),
        out_specs=(P(pair, None, "row", col), P(), P()),
        check_vma=False,
    )
```

```python
import functools

import jax
import jax.numpy as jnp
import numpy as np
from jax import lax
from jax.experimental import pallas as pl
from jax.experimental.pallas import tpu as pltpu
from jax.sharding import Mesh
from jax.sharding import PartitionSpec as P

BLK = 32
RAD = 4
MAXOFF = 8
WIN = 2 * RAD + 1
HALO = MAXOFF + RAD + 1
PITCH = 40
WROWS = 24
GROUP = 4
GROWS = GROUP + WIN - 1
BF = jnp.bfloat16
F32 = jnp.float32


def vmem(n):
    return [pl.BlockSpec(memory_space=pltpu.VMEM)] * n


def params(mib=16):
    return pltpu.CompilerParams(vmem_limit_bytes=mib * 1024 * 1024)


def smem(n):
    return [pl.BlockSpec(memory_space=pltpu.SMEM)] * n


def even(index):
    return lax.rem(index, 2) == 0


def place(axes):
    index = 0
    for axis in axes:
        index = index * lax.axis_size(axis) + lax.axis_index(axis)
    return index


SPACE = ("high", "zh", "zl")
GROUP_AXES = ("row", "high", "zl", "low")


def rows_kernel(frames, first, second, kept):
    rows = frames.shape[1]
    below = even(lax.axis_index("row"))
    for ref, low in ((first, below), (second, jnp.logical_not(below))):
        ref[0:HALO] = frames[1, pl.ds(jnp.where(low, rows - HALO, 0), HALO)]
        ref[HALO] = frames[0, jnp.where(low, rows - 1, 0)]
    kept[...] = frames[...]


def row_pieces(frames):
    cols, ch = frames.shape[2:]
    piece = jax.ShapeDtypeStruct((HALO + 1, cols, ch), BF)
    return pl.pallas_call(
        rows_kernel,
        out_shape=(piece, piece, jax.ShapeDtypeStruct(frames.shape, BF)),
        in_specs=vmem(1),
        out_specs=tuple(vmem(3)),
        compiler_params=params(),
        name="row_pieces",
    )(frames)


def cols_kernel(offs, frames, got_first, got_second, second, first, center, one, ext):
    rows, cols, ch = frames.shape[1:]
    row, column = lax.axis_index("row"), place(SPACE)
    below = even(row)
    count = int(np.prod([lax.axis_size(a) for a in SPACE]))
    base = row * rows // BLK * count
    ext[HALO : HALO + rows] = frames[1]
    one[1 : rows + 1] = frames[0]
    for ref, low in ((got_first, below), (got_second, jnp.logical_not(below))):
        ext[pl.ds(jnp.where(low, HALO + rows, 0), HALO)] = ref[0:HALO]
        one[jnp.where(low, rows + 1, 0)] = ref[HALO]
    center[...] = ext[pl.ds(offs[base + column, 0] + MAXOFF, WROWS + 2)]
    right = even(column)
    col = lax.broadcasted_iota(jnp.int32, (rows + 2, 16, ch), 1)
    for ref, side in ((first, right), (second, jnp.logical_not(right))):
        other = jnp.clip(jnp.where(side, column + 1, column - 1), 0, count - 1)
        start = offs[base + other, 0] + MAXOFF
        at = pl.multiple_of(jnp.where(side, cols - 16, 0), 16)
        ref[...] = ext[pl.ds(start, WROWS + 2), pl.ds(at, 16)]
        border = one[:, pl.ds(at, 16)].astype(F32)
        border = jnp.where(side, border[:, 15:16], border[:, 0:1])
        spare = jnp.where(side, 0, 15)
        ref[0 : rows + 2] = jnp.where(col == spare, border, ref[0 : rows + 2].astype(F32)).astype(BF)


def col_pieces(offs, frames, got):
    rows, cols, ch = frames.shape[1:]
    piece = jax.ShapeDtypeStruct((WROWS + 2, 16, ch), BF)
    return pl.pallas_call(
        cols_kernel,
        out_shape=(
            piece,
            piece,
            jax.ShapeDtypeStruct((WROWS + 2, cols, ch), BF),
            jax.ShapeDtypeStruct((rows + 2, cols, ch), BF),
        ),
        in_specs=smem(1) + vmem(3),
        out_specs=tuple(vmem(4)),
        scratch_shapes=[pltpu.VMEM((rows + 2 * HALO, cols, ch), BF)],
        compiler_params=params(),
        name="col_pieces",
    )(offs, frames, *got)


def swap(pieces, axes, count):
    got = []
    for piece, start in ((pieces[1], 1), (pieces[0], 0)):
        pairs = []
        for i in range(start, count - 1, 2):
            pairs += [(i, i + 1), (i + 1, i)]
        got.append(lax.ppermute(piece, axes, pairs))
    return got[::-1]


def band_kernel(cot, bt, b, lines):
    count, rows, cols = cot.shape
    lanes = GROUP * BLK

    def iota(shape, axis):
        return lax.broadcasted_iota(jnp.int32, shape, axis)

    copy = (iota((cols, lanes), 1) % cols == iota((cols, lanes), 0)).astype(F32).astype(BF)
    wide = jnp.dot(cot[...].reshape(count * rows, cols), copy, preferred_element_type=F32)
    shape = (WIN * 16, count * rows)
    q, d = iota(shape, 0), iota(shape, 1) // rows
    pickd = ((q // 16 * WIN + q % 16 == d) & (q % 16 < WIN)).astype(F32).astype(BF)
    line = iota((count * rows, lanes), 0) % rows
    want = iota((count * rows, lanes), 1) // cols
    gap = iota((PITCH, lanes), 0) - iota((PITCH, lanes), 1) % BLK
    own = iota((16, lanes), 1) // BLK
    for g in range(bt.shape[0]):
        mine = jnp.where(line == want + g * GROUP, wide, 0.0).astype(BF)
        lines[...] = jnp.dot(pickd, mine, preferred_element_type=F32)
        for r in range(GROWS):
            pick = jnp.zeros((16, lanes), F32)
            for yy in range(GROUP):
                a = r - yy
                if 0 <= a < WIN:
                    pick = jnp.where(own == yy, lines[a * 16 : (a + 1) * 16], pick)
            block = jnp.zeros((PITCH, lanes), F32)
            for k in range(WIN):
                block = jnp.where(gap == k, pick[k : k + 1], block)
            bt[g, r * PITCH : (r + 1) * PITCH] = block.astype(BF)
        b[g] = bt[g].astype(F32).T.astype(BF)


def band(cot):
    groups = cot.shape[1] // GROUP
    return pl.pallas_call(
        band_kernel,
        out_shape=(
            jax.ShapeDtypeStruct((groups, GROWS * PITCH, GROUP * BLK), BF),
            jax.ShapeDtypeStruct((groups, GROUP * BLK, GROWS * PITCH), BF),
        ),
        in_specs=vmem(1),
        out_specs=tuple(vmem(2)),
        scratch_shapes=[pltpu.VMEM((WIN * 16, GROUP * BLK), F32)],
        compiler_params=params(),
        cost_estimate=pl.CostEstimate(flops=2_000_000_000, bytes_accessed=1_000_000, transcendentals=0),
        name="band",
    )(cot)


def one_kernel(one, weight, bias, xc1, acc1, ext):
    rows, cols, ch = one.shape[0] - 2, one.shape[1], one.shape[2]
    ext[:, 0:8] = jnp.zeros((rows + 2, 8, ch), F32)
    ext[:, 8 + cols :] = jnp.zeros((rows + 2, 8, ch), F32)
    ext[:, 8 : 8 + cols] = one[...].astype(F32)
    for j in range(3):
        xc1[:, :, j * ch : (j + 1) * ch] = ext[:, 7 + j : 7 + j + cols].astype(BF)
    step = 8

    def conv(n, carry):
        acc = jnp.zeros((step * cols, ch), F32) + bias[...]
        for i in range(3):
            x = xc1[pl.ds(n * step + i, step)].reshape(step * cols, 3 * ch)
            acc = acc + jnp.dot(x, weight[i], preferred_element_type=F32)
        acc1[pl.ds(n * step, step)] = acc.reshape(step, cols, ch)
        return carry

    lax.fori_loop(0, rows // step, conv, 0)


def convolve_one(one, weight, bias):
    rows, cols, ch = one.shape[0] - 2, one.shape[1], one.shape[2]
    return pl.pallas_call(
        one_kernel,
        out_shape=(
            jax.ShapeDtypeStruct((rows + 2, cols, 3 * ch), BF),
            jax.ShapeDtypeStruct((rows, cols, ch), F32),
        ),
        in_specs=vmem(3),
        out_specs=tuple(vmem(2)),
        scratch_shapes=[pltpu.VMEM((rows + 2, cols + 16, ch), F32)],
        compiler_params=params(),
        cost_estimate=pl.CostEstimate(flops=1_500_000_000, bytes_accessed=1_000_000, transcendentals=0),
        name="one",
    )(one, weight, bias)


def half_grad(which, d2t, d1t, xc2, xc1, out):
    ch, rows, cols = d2t.shape[0], xc1.shape[0] - 2, xc1.shape[1]
    for i, lanes, base in (
        (2 * which, pl.ds(0, 3 * ch), 0),
        (1, pl.ds(pl.multiple_of(which * (3 * ch // 2), 128), 3 * ch // 2), 6),
    ):
        width = lanes.size
        x2 = xc2[pl.ds(i, WROWS), :, lanes].reshape(WROWS * PITCH, width)
        x1 = xc1[pl.ds(i, rows), :, lanes].reshape(rows * cols, width)
        acc = jnp.dot(d2t[...], x2, preferred_element_type=F32)
        acc = acc + jnp.dot(d1t[...], x1, preferred_element_type=F32)
        for k in range(width // 128):
            out[(base + k) * ch : (base + k + 1) * ch] = acc[:, k * 128 : (k + 1) * 128].astype(out.dtype)


def main_kernel(
    row_count, col_count,
    offs, center, xc1_in, acc1, got_second, got_first, weight, bias, bt, b,
    send, tail, f1, f2, xc2, xc1, d2t, d1t,
    ext2, pre2, pre1, gwin, d1,
):
    rows, cols, ch = acc1.shape
    height, width = row_count * rows, col_count * cols
    inv_root = ch ** (-0.5)
    row, column = lax.axis_index("row"), place(SPACE)
    block = row * rows // BLK * col_count + column
    oy, ox = offs[block, 0], offs[block, 1]
    c0, gy0, gx0 = ox + 16 - RAD - 1, row * rows + oy - RAD, column * cols + ox - RAD
    right = even(column)
    ext2[:, 16 : 16 + cols] = center[...].astype(F32)
    v_first, v_second = got_first[...].astype(F32), got_second[...].astype(F32)
    for value, side in ((v_first, right), (v_second, jnp.logical_not(right))):
        ext2[:, pl.ds(pl.multiple_of(jnp.where(side, 16 + cols, 0), 16), 16)] = value
    ext2[:, 32 + cols :] = jnp.zeros((WROWS + 2, ext2.shape[1] - 32 - cols, ch), F32)
    xc1[...] = xc1_in[...]
    pre1[...] = acc1[...]
    col = lax.broadcasted_iota(jnp.int32, (rows + 2, 8, ch), 1)
    n1 = rows + 2
    for j, spot, at, value in (
        (0, 0, 0, jnp.where(right, v_second[0:n1, 0:8], v_first[0:n1, 0:8])),
        (2, 7, cols - 8, jnp.where(right, v_first[0:n1, 8:16], v_second[0:n1, 8:16])),
    ):
        value = jnp.where(col == spot, value, 0.0)
        lanes = slice(j * ch, (j + 1) * ch)
        xc1[:, at : at + 8, lanes] = (xc1_in[:, at : at + 8, lanes].astype(F32) + value).astype(BF)
        value = value.astype(BF)
        acc = jnp.zeros((rows * 8, ch), F32)
        for i in range(3):
            x = value[i : i + rows].reshape(rows * 8, ch)
            acc = acc + jnp.dot(x, weight[i, j * ch : (j + 1) * ch], preferred_element_type=F32)
        pre1[:, at : at + 8] = acc1[:, at : at + 8] + acc.reshape(rows, 8, ch)
    f1[...] = jnp.maximum(pre1[...], 0.0).reshape(rows * cols, ch).astype(BF)

    span = PITCH + 16
    base = pl.multiple_of((c0 // 8) * 8, 8)
    turn = span - c0 % 8

    def gather(r, carry):
        row = pltpu.roll(ext2[r, pl.ds(base, span), :], turn, 0)
        for j in range(3):
            xc2[r, :, j * ch : (j + 1) * ch] = row[j : j + PITCH].astype(BF)
        return carry

    lax.fori_loop(0, WROWS + 2, gather, 0, unroll=2)

    shift = bias[...]
    step = 8

    def conv_two(n, carry):
        acc = jnp.zeros((step * PITCH, ch), F32)
        for i in range(3):
            x = xc2[pl.ds(n * step + i, step)].reshape(step * PITCH, 3 * ch)
            acc = acc + jnp.dot(x, weight[i], preferred_element_type=F32)
        acc = (acc + shift).reshape(step, PITCH, ch)
        y = lax.broadcasted_iota(jnp.int32, acc.shape, 0) + n * step + gy0
        x = lax.broadcasted_iota(jnp.int32, acc.shape, 1) + gx0
        ok = (y >= 0) & (y < height) & (x >= 0) & (x < width)
        acc = jnp.maximum(jnp.where(ok, acc, 0.0), 0.0).reshape(step * PITCH, ch)
        pre2[pl.ds(n * step * PITCH, step * PITCH)] = acc
        f2[pl.ds(n * step * PITCH, step * PITCH)] = acc.astype(BF)
        return carry

    lax.fori_loop(0, WROWS // step, conv_two, 0)

    gwin[...] = jnp.zeros(gwin.shape, F32)
    lanes = GROUP * cols
    bsum = jnp.zeros((1, ch), F32)
    for g in range(rows // GROUP):
        at = slice(g * GROUP * PITCH, (g * GROUP + GROWS) * PITCH)
        px = slice(g * lanes, (g + 1) * lanes)
        gwin[at] += jnp.dot(bt[g], f1[px], preferred_element_type=F32)
        delta = jnp.dot(b[g], f2[at], preferred_element_type=F32) * inv_root
        mine = pre1[g * GROUP : (g + 1) * GROUP].reshape(lanes, ch)
        delta = jnp.where(mine > 0, delta, 0.0).astype(BF)
        d1[px] = delta
        bsum = bsum + jnp.sum(delta.astype(F32), axis=0, keepdims=True)
    delta = jnp.where(pre2[...] > 0, gwin[...] * inv_root, 0.0)
    bsum = bsum + jnp.sum(delta, axis=0, keepdims=True)
    d2t[...] = delta.astype(BF).T
    d1t[...] = d1[...].T
    half_grad(1 - lax.axis_index("core"), d2t, d1t, xc2, xc1, send)
    tail[...] = bias_tile(bsum[:, 0:128], bsum[:, 128:])
    send[9 * ch : 9 * ch + 8] = tail[...].astype(BF)
    send[9 * ch + 8 :] = jnp.zeros((send.shape[0] - 9 * ch - 8, 128), BF)


def bias_tile(low, high):
    row = lax.broadcasted_iota(jnp.int32, (8, 128), 0)
    out = jnp.zeros((8, 128), F32)
    for n, value in enumerate((low, high)):
        top = value.astype(BF).astype(F32)
        out = jnp.where(row == n, top, jnp.where(row == n + 2, value - top, out))
    return out


def bias_again(value):
    return bias_tile(value[0:1] + value[2:3], value[1:2] + value[3:4])


def main(offs, center, xc1, acc1, got, weight, bias, bt, b, row_count, col_count, flat):
    rows, cols, ch = acc1.shape
    wpx, n2 = WROWS * PITCH, WROWS + 2
    return pl.pallas_call(
        functools.partial(main_kernel, row_count, col_count),
        out_shape=(
            jax.ShapeDtypeStruct((flat, 128), BF),
            jax.ShapeDtypeStruct((8, 128), F32),
            jax.ShapeDtypeStruct((rows * cols, ch), BF),
            jax.ShapeDtypeStruct((wpx, ch), BF),
            jax.ShapeDtypeStruct((n2, PITCH, 3 * ch), BF),
            jax.ShapeDtypeStruct(xc1.shape, BF),
            jax.ShapeDtypeStruct((ch, wpx), BF),
            jax.ShapeDtypeStruct((ch, rows * cols), BF),
        ),
        in_specs=smem(1) + vmem(9),
        out_specs=tuple(vmem(8)),
        scratch_shapes=[
            pltpu.VMEM((n2, cols + 48, ch), F32),
            pltpu.VMEM((wpx, ch), F32),
            pltpu.VMEM((rows, cols, ch), F32),
            pltpu.VMEM((wpx, ch), F32),
            pltpu.VMEM((rows * cols, ch), BF),
        ],
        compiler_params=params(20),
        cost_estimate=pl.CostEstimate(flops=5_000_000_000, bytes_accessed=8_000_000, transcendentals=0),
        name="main",
    )(offs, center, xc1, acc1, got[1], got[0], weight, bias, bt, b)


def keep_kernel(tail, xc2, xc1, d2t, d1t, keep):
    ch = d2t.shape[0]
    half_grad(lax.axis_index("core"), d2t, d1t, xc2, xc1, keep)
    keep[9 * ch : 9 * ch + 8] = tail[...]
    keep[9 * ch + 8 :] = jnp.zeros((keep.shape[0] - 9 * ch - 8, 128), F32)


def keep_half(tail, xc2, xc1, d2t, d1t, flat):
    return pl.pallas_call(
        keep_kernel,
        out_shape=jax.ShapeDtypeStruct((flat, 128), F32),
        in_specs=vmem(5),
        out_specs=vmem(1)[0],
        compiler_params=params(),
        cost_estimate=pl.CostEstimate(flops=1_000_000_000, bytes_accessed=1_000_000, transcendentals=0),
        name="keep",
    )(tail, xc2, xc1, d2t, d1t)


def corr_kernel(f1, f2, before, out, token, lines):
    lanes = GROUP * BLK
    inv_root = f1.shape[1] ** (-0.5)
    lane = lax.broadcasted_iota(jnp.int32, (PITCH, lanes), 1)
    gap = lax.broadcasted_iota(jnp.int32, (PITCH, lanes), 0) - lane % BLK
    own = lane // BLK
    token[...] = jnp.zeros(token.shape, F32)
    lines[WIN * WIN - 1 :] = jnp.zeros((128 - WIN * WIN + 1, lanes), F32)
    for g in range(f1.shape[0] // lanes):
        at = slice(g * GROUP * PITCH, (g * GROUP + GROWS) * PITCH)
        scores = lax.dot_general(
            f2[at], f1[g * lanes : (g + 1) * lanes], (((1,), (1,)), ((), ())),
            preferred_element_type=F32,
        )
        for a in range(WIN):
            pick = scores[a * PITCH : (a + 1) * PITCH]
            for yy in range(1, GROUP):
                pick = jnp.where(own == yy, scores[(a + yy) * PITCH : (a + yy + 1) * PITCH], pick)
            for d in range(WIN):
                line = jnp.sum(jnp.where(gap == d, pick, 0.0), axis=0, keepdims=True) * inv_root
                lines[a * WIN + d : a * WIN + d + 1] = line
        out[g * lanes : (g + 1) * lanes] = lines[...].T[:, : WIN * WIN].astype(BF)


def correlate(f1, f2, before):
    return pl.pallas_call(
        corr_kernel,
        out_shape=(jax.ShapeDtypeStruct((f1.shape[0], WIN * WIN), BF), jax.ShapeDtypeStruct((8, 128), F32)),
        in_specs=vmem(3),
        out_specs=tuple(vmem(2)),
        scratch_shapes=[pltpu.VMEM((128, GROUP * BLK), F32)],
        compiler_params=params(),
        cost_estimate=pl.CostEstimate(flops=300_000_000, bytes_accessed=1_000_000, transcendentals=0),
        name="corr",
    )(f1, f2, before)


def sum_kernel(rows, parts, after, out):
    size = parts.shape[1]
    for s in range(0, size, 8):
        value = parts[0, s : s + 8].astype(F32)
        for n in range(1, parts.shape[0]):
            value = value + parts[n, s : s + 8].astype(F32)
        if s == rows % size:
            value = jnp.where(place(GROUP_AXES) == rows // size, bias_again(value), value)
        value = value.astype(BF)
        for k in range(out.shape[0]):
            out[k, s : s + 8] = value


def sum_and_copy(parts, copies, rows, after):
    return pl.pallas_call(
        functools.partial(sum_kernel, rows),
        out_shape=jax.ShapeDtypeStruct((copies,) + parts.shape[1:], BF),
        in_specs=vmem(2),
        out_specs=vmem(1)[0],
        compiler_params=params(),
        name="sum",
    )(parts, after)


def merge_kernel(rows, kept, got, out, token):
    out[...] = (kept[...] + got[...].astype(F32)).astype(BF)
    tail = kept[rows : rows + 8] + got[rows : rows + 8].astype(F32)
    out[rows : rows + 8] = bias_again(tail).astype(BF)
    token[...] = jnp.zeros(token.shape, F32)


def merge(kept, got, rows):
    return pl.pallas_call(
        functools.partial(merge_kernel, rows),
        out_shape=(jax.ShapeDtypeStruct(got.shape, BF), jax.ShapeDtypeStruct((8, 128), F32)),
        in_specs=vmem(2),
        out_specs=tuple(vmem(2)),
        compiler_params=params(),
        name="merge",
    )(kept, got)


def unpack_half(which, part, held, grad, sems):
    ch = held.shape[1]
    first, rest = which * 6 * ch, 3 * ch + which * (3 * ch // 2) - 6 * 128
    copies = []
    for k in range(9):
        held[k * 128 : (k + 1) * 128] = part[k * ch : (k + 1) * ch].T.astype(F32)
        row = pl.multiple_of((first if k < 6 else rest) + k * 128, 128)
        copies.append(
            pltpu.make_async_copy(held.at[k * 128 : (k + 1) * 128], grad.at[pl.ds(row, 128)], sems.at[k])
        )
        copies[-1].start()
    return copies


def own_kernel(own, grad, held, sems):
    for copy in unpack_half(lax.axis_index("core"), own, held, grad, sems):
        copy.wait()


def other_kernel(own, other, grad_in, grad, bias, held, line, sems):
    core = lax.axis_index("core")
    ch = held.shape[1]
    rows = slice(9 * ch, 9 * ch + 8)
    first = jnp.where(core == 0, own[rows].astype(F32), other[rows].astype(F32))
    line[:, 0:128] = first[0:1] + first[2:3]
    line[:, 128:] = first[1:2] + first[3:4]
    copy = pltpu.make_async_copy(line, bias, sems.at[9])
    copy.start()
    for other_copy in unpack_half(1 - core, other, held, grad, sems):
        other_copy.wait()
    copy.wait()


def unpack(own, other, ch):
    grad = jax.ShapeDtypeStruct((9 * ch, ch), F32)
    held = pltpu.VMEM((9 * ch // 2, ch), F32)
    outside = [pl.BlockSpec(memory_space=pl.ANY)]
    part = pl.pallas_call(
        own_kernel,
        out_shape=grad,
        in_specs=vmem(1),
        out_specs=outside[0],
        scratch_shapes=[held, pltpu.SemaphoreType.DMA((9,))],
        compiler_params=params(),
        cost_estimate=pl.CostEstimate(flops=10_000_000, bytes_accessed=3_000_000, transcendentals=0),
        name="unpack_own",
    )(own)
    return pl.pallas_call(
        other_kernel,
        out_shape=(grad, jax.ShapeDtypeStruct((1, ch), F32)),
        in_specs=vmem(2) + outside,
        out_specs=tuple(outside * 2),
        scratch_shapes=[held, pltpu.VMEM((1, ch), F32), pltpu.SemaphoreType.DMA((10,))],
        input_output_aliases={2: 0},
        compiler_params=params(),
        name="unpack_other",
    )(own, other, part)


def shards(row_count, col_count, space, group, frames, offsets, weight, bias, cotangent):
    rows, cols, ch = frames.shape[2:]
    offs = offsets.reshape(-1, 2)
    *sent, kept = row_pieces(frames[0])
    got = swap(sent, "row", row_count)
    bt, b = band(cotangent[0])
    second, first, center, one = col_pieces(offs, kept, got)
    got = swap((first, second), space, col_count)
    taps, bias = weight.reshape(3, 3 * ch, ch), bias.reshape(1, ch)
    xc1, acc1 = convolve_one(one, taps, bias)
    count = int(np.prod([lax.axis_size(a) for a in group]))
    depth = lax.axis_size("zh")
    half = 9 * ch
    size = (half + 8 + 8 * count - 1) // (8 * count) * 8
    sent, tail, f1, f2, *rest = main(
        offs, center, xc1, acc1, got, taps, bias, bt, b, row_count, col_count, size * count
    )
    cores = [(0, 1), (1, 0)]
    got = lax.ppermute(sent, "core", cores)
    kept = keep_half(tail, *rest, size * count)
    parts, token = merge(kept, got, half)
    corr, token = correlate(f1, f2, token)
    parts = lax.all_to_all(parts.reshape(count, size, 128), group, 0, 0, tiled=True)
    parts = lax.all_to_all(sum_and_copy(parts, depth, half, token), "zh", 0, 0, tiled=True)
    parts = lax.all_to_all(sum_and_copy(parts, count, half, token), group, 0, 0, tiled=True)
    parts = parts.reshape(count * size, 128)
    grad_w, grad_b = unpack(parts, lax.ppermute(parts, "core", cores), ch)
    corr = jnp.transpose(corr.reshape(1, rows, cols, WIN * WIN), (0, 3, 1, 2))
    return corr, grad_w.reshape(3, 3, ch, ch), grad_b.reshape(ch)


def solution(mesh):
    row_count, col_count, pair_count = (mesh.shape[a] for a in ("row", "col", "pair"))
    high = 2 if col_count == 16 else 1
    near = 2 if col_count // high >= 4 else 1
    fine = Mesh(
        mesh.devices.reshape(row_count, high, col_count // high // near, near, pair_count // 2, 2),
        ("row", "high", "zh", "zl", "low", "core"),
    )
    col, pair = SPACE, ("low", "core")
    return jax.shard_map(
        functools.partial(shards, row_count, col_count, col, GROUP_AXES),
        mesh=fine,
        in_specs=(
            P(pair, None, "row", col, None),
            P(pair, None, None, None),
            P(),
            P(),
            P(pair, None, "row", col),
        ),
        out_specs=(P(pair, None, "row", col), P(), P()),
        check_vma=False,
    )
```

```python
import functools

import jax
import jax.numpy as jnp
import numpy as np
from jax import lax
from jax.experimental import pallas as pl
from jax.experimental.pallas import tpu as pltpu
from jax.sharding import Mesh
from jax.sharding import PartitionSpec as P

BLK = 32
RAD = 4
MAXOFF = 8
WIN = 2 * RAD + 1
HALO = MAXOFF + RAD + 1
PITCH = 40
WROWS = 24
GROUP = 4
GROWS = GROUP + WIN - 1
BF = jnp.bfloat16
F32 = jnp.float32


def vmem(n):
    return [pl.BlockSpec(memory_space=pltpu.VMEM)] * n


def params(mib=16):
    return pltpu.CompilerParams(vmem_limit_bytes=mib * 1024 * 1024)


def smem(n):
    return [pl.BlockSpec(memory_space=pltpu.SMEM)] * n


def even(index):
    return lax.rem(index, 2) == 0


def place(axes):
    index = 0
    for axis in axes:
        index = index * lax.axis_size(axis) + lax.axis_index(axis)
    return index


SPACE = ("high", "zh", "zl")
GROUP_AXES = ("row", "high", "zl", "low")


def rows_kernel(frames, first, second, kept):
    rows = frames.shape[1]
    below = even(lax.axis_index("row"))
    for ref, low in ((first, below), (second, jnp.logical_not(below))):
        ref[0:HALO] = frames[1, pl.ds(jnp.where(low, rows - HALO, 0), HALO)]
        ref[HALO] = frames[0, jnp.where(low, rows - 1, 0)]
    kept[...] = frames[...]


def row_pieces(frames):
    cols, ch = frames.shape[2:]
    piece = jax.ShapeDtypeStruct((HALO + 1, cols, ch), BF)
    return pl.pallas_call(
        rows_kernel,
        out_shape=(piece, piece, jax.ShapeDtypeStruct(frames.shape, BF)),
        in_specs=vmem(1),
        out_specs=tuple(vmem(3)),
        compiler_params=params(),
        name="row_pieces",
    )(frames)


def cols_kernel(offs_in, frames, got_first, got_second, second, first, center, one, ext, offs, sem):
    rows, cols, ch = frames.shape[1:]
    fetch = pltpu.make_async_copy(offs_in, offs, sem)
    fetch.start()
    row, column = lax.axis_index("row"), place(SPACE)
    below = even(row)
    count = int(np.prod([lax.axis_size(a) for a in SPACE]))
    base = row * rows // BLK * count
    ext[HALO : HALO + rows] = frames[1]
    one[1 : rows + 1] = frames[0]
    for ref, low in ((got_first, below), (got_second, jnp.logical_not(below))):
        ext[pl.ds(jnp.where(low, HALO + rows, 0), HALO)] = ref[0:HALO]
        one[jnp.where(low, rows + 1, 0)] = ref[HALO]
    fetch.wait()
    center[...] = ext[pl.ds(offs[base + column, 0] + MAXOFF, WROWS + 2)]
    right = even(column)
    col = lax.broadcasted_iota(jnp.int32, (rows + 2, 16, ch), 1)
    for ref, side in ((first, right), (second, jnp.logical_not(right))):
        other = jnp.clip(jnp.where(side, column + 1, column - 1), 0, count - 1)
        start = offs[base + other, 0] + MAXOFF
        at = pl.multiple_of(jnp.where(side, cols - 16, 0), 16)
        ref[...] = ext[pl.ds(start, WROWS + 2), pl.ds(at, 16)]
        border = one[:, pl.ds(at, 16)].astype(F32)
        border = jnp.where(side, border[:, 15:16], border[:, 0:1])
        spare = jnp.where(side, 0, 15)
        ref[0 : rows + 2] = jnp.where(col == spare, border, ref[0 : rows + 2].astype(F32)).astype(BF)


def col_pieces(offs, frames, got):
    rows, cols, ch = frames.shape[1:]
    piece = jax.ShapeDtypeStruct((WROWS + 2, 16, ch), BF)
    return pl.pallas_call(
        cols_kernel,
        out_shape=(
            piece,
            piece,
            jax.ShapeDtypeStruct((WROWS + 2, cols, ch), BF),
            jax.ShapeDtypeStruct((rows + 2, cols, ch), BF),
        ),
        in_specs=[pl.BlockSpec(memory_space=pl.ANY)] + vmem(3),
        out_specs=tuple(vmem(4)),
        scratch_shapes=[
            pltpu.VMEM((rows + 2 * HALO, cols, ch), BF),
            pltpu.SMEM(offs.shape, jnp.int32),
            pltpu.SemaphoreType.DMA(()),
        ],
        compiler_params=params(),
        name="col_pieces",
    )(offs, frames, *got)


def swap(pieces, axes, count):
    got = []
    for piece, start in ((pieces[1], 1), (pieces[0], 0)):
        pairs = []
        for i in range(start, count - 1, 2):
            pairs += [(i, i + 1), (i + 1, i)]
        got.append(lax.ppermute(piece, axes, pairs))
    return got[::-1]


def band_kernel(cot, bt, b, lines):
    count, rows, cols = cot.shape
    lanes = GROUP * BLK

    def iota(shape, axis):
        return lax.broadcasted_iota(jnp.int32, shape, axis)

    copy = (iota((cols, lanes), 1) % cols == iota((cols, lanes), 0)).astype(F32).astype(BF)
    wide = jnp.dot(cot[...].reshape(count * rows, cols), copy, preferred_element_type=F32)
    shape = (WIN * 16, count * rows)
    q, d = iota(shape, 0), iota(shape, 1) // rows
    pickd = ((q // 16 * WIN + q % 16 == d) & (q % 16 < WIN)).astype(F32).astype(BF)
    line = iota((count * rows, lanes), 0) % rows
    want = iota((count * rows, lanes), 1) // cols
    gap = iota((PITCH, lanes), 0) - iota((PITCH, lanes), 1) % BLK
    own = iota((16, lanes), 1) // BLK
    for g in range(bt.shape[0]):
        mine = jnp.where(line == want + g * GROUP, wide, 0.0).astype(BF)
        lines[...] = jnp.dot(pickd, mine, preferred_element_type=F32)
        for r in range(GROWS):
            pick = jnp.zeros((16, lanes), F32)
            for yy in range(GROUP):
                a = r - yy
                if 0 <= a < WIN:
                    pick = jnp.where(own == yy, lines[a * 16 : (a + 1) * 16], pick)
            block = jnp.zeros((PITCH, lanes), F32)
            for k in range(WIN):
                block = jnp.where(gap == k, pick[k : k + 1], block)
            bt[g, r * PITCH : (r + 1) * PITCH] = block.astype(BF)
        b[g] = bt[g].astype(F32).T.astype(BF)


def band(cot):
    groups = cot.shape[1] // GROUP
    return pl.pallas_call(
        band_kernel,
        out_shape=(
            jax.ShapeDtypeStruct((groups, GROWS * PITCH, GROUP * BLK), BF),
            jax.ShapeDtypeStruct((groups, GROUP * BLK, GROWS * PITCH), BF),
        ),
        in_specs=vmem(1),
        out_specs=tuple(vmem(2)),
        scratch_shapes=[pltpu.VMEM((WIN * 16, GROUP * BLK), F32)],
        compiler_params=params(),
        cost_estimate=pl.CostEstimate(flops=2_000_000_000, bytes_accessed=1_000_000, transcendentals=0),
        name="band",
    )(cot)


def one_kernel(one, weight, bias, xc1, acc1, ext):
    rows, cols, ch = one.shape[0] - 2, one.shape[1], one.shape[2]
    ext[:, 0:8] = jnp.zeros((rows + 2, 8, ch), F32)
    ext[:, 8 + cols :] = jnp.zeros((rows + 2, 8, ch), F32)
    ext[:, 8 : 8 + cols] = one[...].astype(F32)
    for j in range(3):
        xc1[:, :, j * ch : (j + 1) * ch] = ext[:, 7 + j : 7 + j + cols].astype(BF)
    step = 8

    def conv(n, carry):
        acc = jnp.zeros((step * cols, ch), F32) + bias[...]
        for i in range(3):
            x = xc1[pl.ds(n * step + i, step)].reshape(step * cols, 3 * ch)
            acc = acc + jnp.dot(x, weight[i], preferred_element_type=F32)
        acc1[pl.ds(n * step, step)] = acc.reshape(step, cols, ch)
        return carry

    lax.fori_loop(0, rows // step, conv, 0)


def convolve_one(one, weight, bias):
    rows, cols, ch = one.shape[0] - 2, one.shape[1], one.shape[2]
    return pl.pallas_call(
        one_kernel,
        out_shape=(
            jax.ShapeDtypeStruct((rows + 2, cols, 3 * ch), BF),
            jax.ShapeDtypeStruct((rows, cols, ch), F32),
        ),
        in_specs=vmem(3),
        out_specs=tuple(vmem(2)),
        scratch_shapes=[pltpu.VMEM((rows + 2, cols + 16, ch), F32)],
        compiler_params=params(),
        cost_estimate=pl.CostEstimate(flops=1_500_000_000, bytes_accessed=1_000_000, transcendentals=0),
        name="one",
    )(one, weight, bias)


def half_grad(which, d2t, d1t, xc2, xc1, out):
    ch, rows, cols = d2t.shape[0], xc1.shape[0] - 2, xc1.shape[1]
    for i, lanes, base in (
        (2 * which, pl.ds(0, 3 * ch), 0),
        (1, pl.ds(pl.multiple_of(which * (3 * ch // 2), 128), 3 * ch // 2), 6),
    ):
        width = lanes.size
        x2 = xc2[pl.ds(i, WROWS), :, lanes].reshape(WROWS * PITCH, width)
        x1 = xc1[pl.ds(i, rows), :, lanes].reshape(rows * cols, width)
        acc = jnp.dot(d2t[...], x2, preferred_element_type=F32)
        acc = acc + jnp.dot(d1t[...], x1, preferred_element_type=F32)
        for k in range(width // 128):
            out[(base + k) * ch : (base + k + 1) * ch] = acc[:, k * 128 : (k + 1) * 128].astype(out.dtype)


def main_kernel(
    row_count, col_count,
    offs_in, center, xc1_in, acc1, got_second, got_first, weight, bias, bt, b,
    send, tail, f1, f2, xc2, xc1, d2t, d1t,
    ext2, pre2, pre1, gwin, d1, offs, sem,
):
    rows, cols, ch = acc1.shape
    fetch = pltpu.make_async_copy(offs_in, offs, sem)
    fetch.start()
    height, width = row_count * rows, col_count * cols
    inv_root = ch ** (-0.5)
    row, column = lax.axis_index("row"), place(SPACE)
    right = even(column)
    ext2[:, 16 : 16 + cols] = center[...].astype(F32)
    v_first, v_second = got_first[...].astype(F32), got_second[...].astype(F32)
    for value, side in ((v_first, right), (v_second, jnp.logical_not(right))):
        ext2[:, pl.ds(pl.multiple_of(jnp.where(side, 16 + cols, 0), 16), 16)] = value
    ext2[:, 32 + cols :] = jnp.zeros((WROWS + 2, ext2.shape[1] - 32 - cols, ch), F32)
    xc1[...] = xc1_in[...]
    pre1[...] = acc1[...]
    col = lax.broadcasted_iota(jnp.int32, (rows + 2, 8, ch), 1)
    n1 = rows + 2
    for j, spot, at, value in (
        (0, 0, 0, jnp.where(right, v_second[0:n1, 0:8], v_first[0:n1, 0:8])),
        (2, 7, cols - 8, jnp.where(right, v_first[0:n1, 8:16], v_second[0:n1, 8:16])),
    ):
        value = jnp.where(col == spot, value, 0.0)
        lanes = slice(j * ch, (j + 1) * ch)
        xc1[:, at : at + 8, lanes] = (xc1_in[:, at : at + 8, lanes].astype(F32) + value).astype(BF)
        value = value.astype(BF)
        acc = jnp.zeros((rows * 8, ch), F32)
        for i in range(3):
            x = value[i : i + rows].reshape(rows * 8, ch)
            acc = acc + jnp.dot(x, weight[i, j * ch : (j + 1) * ch], preferred_element_type=F32)
        pre1[:, at : at + 8] = acc1[:, at : at + 8] + acc.reshape(rows, 8, ch)
    f1[...] = jnp.maximum(pre1[...], 0.0).reshape(rows * cols, ch).astype(BF)

    fetch.wait()
    block = row * rows // BLK * col_count + column
    oy, ox = offs[block, 0], offs[block, 1]
    c0, gy0, gx0 = ox + 16 - RAD - 1, row * rows + oy - RAD, column * cols + ox - RAD
    span = PITCH + 16
    base = pl.multiple_of((c0 // 8) * 8, 8)
    turn = span - c0 % 8

    def gather(r, carry):
        row = pltpu.roll(ext2[r, pl.ds(base, span), :], turn, 0)
        for j in range(3):
            xc2[r, :, j * ch : (j + 1) * ch] = row[j : j + PITCH].astype(BF)
        return carry

    lax.fori_loop(0, WROWS + 2, gather, 0, unroll=2)

    shift = bias[...]
    step = 8

    def conv_two(n, carry):
        acc = jnp.zeros((step * PITCH, ch), F32)
        for i in range(3):
            x = xc2[pl.ds(n * step + i, step)].reshape(step * PITCH, 3 * ch)
            acc = acc + jnp.dot(x, weight[i], preferred_element_type=F32)
        acc = (acc + shift).reshape(step, PITCH, ch)
        y = lax.broadcasted_iota(jnp.int32, acc.shape, 0) + n * step + gy0
        x = lax.broadcasted_iota(jnp.int32, acc.shape, 1) + gx0
        ok = (y >= 0) & (y < height) & (x >= 0) & (x < width)
        acc = jnp.maximum(jnp.where(ok, acc, 0.0), 0.0).reshape(step * PITCH, ch)
        pre2[pl.ds(n * step * PITCH, step * PITCH)] = acc
        f2[pl.ds(n * step * PITCH, step * PITCH)] = acc.astype(BF)
        return carry

    lax.fori_loop(0, WROWS // step, conv_two, 0)

    gwin[...] = jnp.zeros(gwin.shape, F32)
    lanes = GROUP * cols
    bsum = jnp.zeros((1, ch), F32)
    for g in range(rows // GROUP):
        at = slice(g * GROUP * PITCH, (g * GROUP + GROWS) * PITCH)
        px = slice(g * lanes, (g + 1) * lanes)
        gwin[at] += jnp.dot(bt[g], f1[px], preferred_element_type=F32)
        delta = jnp.dot(b[g], f2[at], preferred_element_type=F32) * inv_root
        mine = pre1[g * GROUP : (g + 1) * GROUP].reshape(lanes, ch)
        delta = jnp.where(mine > 0, delta, 0.0).astype(BF)
        d1[px] = delta
        bsum = bsum + jnp.sum(delta.astype(F32), axis=0, keepdims=True)
    delta = jnp.where(pre2[...] > 0, gwin[...] * inv_root, 0.0)
    bsum = bsum + jnp.sum(delta, axis=0, keepdims=True)
    d2t[...] = delta.astype(BF).T
    d1t[...] = d1[...].T
    half_grad(1 - lax.axis_index("core"), d2t, d1t, xc2, xc1, send)
    tail[...] = bias_tile(bsum[:, 0:128], bsum[:, 128:])
    send[9 * ch : 9 * ch + 8] = tail[...].astype(BF)
    send[9 * ch + 8 :] = jnp.zeros((send.shape[0] - 9 * ch - 8, 128), BF)


def bias_tile(low, high):
    row = lax.broadcasted_iota(jnp.int32, (8, 128), 0)
    out = jnp.zeros((8, 128), F32)
    for n, value in enumerate((low, high)):
        top = value.astype(BF).astype(F32)
        out = jnp.where(row == n, top, jnp.where(row == n + 2, value - top, out))
    return out


def bias_again(value):
    return bias_tile(value[0:1] + value[2:3], value[1:2] + value[3:4])


def main(offs, center, xc1, acc1, got, weight, bias, bt, b, row_count, col_count, flat):
    rows, cols, ch = acc1.shape
    wpx, n2 = WROWS * PITCH, WROWS + 2
    return pl.pallas_call(
        functools.partial(main_kernel, row_count, col_count),
        out_shape=(
            jax.ShapeDtypeStruct((flat, 128), BF),
            jax.ShapeDtypeStruct((8, 128), F32),
            jax.ShapeDtypeStruct((rows * cols, ch), BF),
            jax.ShapeDtypeStruct((wpx, ch), BF),
            jax.ShapeDtypeStruct((n2, PITCH, 3 * ch), BF),
            jax.ShapeDtypeStruct(xc1.shape, BF),
            jax.ShapeDtypeStruct((ch, wpx), BF),
            jax.ShapeDtypeStruct((ch, rows * cols), BF),
        ),
        in_specs=[pl.BlockSpec(memory_space=pl.ANY)] + vmem(9),
        out_specs=tuple(vmem(8)),
        scratch_shapes=[
            pltpu.VMEM((n2, cols + 48, ch), F32),
            pltpu.VMEM((wpx, ch), F32),
            pltpu.VMEM((rows, cols, ch), F32),
            pltpu.VMEM((wpx, ch), F32),
            pltpu.VMEM((rows * cols, ch), BF),
            pltpu.SMEM(offs.shape, jnp.int32),
            pltpu.SemaphoreType.DMA(()),
        ],
        compiler_params=params(20),
        cost_estimate=pl.CostEstimate(flops=5_000_000_000, bytes_accessed=8_000_000, transcendentals=0),
        name="main",
    )(offs, center, xc1, acc1, got[1], got[0], weight, bias, bt, b)


def keep_kernel(tail, xc2, xc1, d2t, d1t, keep):
    ch = d2t.shape[0]
    half_grad(lax.axis_index("core"), d2t, d1t, xc2, xc1, keep)
    keep[9 * ch : 9 * ch + 8] = tail[...]
    keep[9 * ch + 8 :] = jnp.zeros((keep.shape[0] - 9 * ch - 8, 128), F32)


def keep_half(tail, xc2, xc1, d2t, d1t, flat):
    return pl.pallas_call(
        keep_kernel,
        out_shape=jax.ShapeDtypeStruct((flat, 128), F32),
        in_specs=vmem(5),
        out_specs=vmem(1)[0],
        compiler_params=params(),
        cost_estimate=pl.CostEstimate(flops=1_000_000_000, bytes_accessed=1_000_000, transcendentals=0),
        name="keep",
    )(tail, xc2, xc1, d2t, d1t)


def corr_kernel(f1, f2, before, out, token, lines):
    lanes = GROUP * BLK
    inv_root = f1.shape[1] ** (-0.5)
    lane = lax.broadcasted_iota(jnp.int32, (PITCH, lanes), 1)
    gap = lax.broadcasted_iota(jnp.int32, (PITCH, lanes), 0) - lane % BLK
    own = lane // BLK
    token[...] = jnp.zeros(token.shape, F32)
    lines[WIN * WIN - 1 :] = jnp.zeros((128 - WIN * WIN + 1, lanes), F32)
    for g in range(f1.shape[0] // lanes):
        at = slice(g * GROUP * PITCH, (g * GROUP + GROWS) * PITCH)
        scores = lax.dot_general(
            f2[at], f1[g * lanes : (g + 1) * lanes], (((1,), (1,)), ((), ())),
            preferred_element_type=F32,
        )
        for a in range(WIN):
            pick = scores[a * PITCH : (a + 1) * PITCH]
            for yy in range(1, GROUP):
                pick = jnp.where(own == yy, scores[(a + yy) * PITCH : (a + yy + 1) * PITCH], pick)
            for d in range(WIN):
                line = jnp.sum(jnp.where(gap == d, pick, 0.0), axis=0, keepdims=True) * inv_root
                lines[a * WIN + d : a * WIN + d + 1] = line
        out[g * lanes : (g + 1) * lanes] = lines[...].T[:, : WIN * WIN].astype(BF)


def correlate(f1, f2, before):
    return pl.pallas_call(
        corr_kernel,
        out_shape=(jax.ShapeDtypeStruct((f1.shape[0], WIN * WIN), BF), jax.ShapeDtypeStruct((8, 128), F32)),
        in_specs=vmem(3),
        out_specs=tuple(vmem(2)),
        scratch_shapes=[pltpu.VMEM((128, GROUP * BLK), F32)],
        compiler_params=params(),
        cost_estimate=pl.CostEstimate(flops=300_000_000, bytes_accessed=1_000_000, transcendentals=0),
        name="corr",
    )(f1, f2, before)


def sum_kernel(rows, parts, after, out, token):
    size = parts.shape[1]
    token[...] = jnp.zeros(token.shape, F32)
    for s in range(0, size, 8):
        value = parts[0, s : s + 8].astype(F32)
        for n in range(1, parts.shape[0]):
            value = value + parts[n, s : s + 8].astype(F32)
        if s == rows % size:
            value = jnp.where(place(GROUP_AXES) == rows // size, bias_again(value), value)
        value = value.astype(BF)
        for k in range(out.shape[0]):
            out[k, s : s + 8] = value


def sum_and_copy(parts, copies, rows, after):
    return pl.pallas_call(
        functools.partial(sum_kernel, rows),
        out_shape=(
            jax.ShapeDtypeStruct((copies,) + parts.shape[1:], BF),
            jax.ShapeDtypeStruct((8, 128), F32),
        ),
        in_specs=vmem(2),
        out_specs=tuple(vmem(2)),
        compiler_params=params(),
        name="sum",
    )(parts, after)


def merge_kernel(rows, kept, got, out):
    out[...] = (kept[...] + got[...].astype(F32)).astype(BF)
    tail = kept[rows : rows + 8] + got[rows : rows + 8].astype(F32)
    out[rows : rows + 8] = bias_again(tail).astype(BF)


def merge(kept, got, rows):
    return pl.pallas_call(
        functools.partial(merge_kernel, rows),
        out_shape=jax.ShapeDtypeStruct(got.shape, BF),
        in_specs=vmem(2),
        out_specs=vmem(1)[0],
        compiler_params=params(),
        name="merge",
    )(kept, got)


def unpack_half(which, part, held, grad, sems):
    ch = held.shape[1]
    first, rest = which * 6 * ch, 3 * ch + which * (3 * ch // 2) - 6 * 128
    copies = []
    for k in range(9):
        held[k * 128 : (k + 1) * 128] = part[k * ch : (k + 1) * ch].T.astype(F32)
        row = pl.multiple_of((first if k < 6 else rest) + k * 128, 128)
        copies.append(
            pltpu.make_async_copy(held.at[k * 128 : (k + 1) * 128], grad.at[pl.ds(row, 128)], sems.at[k])
        )
        copies[-1].start()
    return copies


def own_kernel(own, grad, held, sems):
    for copy in unpack_half(lax.axis_index("core"), own, held, grad, sems):
        copy.wait()


def other_kernel(own, other, grad_in, grad, bias, held, line, sems):
    core = lax.axis_index("core")
    ch = held.shape[1]
    rows = slice(9 * ch, 9 * ch + 8)
    first = jnp.where(core == 0, own[rows].astype(F32), other[rows].astype(F32))
    line[:, 0:128] = first[0:1] + first[2:3]
    line[:, 128:] = first[1:2] + first[3:4]
    copy = pltpu.make_async_copy(line, bias, sems.at[9])
    copy.start()
    for other_copy in unpack_half(1 - core, other, held, grad, sems):
        other_copy.wait()
    copy.wait()


def unpack(own, other, ch):
    grad = jax.ShapeDtypeStruct((9 * ch, ch), F32)
    held = pltpu.VMEM((9 * ch // 2, ch), F32)
    outside = [pl.BlockSpec(memory_space=pl.ANY)]
    part = pl.pallas_call(
        own_kernel,
        out_shape=grad,
        in_specs=vmem(1),
        out_specs=outside[0],
        scratch_shapes=[held, pltpu.SemaphoreType.DMA((9,))],
        compiler_params=params(),
        cost_estimate=pl.CostEstimate(flops=10_000_000, bytes_accessed=3_000_000, transcendentals=0),
        name="unpack_own",
    )(own)
    return pl.pallas_call(
        other_kernel,
        out_shape=(grad, jax.ShapeDtypeStruct((1, ch), F32)),
        in_specs=vmem(2) + outside,
        out_specs=tuple(outside * 2),
        scratch_shapes=[held, pltpu.VMEM((1, ch), F32), pltpu.SemaphoreType.DMA((10,))],
        input_output_aliases={2: 0},
        compiler_params=params(),
        name="unpack_other",
    )(own, other, part)


def shards(row_count, col_count, space, group, frames, offsets, weight, bias, cotangent):
    rows, cols, ch = frames.shape[2:]
    offs = offsets.reshape(-1, 2)
    *sent, kept = row_pieces(frames[0])
    got = swap(sent, "row", row_count)
    bt, b = band(cotangent[0])
    second, first, center, one = col_pieces(offs, kept, got)
    got = swap((first, second), space, col_count)
    taps, bias = weight.reshape(3, 3 * ch, ch), bias.reshape(1, ch)
    xc1, acc1 = convolve_one(one, taps, bias)
    count = int(np.prod([lax.axis_size(a) for a in group]))
    depth = lax.axis_size("zh")
    half = 9 * ch
    size = (half + 8 + 8 * count - 1) // (8 * count) * 8
    sent, tail, f1, f2, *rest = main(
        offs, center, xc1, acc1, got, taps, bias, bt, b, row_count, col_count, size * count
    )
    cores = [(0, 1), (1, 0)]
    got = lax.ppermute(sent, "core", cores)
    kept = keep_half(tail, *rest, size * count)
    parts = merge(kept, got, half)
    parts = lax.all_to_all(parts.reshape(count, size, 128), group, 0, 0, tiled=True)
    parts, token = sum_and_copy(parts, depth, half, tail)
    corr, token = correlate(f1, f2, token)
    parts = lax.all_to_all(parts, "zh", 0, 0, tiled=True)
    parts, _ = sum_and_copy(parts, count, half, token)
    parts = lax.all_to_all(parts, group, 0, 0, tiled=True)
    parts = parts.reshape(count * size, 128)
    grad_w, grad_b = unpack(parts, lax.ppermute(parts, "core", cores), ch)
    corr = jnp.transpose(corr.reshape(1, rows, cols, WIN * WIN), (0, 3, 1, 2))
    return corr, grad_w.reshape(3, 3, ch, ch), grad_b.reshape(ch)


def solution(mesh):
    row_count, col_count, pair_count = (mesh.shape[a] for a in ("row", "col", "pair"))
    high = 2 if col_count == 16 else 1
    near = 2 if col_count // high >= 4 else 1
    fine = Mesh(
        mesh.devices.reshape(row_count, high, col_count // high // near, near, pair_count // 2, 2),
        ("row", "high", "zh", "zl", "low", "core"),
    )
    col, pair = SPACE, ("low", "core")
    return jax.shard_map(
        functools.partial(shards, row_count, col_count, col, GROUP_AXES),
        mesh=fine,
        in_specs=(
            P(pair, None, "row", col, None),
            P(pair, None, None, None),
            P(),
            P(),
            P(pair, None, "row", col),
        ),
        out_specs=(P(pair, None, "row", col), P(), P()),
        check_vma=False,
    )
```

```python
import functools

import jax
import jax.numpy as jnp
import numpy as np
from jax import lax
from jax.experimental import pallas as pl
from jax.experimental.pallas import tpu as pltpu
from jax.sharding import Mesh
from jax.sharding import PartitionSpec as P

BLK = 32
RAD = 4
MAXOFF = 8
WIN = 2 * RAD + 1
HALO = MAXOFF + RAD + 1
PITCH = 40
WROWS = 24
GROUP = 4
GROWS = GROUP + WIN - 1
BF = jnp.bfloat16
F32 = jnp.float32


def vmem(n):
    return [pl.BlockSpec(memory_space=pltpu.VMEM)] * n


def params(mib=16):
    return pltpu.CompilerParams(vmem_limit_bytes=mib * 1024 * 1024)


def smem(n):
    return [pl.BlockSpec(memory_space=pltpu.SMEM)] * n


def even(index):
    return lax.rem(index, 2) == 0


def place(axes):
    index = 0
    for axis in axes:
        index = index * lax.axis_size(axis) + lax.axis_index(axis)
    return index


SPACE = ("high", "zh", "zl")
GROUP_AXES = ("row", "high", "zl", "low")


def with_border(piece, border, side):
    col = lax.broadcasted_iota(jnp.int32, piece.shape, 1)
    border = jnp.where(side, border[:, 15:16].astype(F32), border[:, 0:1].astype(F32))
    return jnp.where(col == jnp.where(side, 0, 15), border, piece.astype(F32)).astype(BF)


def rows_kernel(frames, first, second, far, near, kept):
    rows, cols = frames.shape[1], frames.shape[2]
    below, right = even(lax.axis_index("row")), even(place(SPACE))
    for ref, low in ((first, below), (second, jnp.logical_not(below))):
        ref[0:HALO] = frames[1, pl.ds(jnp.where(low, rows - HALO, 0), HALO)]
        ref[HALO] = frames[0, jnp.where(low, rows - 1, 0)]
    for ref, side in ((near, right), (far, jnp.logical_not(right))):
        at = pl.ds(pl.multiple_of(jnp.where(side, cols - 16, 0), 16), 16)
        ref[...] = with_border(frames[1, :, at], frames[0, :, at].astype(F32), side)
    kept[...] = frames[...]


def row_pieces(frames):
    rows, cols, ch = frames.shape[1:]
    piece = jax.ShapeDtypeStruct((HALO + 1, cols, ch), BF)
    side = jax.ShapeDtypeStruct((rows, 16, ch), BF)
    return pl.pallas_call(
        rows_kernel,
        out_shape=(piece, piece, side, side, jax.ShapeDtypeStruct(frames.shape, BF)),
        in_specs=vmem(1),
        out_specs=tuple(vmem(5)),
        compiler_params=params(),
        name="row_pieces",
    )(frames)


def corners_kernel(offs_in, frames, got_first, got_second, far, near, center, one, ext, offs, sem):
    rows, cols, ch = frames.shape[1:]
    fetch = pltpu.make_async_copy(offs_in, offs, sem)
    fetch.start()
    row, column = lax.axis_index("row"), place(SPACE)
    below = even(row)
    count = int(np.prod([lax.axis_size(a) for a in SPACE]))
    base = row * rows // BLK * count
    ext[HALO : HALO + rows] = frames[1]
    one[1 : rows + 1] = frames[0]
    for ref, low in ((got_first, below), (got_second, jnp.logical_not(below))):
        ext[pl.ds(jnp.where(low, HALO + rows, 0), HALO)] = ref[0:HALO]
        one[jnp.where(low, rows + 1, 0)] = ref[HALO]
    fetch.wait()
    center[...] = ext[pl.ds(offs[base + column, 0] + MAXOFF, WROWS + 2)]
    right = even(column)
    for ref, side in ((near, right), (far, jnp.logical_not(right))):
        other = jnp.clip(jnp.where(side, column + 1, column - 1), 0, count - 1)
        start = offs[base + other, 0] + MAXOFF
        above = jnp.maximum(HALO - start, 0)
        at = pl.ds(pl.multiple_of(jnp.where(side, cols - 16, 0), 16), 16)
        ref[...] = ext[pl.ds(HALO + rows - above, HALO), at]
        for k in range(HALO):

            @pl.when(k < above)
            def _():
                ref[k] = ext[start + k, at]

        border = jnp.concatenate([one[0:1, at], one[rows + 1 :, at]], axis=0)
        ref[0:2] = with_border(ref[0:2], border, side)


def corner_pieces(offs, frames, got):
    rows, cols, ch = frames.shape[1:]
    piece = jax.ShapeDtypeStruct((HALO, 16, ch), BF)
    return pl.pallas_call(
        corners_kernel,
        out_shape=(
            piece,
            piece,
            jax.ShapeDtypeStruct((WROWS + 2, cols, ch), BF),
            jax.ShapeDtypeStruct((rows + 2, cols, ch), BF),
        ),
        in_specs=[pl.BlockSpec(memory_space=pl.ANY)] + vmem(3),
        out_specs=tuple(vmem(4)),
        scratch_shapes=[
            pltpu.VMEM((rows + 2 * HALO, cols, ch), BF),
            pltpu.SMEM(offs.shape, jnp.int32),
            pltpu.SemaphoreType.DMA(()),
        ],
        compiler_params=params(),
        name="corner_pieces",
    )(offs, frames, *got)


def swap(pieces, axes, count):
    got = []
    for piece, start in ((pieces[1], 1), (pieces[0], 0)):
        pairs = []
        for i in range(start, count - 1, 2):
            pairs += [(i, i + 1), (i + 1, i)]
        got.append(lax.ppermute(piece, axes, pairs))
    return got[::-1]


def band_kernel(cot, bt, b, lines):
    count, rows, cols = cot.shape
    lanes = GROUP * BLK

    def iota(shape, axis):
        return lax.broadcasted_iota(jnp.int32, shape, axis)

    copy = (iota((cols, lanes), 1) % cols == iota((cols, lanes), 0)).astype(F32).astype(BF)
    wide = jnp.dot(cot[...].reshape(count * rows, cols), copy, preferred_element_type=F32)
    shape = (WIN * 16, count * rows)
    q, d = iota(shape, 0), iota(shape, 1) // rows
    pickd = ((q // 16 * WIN + q % 16 == d) & (q % 16 < WIN)).astype(F32).astype(BF)
    line = iota((count * rows, lanes), 0) % rows
    want = iota((count * rows, lanes), 1) // cols
    gap = iota((PITCH, lanes), 0) - iota((PITCH, lanes), 1) % BLK
    own = iota((16, lanes), 1) // BLK
    for g in range(bt.shape[0]):
        mine = jnp.where(line == want + g * GROUP, wide, 0.0).astype(BF)
        lines[...] = jnp.dot(pickd, mine, preferred_element_type=F32)
        for r in range(GROWS):
            pick = jnp.zeros((16, lanes), F32)
            for yy in range(GROUP):
                a = r - yy
                if 0 <= a < WIN:
                    pick = jnp.where(own == yy, lines[a * 16 : (a + 1) * 16], pick)
            block = jnp.zeros((PITCH, lanes), F32)
            for k in range(WIN):
                block = jnp.where(gap == k, pick[k : k + 1], block)
            bt[g, r * PITCH : (r + 1) * PITCH] = block.astype(BF)
        b[g] = bt[g].astype(F32).T.astype(BF)


def band(cot):
    groups = cot.shape[1] // GROUP
    return pl.pallas_call(
        band_kernel,
        out_shape=(
            jax.ShapeDtypeStruct((groups, GROWS * PITCH, GROUP * BLK), BF),
            jax.ShapeDtypeStruct((groups, GROUP * BLK, GROWS * PITCH), BF),
        ),
        in_specs=vmem(1),
        out_specs=tuple(vmem(2)),
        scratch_shapes=[pltpu.VMEM((WIN * 16, GROUP * BLK), F32)],
        compiler_params=params(),
        cost_estimate=pl.CostEstimate(flops=2_000_000_000, bytes_accessed=1_000_000, transcendentals=0),
        name="band",
    )(cot)


def one_kernel(one, weight, bias, xc1, acc1, ext):
    rows, cols, ch = one.shape[0] - 2, one.shape[1], one.shape[2]
    ext[:, 0:8] = jnp.zeros((rows + 2, 8, ch), F32)
    ext[:, 8 + cols :] = jnp.zeros((rows + 2, 8, ch), F32)
    ext[:, 8 : 8 + cols] = one[...].astype(F32)
    for j in range(3):
        xc1[:, :, j * ch : (j + 1) * ch] = ext[:, 7 + j : 7 + j + cols].astype(BF)
    step = 8

    def conv(n, carry):
        acc = jnp.zeros((step * cols, ch), F32) + bias[...]
        for i in range(3):
            x = xc1[pl.ds(n * step + i, step)].reshape(step * cols, 3 * ch)
            acc = acc + jnp.dot(x, weight[i], preferred_element_type=F32)
        acc1[pl.ds(n * step, step)] = acc.reshape(step, cols, ch)
        return carry

    lax.fori_loop(0, rows // step, conv, 0)


def convolve_one(one, weight, bias):
    rows, cols, ch = one.shape[0] - 2, one.shape[1], one.shape[2]
    return pl.pallas_call(
        one_kernel,
        out_shape=(
            jax.ShapeDtypeStruct((rows + 2, cols, 3 * ch), BF),
            jax.ShapeDtypeStruct((rows, cols, ch), F32),
        ),
        in_specs=vmem(3),
        out_specs=tuple(vmem(2)),
        scratch_shapes=[pltpu.VMEM((rows + 2, cols + 16, ch), F32)],
        compiler_params=params(),
        cost_estimate=pl.CostEstimate(flops=1_500_000_000, bytes_accessed=1_000_000, transcendentals=0),
        name="one",
    )(one, weight, bias)


def half_grad(which, d2t, d1t, xc2, xc1, out):
    ch, rows, cols = d2t.shape[0], xc1.shape[0] - 2, xc1.shape[1]
    for i, lanes, base in (
        (2 * which, pl.ds(0, 3 * ch), 0),
        (1, pl.ds(pl.multiple_of(which * (3 * ch // 2), 128), 3 * ch // 2), 6),
    ):
        width = lanes.size
        x2 = xc2[pl.ds(i, WROWS), :, lanes].reshape(WROWS * PITCH, width)
        x1 = xc1[pl.ds(i, rows), :, lanes].reshape(rows * cols, width)
        acc = jnp.dot(d2t[...], x2, preferred_element_type=F32)
        acc = acc + jnp.dot(d1t[...], x1, preferred_element_type=F32)
        for k in range(width // 128):
            out[(base + k) * ch : (base + k + 1) * ch] = acc[:, k * 128 : (k + 1) * 128].astype(out.dtype)


def main_kernel(
    row_count, col_count,
    offs_in, center, xc1_in, acc1, far, near, far_corner, near_corner, weight, bias, bt, b,
    send, tail, f1, f2, xc2, xc1, d2t, d1t,
    ext2, pre2, pre1, gwin, d1, sides, offs, sem,
):
    rows, cols, ch = acc1.shape
    fetch = pltpu.make_async_copy(offs_in, offs, sem)
    fetch.start()
    height, width = row_count * rows, col_count * cols
    inv_root = ch ** (-0.5)
    row, column = lax.axis_index("row"), place(SPACE)
    right = even(column)
    ext2[:, 16 : 16 + cols] = center[...].astype(F32)
    ext2[:, 32 + cols :] = jnp.zeros((WROWS + 2, ext2.shape[1] - 32 - cols, ch), F32)
    xc1[...] = xc1_in[...]
    pre1[...] = acc1[...]
    n1 = rows + 2
    col = lax.broadcasted_iota(jnp.int32, (n1, 8, ch), 1)

    def border(corner, side, at):
        parts = [corner[0:1, at : at + 8], side[:, at : at + 8], corner[1:2, at : at + 8]]
        return jnp.concatenate([part.astype(F32) for part in parts], axis=0)

    for j, spot, at, value in (
        (0, 0, 0, jnp.where(right, border(far_corner, far, 0), border(near_corner, near, 0))),
        (2, 7, cols - 8, jnp.where(right, border(near_corner, near, 8), border(far_corner, far, 8))),
    ):
        value = jnp.where(col == spot, value, 0.0)
        lanes = slice(j * ch, (j + 1) * ch)
        xc1[:, at : at + 8, lanes] = (xc1_in[:, at : at + 8, lanes].astype(F32) + value).astype(BF)
        value = value.astype(BF)
        acc = jnp.zeros((rows * 8, ch), F32)
        for i in range(3):
            x = value[i : i + rows].reshape(rows * 8, ch)
            acc = acc + jnp.dot(x, weight[i, j * ch : (j + 1) * ch], preferred_element_type=F32)
        pre1[:, at : at + 8] = acc1[:, at : at + 8] + acc.reshape(rows, 8, ch)
    f1[...] = jnp.maximum(pre1[...], 0.0).reshape(rows * cols, ch).astype(BF)

    fetch.wait()
    block = row * rows // BLK * col_count + column
    oy, ox = offs[block, 0], offs[block, 1]
    start = oy + MAXOFF
    above = jnp.maximum(HALO - start, 0)
    for side, corner, to_right in ((near, near_corner, right), (far, far_corner, jnp.logical_not(right))):
        sides[HALO : HALO + rows] = side[...]
        for k in range(HALO):
            sides[jnp.where(k < above, start + k, HALO + rows + k - above)] = corner[k]
        at = pl.ds(pl.multiple_of(jnp.where(to_right, 16 + cols, 0), 16), 16)
        ext2[:, at] = sides[pl.ds(start, WROWS + 2)].astype(F32)
    c0, gy0, gx0 = ox + 16 - RAD - 1, row * rows + oy - RAD, column * cols + ox - RAD
    span = PITCH + 16
    base = pl.multiple_of((c0 // 8) * 8, 8)
    turn = span - c0 % 8

    def gather(r, carry):
        row = pltpu.roll(ext2[r, pl.ds(base, span), :], turn, 0)
        for j in range(3):
            xc2[r, :, j * ch : (j + 1) * ch] = row[j : j + PITCH].astype(BF)
        return carry

    lax.fori_loop(0, WROWS + 2, gather, 0, unroll=2)

    shift = bias[...]
    step = 8

    def conv_two(n, carry):
        acc = jnp.zeros((step * PITCH, ch), F32)
        for i in range(3):
            x = xc2[pl.ds(n * step + i, step)].reshape(step * PITCH, 3 * ch)
            acc = acc + jnp.dot(x, weight[i], preferred_element_type=F32)
        acc = (acc + shift).reshape(step, PITCH, ch)
        y = lax.broadcasted_iota(jnp.int32, acc.shape, 0) + n * step + gy0
        x = lax.broadcasted_iota(jnp.int32, acc.shape, 1) + gx0
        ok = (y >= 0) & (y < height) & (x >= 0) & (x < width)
        acc = jnp.maximum(jnp.where(ok, acc, 0.0), 0.0).reshape(step * PITCH, ch)
        pre2[pl.ds(n * step * PITCH, step * PITCH)] = acc
        f2[pl.ds(n * step * PITCH, step * PITCH)] = acc.astype(BF)
        return carry

    lax.fori_loop(0, WROWS // step, conv_two, 0)

    gwin[...] = jnp.zeros(gwin.shape, F32)
    lanes = GROUP * cols
    bsum = jnp.zeros((1, ch), F32)
    for g in range(rows // GROUP):
        at = slice(g * GROUP * PITCH, (g * GROUP + GROWS) * PITCH)
        px = slice(g * lanes, (g + 1) * lanes)
        gwin[at] += jnp.dot(bt[g], f1[px], preferred_element_type=F32)
        delta = jnp.dot(b[g], f2[at], preferred_element_type=F32) * inv_root
        mine = pre1[g * GROUP : (g + 1) * GROUP].reshape(lanes, ch)
        delta = jnp.where(mine > 0, delta, 0.0).astype(BF)
        d1[px] = delta
        bsum = bsum + jnp.sum(delta.astype(F32), axis=0, keepdims=True)
    delta = jnp.where(pre2[...] > 0, gwin[...] * inv_root, 0.0)
    bsum = bsum + jnp.sum(delta, axis=0, keepdims=True)
    d2t[...] = delta.astype(BF).T
    d1t[...] = d1[...].T
    half_grad(1 - lax.axis_index("core"), d2t, d1t, xc2, xc1, send)
    tail[...] = bias_tile(bsum[:, 0:128], bsum[:, 128:])
    send[9 * ch : 9 * ch + 8] = tail[...].astype(BF)
    send[9 * ch + 8 :] = jnp.zeros((send.shape[0] - 9 * ch - 8, 128), BF)


def bias_tile(low, high):
    row = lax.broadcasted_iota(jnp.int32, (8, 128), 0)
    out = jnp.zeros((8, 128), F32)
    for n, value in enumerate((low, high)):
        top = value.astype(BF).astype(F32)
        out = jnp.where(row == n, top, jnp.where(row == n + 2, value - top, out))
    return out


def bias_again(value):
    return bias_tile(value[0:1] + value[2:3], value[1:2] + value[3:4])


def main(offs, center, xc1, acc1, sides, weight, bias, bt, b, row_count, col_count, flat):
    rows, cols, ch = acc1.shape
    wpx, n2 = WROWS * PITCH, WROWS + 2
    return pl.pallas_call(
        functools.partial(main_kernel, row_count, col_count),
        out_shape=(
            jax.ShapeDtypeStruct((flat, 128), BF),
            jax.ShapeDtypeStruct((8, 128), F32),
            jax.ShapeDtypeStruct((rows * cols, ch), BF),
            jax.ShapeDtypeStruct((wpx, ch), BF),
            jax.ShapeDtypeStruct((n2, PITCH, 3 * ch), BF),
            jax.ShapeDtypeStruct(xc1.shape, BF),
            jax.ShapeDtypeStruct((ch, wpx), BF),
            jax.ShapeDtypeStruct((ch, rows * cols), BF),
        ),
        in_specs=[pl.BlockSpec(memory_space=pl.ANY)] + vmem(11),
        out_specs=tuple(vmem(8)),
        scratch_shapes=[
            pltpu.VMEM((n2, cols + 48, ch), F32),
            pltpu.VMEM((wpx, ch), F32),
            pltpu.VMEM((rows, cols, ch), F32),
            pltpu.VMEM((wpx, ch), F32),
            pltpu.VMEM((rows * cols, ch), BF),
            pltpu.VMEM((rows + 2 * HALO, 16, ch), BF),
            pltpu.SMEM(offs.shape, jnp.int32),
            pltpu.SemaphoreType.DMA(()),
        ],
        compiler_params=params(20),
        cost_estimate=pl.CostEstimate(flops=5_000_000_000, bytes_accessed=8_000_000, transcendentals=0),
        name="main",
    )(offs, center, xc1, acc1, *sides, weight, bias, bt, b)


def keep_kernel(tail, xc2, xc1, d2t, d1t, keep):
    ch = d2t.shape[0]
    half_grad(lax.axis_index("core"), d2t, d1t, xc2, xc1, keep)
    keep[9 * ch : 9 * ch + 8] = tail[...]
    keep[9 * ch + 8 :] = jnp.zeros((keep.shape[0] - 9 * ch - 8, 128), F32)


def keep_half(tail, xc2, xc1, d2t, d1t, flat):
    return pl.pallas_call(
        keep_kernel,
        out_shape=jax.ShapeDtypeStruct((flat, 128), F32),
        in_specs=vmem(5),
        out_specs=vmem(1)[0],
        compiler_params=params(),
        cost_estimate=pl.CostEstimate(flops=1_000_000_000, bytes_accessed=1_000_000, transcendentals=0),
        name="keep",
    )(tail, xc2, xc1, d2t, d1t)


def corr_kernel(f1, f2, before, out, token, lines):
    lanes = GROUP * BLK
    inv_root = f1.shape[1] ** (-0.5)
    lane = lax.broadcasted_iota(jnp.int32, (PITCH, lanes), 1)
    gap = lax.broadcasted_iota(jnp.int32, (PITCH, lanes), 0) - lane % BLK
    own = lane // BLK
    token[...] = jnp.zeros(token.shape, F32)
    lines[WIN * WIN - 1 :] = jnp.zeros((128 - WIN * WIN + 1, lanes), F32)
    for g in range(f1.shape[0] // lanes):
        at = slice(g * GROUP * PITCH, (g * GROUP + GROWS) * PITCH)
        scores = lax.dot_general(
            f2[at], f1[g * lanes : (g + 1) * lanes], (((1,), (1,)), ((), ())),
            preferred_element_type=F32,
        )
        for a in range(WIN):
            pick = scores[a * PITCH : (a + 1) * PITCH]
            for yy in range(1, GROUP):
                pick = jnp.where(own == yy, scores[(a + yy) * PITCH : (a + yy + 1) * PITCH], pick)
            for d in range(WIN):
                line = jnp.sum(jnp.where(gap == d, pick, 0.0), axis=0, keepdims=True) * inv_root
                lines[a * WIN + d : a * WIN + d + 1] = line
        out[g * lanes : (g + 1) * lanes] = lines[...].T[:, : WIN * WIN].astype(BF)


def correlate(f1, f2, before):
    return pl.pallas_call(
        corr_kernel,
        out_shape=(jax.ShapeDtypeStruct((f1.shape[0], WIN * WIN), BF), jax.ShapeDtypeStruct((8, 128), F32)),
        in_specs=vmem(2) + [pl.BlockSpec(memory_space=pl.ANY)],
        out_specs=tuple(vmem(2)),
        scratch_shapes=[pltpu.VMEM((128, GROUP * BLK), F32)],
        compiler_params=params(),
        cost_estimate=pl.CostEstimate(flops=300_000_000, bytes_accessed=1_000_000, transcendentals=0),
        name="corr",
    )(f1, f2, before)


def sum_kernel(rows, parts, after, out):
    size = parts.shape[1]
    for s in range(0, size, 8):
        value = parts[0, s : s + 8].astype(F32)
        for n in range(1, parts.shape[0]):
            value = value + parts[n, s : s + 8].astype(F32)
        if s == rows % size:
            value = jnp.where(place(GROUP_AXES) == rows // size, bias_again(value), value)
        value = value.astype(BF)
        for k in range(out.shape[0]):
            out[k, s : s + 8] = value


def sum_and_copy(parts, copies, rows, after):
    return pl.pallas_call(
        functools.partial(sum_kernel, rows),
        out_shape=jax.ShapeDtypeStruct((copies,) + parts.shape[1:], BF),
        in_specs=vmem(2),
        out_specs=vmem(1)[0],
        compiler_params=params(),
        name="sum",
    )(parts, after)


def merge_kernel(rows, kept, got, out):
    out[...] = (kept[...] + got[...].astype(F32)).astype(BF)
    tail = kept[rows : rows + 8] + got[rows : rows + 8].astype(F32)
    out[rows : rows + 8] = bias_again(tail).astype(BF)


def merge(kept, got, rows):
    return pl.pallas_call(
        functools.partial(merge_kernel, rows),
        out_shape=jax.ShapeDtypeStruct(got.shape, BF),
        in_specs=vmem(2),
        out_specs=vmem(1)[0],
        compiler_params=params(),
        name="merge",
    )(kept, got)


def unpack_half(which, part, held, grad, sems):
    ch = held.shape[1]
    first, rest = which * 6 * ch, 3 * ch + which * (3 * ch // 2) - 6 * 128
    copies = []
    for k in range(9):
        held[k * 128 : (k + 1) * 128] = part[k * ch : (k + 1) * ch].T.astype(F32)
        row = pl.multiple_of((first if k < 6 else rest) + k * 128, 128)
        copies.append(
            pltpu.make_async_copy(held.at[k * 128 : (k + 1) * 128], grad.at[pl.ds(row, 128)], sems.at[k])
        )
        copies[-1].start()
    return copies


def own_kernel(own, grad, held, sems):
    for copy in unpack_half(lax.axis_index("core"), own, held, grad, sems):
        copy.wait()


def other_kernel(own, other, grad_in, grad, bias, held, line, sems):
    core = lax.axis_index("core")
    ch = held.shape[1]
    rows = slice(9 * ch, 9 * ch + 8)
    first = jnp.where(core == 0, own[rows].astype(F32), other[rows].astype(F32))
    line[:, 0:128] = first[0:1] + first[2:3]
    line[:, 128:] = first[1:2] + first[3:4]
    copy = pltpu.make_async_copy(line, bias, sems.at[9])
    copy.start()
    for other_copy in unpack_half(1 - core, other, held, grad, sems):
        other_copy.wait()
    copy.wait()


def unpack(own, other, ch):
    grad = jax.ShapeDtypeStruct((9 * ch, ch), F32)
    held = pltpu.VMEM((9 * ch // 2, ch), F32)
    outside = [pl.BlockSpec(memory_space=pl.ANY)]
    part = pl.pallas_call(
        own_kernel,
        out_shape=grad,
        in_specs=vmem(1),
        out_specs=outside[0],
        scratch_shapes=[held, pltpu.SemaphoreType.DMA((9,))],
        compiler_params=params(),
        cost_estimate=pl.CostEstimate(flops=10_000_000, bytes_accessed=3_000_000, transcendentals=0),
        name="unpack_own",
    )(own)
    return pl.pallas_call(
        other_kernel,
        out_shape=(grad, jax.ShapeDtypeStruct((1, ch), F32)),
        in_specs=vmem(2) + outside,
        out_specs=tuple(outside * 2),
        scratch_shapes=[held, pltpu.VMEM((1, ch), F32), pltpu.SemaphoreType.DMA((10,))],
        input_output_aliases={2: 0},
        compiler_params=params(),
        name="unpack_other",
    )(own, other, part)


def shards(row_count, col_count, space, group, frames, offsets, weight, bias, cotangent):
    rows, cols, ch = frames.shape[2:]
    offs = offsets.reshape(-1, 2)
    *sent, far, near, kept = row_pieces(frames[0])
    got = swap(sent, "row", row_count)
    near, far = swap((near, far), space, col_count)
    bt, b = band(cotangent[0])
    far_corner, near_corner, center, one = corner_pieces(offs, kept, got)
    near_corner, far_corner = swap((near_corner, far_corner), space, col_count)
    sides = (far, near, far_corner, near_corner)
    taps, bias = weight.reshape(3, 3 * ch, ch), bias.reshape(1, ch)
    xc1, acc1 = convolve_one(one, taps, bias)
    count = int(np.prod([lax.axis_size(a) for a in group]))
    depth = lax.axis_size("zh")
    half = 9 * ch
    size = (half + 8 + 8 * count - 1) // (8 * count) * 8
    sent, tail, f1, f2, *rest = main(
        offs, center, xc1, acc1, sides, taps, bias, bt, b, row_count, col_count, size * count
    )
    cores = [(0, 1), (1, 0)]
    got = lax.ppermute(sent, "core", cores)
    kept = keep_half(tail, *rest, size * count)
    parts = merge(kept, got, half)
    parts = lax.all_to_all(parts.reshape(count, size, 128), group, 0, 0, tiled=True)
    parts = sum_and_copy(parts, depth, half, tail)
    corr, token = correlate(f1, f2, parts)
    parts = lax.all_to_all(parts, "zh", 0, 0, tiled=True)
    parts = sum_and_copy(parts, count, half, token)
    parts = lax.all_to_all(parts, group, 0, 0, tiled=True)
    parts = parts.reshape(count * size, 128)
    grad_w, grad_b = unpack(parts, lax.ppermute(parts, "core", cores), ch)
    corr = jnp.transpose(corr.reshape(1, rows, cols, WIN * WIN), (0, 3, 1, 2))
    return corr, grad_w.reshape(3, 3, ch, ch), grad_b.reshape(ch)


def solution(mesh):
    row_count, col_count, pair_count = (mesh.shape[a] for a in ("row", "col", "pair"))
    high = 2 if col_count == 16 else 1
    near = 2 if col_count // high >= 4 else 1
    fine = Mesh(
        mesh.devices.reshape(row_count, high, col_count // high // near, near, pair_count // 2, 2),
        ("row", "high", "zh", "zl", "low", "core"),
    )
    col, pair = SPACE, ("low", "core")
    return jax.shard_map(
        functools.partial(shards, row_count, col_count, col, GROUP_AXES),
        mesh=fine,
        in_specs=(
            P(pair, None, "row", col, None),
            P(pair, None, None, None),
            P(),
            P(),
            P(pair, None, "row", col),
        ),
        out_specs=(P(pair, None, "row", col), P(), P()),
        check_vma=False,
    )
```

```python
import functools

import jax
import jax.numpy as jnp
import numpy as np
from jax import lax
from jax.experimental import pallas as pl
from jax.experimental.pallas import tpu as pltpu
from jax.sharding import Mesh
from jax.sharding import PartitionSpec as P

BLK = 32
RAD = 4
MAXOFF = 8
WIN = 2 * RAD + 1
HALO = MAXOFF + RAD + 1
PITCH = 40
WROWS = 24
GROUP = 4
GROWS = GROUP + WIN - 1
BF = jnp.bfloat16
F32 = jnp.float32


def vmem(n):
    return [pl.BlockSpec(memory_space=pltpu.VMEM)] * n


def params(mib=16):
    return pltpu.CompilerParams(vmem_limit_bytes=mib * 1024 * 1024)


def smem(n):
    return [pl.BlockSpec(memory_space=pltpu.SMEM)] * n


def even(index):
    return lax.rem(index, 2) == 0


def place(axes):
    index = 0
    for axis in axes:
        index = index * lax.axis_size(axis) + lax.axis_index(axis)
    return index


SPACE = ("high", "zh", "zl")
GROUP_AXES = ("row", "high", "zl", "low")


def rows_kernel(frames, first, second, kept):
    rows = frames.shape[1]
    below = even(lax.axis_index("row"))
    for ref, low in ((first, below), (second, jnp.logical_not(below))):
        ref[0:HALO] = frames[1, pl.ds(jnp.where(low, rows - HALO, 0), HALO)]
        ref[HALO] = frames[0, jnp.where(low, rows - 1, 0)]
    kept[...] = frames[...]


def row_pieces(frames):
    cols, ch = frames.shape[2:]
    piece = jax.ShapeDtypeStruct((HALO + 1, cols, ch), BF)
    return pl.pallas_call(
        rows_kernel,
        out_shape=(piece, piece, jax.ShapeDtypeStruct(frames.shape, BF)),
        in_specs=vmem(1),
        out_specs=tuple(vmem(3)),
        compiler_params=params(),
        name="row_pieces",
    )(frames)


def cols_kernel(offs_in, frames, got_first, got_second, second, first, center, one, ext, offs, sem):
    rows, cols, ch = frames.shape[1:]
    fetch = pltpu.make_async_copy(offs_in, offs, sem)
    fetch.start()
    row, column = lax.axis_index("row"), place(SPACE)
    below = even(row)
    count = int(np.prod([lax.axis_size(a) for a in SPACE]))
    base = row * rows // BLK * count
    ext[HALO : HALO + rows] = frames[1]
    one[1 : rows + 1] = frames[0]
    for ref, low in ((got_first, below), (got_second, jnp.logical_not(below))):
        ext[pl.ds(jnp.where(low, HALO + rows, 0), HALO)] = ref[0:HALO]
        one[jnp.where(low, rows + 1, 0)] = ref[HALO]
    fetch.wait()
    center[...] = ext[pl.ds(offs[base + column, 0] + MAXOFF, WROWS + 2)]
    right = even(column)
    col = lax.broadcasted_iota(jnp.int32, (rows + 2, 16, ch), 1)
    for ref, side in ((first, right), (second, jnp.logical_not(right))):
        other = jnp.clip(jnp.where(side, column + 1, column - 1), 0, count - 1)
        start = offs[base + other, 0] + MAXOFF
        at = pl.multiple_of(jnp.where(side, cols - 16, 0), 16)
        ref[...] = ext[pl.ds(start, WROWS + 2), pl.ds(at, 16)]
        border = one[:, pl.ds(at, 16)].astype(F32)
        border = jnp.where(side, border[:, 15:16], border[:, 0:1])
        spare = jnp.where(side, 0, 15)
        ref[0 : rows + 2] = jnp.where(col == spare, border, ref[0 : rows + 2].astype(F32)).astype(BF)


def col_pieces(offs, frames, got):
    rows, cols, ch = frames.shape[1:]
    piece = jax.ShapeDtypeStruct((WROWS + 2, 16, ch), BF)
    return pl.pallas_call(
        cols_kernel,
        out_shape=(
            piece,
            piece,
            jax.ShapeDtypeStruct((WROWS + 2, cols, ch), BF),
            jax.ShapeDtypeStruct((rows + 2, cols, ch), BF),
        ),
        in_specs=[pl.BlockSpec(memory_space=pl.ANY)] + vmem(3),
        out_specs=tuple(vmem(4)),
        scratch_shapes=[
            pltpu.VMEM((rows + 2 * HALO, cols, ch), BF),
            pltpu.SMEM(offs.shape, jnp.int32),
            pltpu.SemaphoreType.DMA(()),
        ],
        compiler_params=params(),
        name="col_pieces",
    )(offs, frames, *got)


def swap(pieces, axes, count):
    got = []
    for piece, start in ((pieces[1], 1), (pieces[0], 0)):
        pairs = []
        for i in range(start, count - 1, 2):
            pairs += [(i, i + 1), (i + 1, i)]
        got.append(lax.ppermute(piece, axes, pairs))
    return got[::-1]


def band_kernel(cot, bt, b, lines):
    count, rows, cols = cot.shape
    lanes = GROUP * BLK

    def iota(shape, axis):
        return lax.broadcasted_iota(jnp.int32, shape, axis)

    copy = (iota((cols, lanes), 1) % cols == iota((cols, lanes), 0)).astype(F32).astype(BF)
    wide = jnp.dot(cot[...].reshape(count * rows, cols), copy, preferred_element_type=F32)
    shape = (WIN * 16, count * rows)
    q, d = iota(shape, 0), iota(shape, 1) // rows
    pickd = ((q // 16 * WIN + q % 16 == d) & (q % 16 < WIN)).astype(F32).astype(BF)
    line = iota((count * rows, lanes), 0) % rows
    want = iota((count * rows, lanes), 1) // cols
    gap = iota((PITCH, lanes), 0) - iota((PITCH, lanes), 1) % BLK
    own = iota((16, lanes), 1) // BLK
    for g in range(bt.shape[0]):
        mine = jnp.where(line == want + g * GROUP, wide, 0.0).astype(BF)
        lines[...] = jnp.dot(pickd, mine, preferred_element_type=F32)
        for r in range(GROWS):
            pick = jnp.zeros((16, lanes), F32)
            for yy in range(GROUP):
                a = r - yy
                if 0 <= a < WIN:
                    pick = jnp.where(own == yy, lines[a * 16 : (a + 1) * 16], pick)
            block = jnp.zeros((PITCH, lanes), F32)
            for k in range(WIN):
                block = jnp.where(gap == k, pick[k : k + 1], block)
            bt[g, r * PITCH : (r + 1) * PITCH] = block.astype(BF)
        b[g] = bt[g].astype(F32).T.astype(BF)


def band(cot):
    groups = cot.shape[1] // GROUP
    return pl.pallas_call(
        band_kernel,
        out_shape=(
            jax.ShapeDtypeStruct((groups, GROWS * PITCH, GROUP * BLK), BF),
            jax.ShapeDtypeStruct((groups, GROUP * BLK, GROWS * PITCH), BF),
        ),
        in_specs=vmem(1),
        out_specs=tuple(vmem(2)),
        scratch_shapes=[pltpu.VMEM((WIN * 16, GROUP * BLK), F32)],
        compiler_params=params(),
        cost_estimate=pl.CostEstimate(flops=2_000_000_000, bytes_accessed=1_000_000, transcendentals=0),
        name="band",
    )(cot)


def one_kernel(one, weight, bias, xc1, acc1, ext):
    rows, cols, ch = one.shape[0] - 2, one.shape[1], one.shape[2]
    ext[:, 0:8] = jnp.zeros((rows + 2, 8, ch), F32)
    ext[:, 8 + cols :] = jnp.zeros((rows + 2, 8, ch), F32)
    ext[:, 8 : 8 + cols] = one[...].astype(F32)
    for j in range(3):
        xc1[:, :, j * ch : (j + 1) * ch] = ext[:, 7 + j : 7 + j + cols].astype(BF)
    step = 8

    def conv(n, carry):
        acc = jnp.zeros((step * cols, ch), F32) + bias[...]
        for i in range(3):
            x = xc1[pl.ds(n * step + i, step)].reshape(step * cols, 3 * ch)
            acc = acc + jnp.dot(x, weight[i], preferred_element_type=F32)
        acc1[pl.ds(n * step, step)] = acc.reshape(step, cols, ch)
        return carry

    lax.fori_loop(0, rows // step, conv, 0)


def convolve_one(one, weight, bias):
    rows, cols, ch = one.shape[0] - 2, one.shape[1], one.shape[2]
    return pl.pallas_call(
        one_kernel,
        out_shape=(
            jax.ShapeDtypeStruct((rows + 2, cols, 3 * ch), BF),
            jax.ShapeDtypeStruct((rows, cols, ch), F32),
        ),
        in_specs=vmem(3),
        out_specs=tuple(vmem(2)),
        scratch_shapes=[pltpu.VMEM((rows + 2, cols + 16, ch), F32)],
        compiler_params=params(),
        cost_estimate=pl.CostEstimate(flops=1_500_000_000, bytes_accessed=1_000_000, transcendentals=0),
        name="one",
    )(one, weight, bias)


def half_grad(which, d2t, d1t, xc2, xc1, out):
    ch, rows, cols = d2t.shape[0], xc1.shape[0] - 2, xc1.shape[1]
    for i, lanes, base in (
        (2 * which, pl.ds(0, 3 * ch), 0),
        (1, pl.ds(pl.multiple_of(which * (3 * ch // 2), 128), 3 * ch // 2), 6),
    ):
        width = lanes.size
        x2 = xc2[pl.ds(i, WROWS), :, lanes].reshape(WROWS * PITCH, width)
        x1 = xc1[pl.ds(i, rows), :, lanes].reshape(rows * cols, width)
        acc = jnp.dot(d2t[...], x2, preferred_element_type=F32)
        acc = acc + jnp.dot(d1t[...], x1, preferred_element_type=F32)
        for k in range(width // 128):
            out[(base + k) * ch : (base + k + 1) * ch] = acc[:, k * 128 : (k + 1) * 128].astype(out.dtype)


def main_kernel(
    row_count, col_count,
    offs_in, center, xc1_in, acc1, got_second, got_first, weight, bias, bt, b,
    send, tail, f1, f2, xc2, xc1, d2t, d1t,
    ext2, pre2, pre1, gwin, d1, offs, sem,
):
    rows, cols, ch = acc1.shape
    fetch = pltpu.make_async_copy(offs_in, offs, sem)
    fetch.start()
    height, width = row_count * rows, col_count * cols
    inv_root = ch ** (-0.5)
    row, column = lax.axis_index("row"), place(SPACE)
    right = even(column)
    ext2[:, 16 : 16 + cols] = center[...].astype(F32)
    v_first, v_second = got_first[...].astype(F32), got_second[...].astype(F32)
    for value, side in ((v_first, right), (v_second, jnp.logical_not(right))):
        ext2[:, pl.ds(pl.multiple_of(jnp.where(side, 16 + cols, 0), 16), 16)] = value
    ext2[:, 32 + cols :] = jnp.zeros((WROWS + 2, ext2.shape[1] - 32 - cols, ch), F32)
    xc1[...] = xc1_in[...]
    pre1[...] = acc1[...]
    col = lax.broadcasted_iota(jnp.int32, (rows + 2, 8, ch), 1)
    n1 = rows + 2
    for j, spot, at, value in (
        (0, 0, 0, jnp.where(right, v_second[0:n1, 0:8], v_first[0:n1, 0:8])),
        (2, 7, cols - 8, jnp.where(right, v_first[0:n1, 8:16], v_second[0:n1, 8:16])),
    ):
        value = jnp.where(col == spot, value, 0.0)
        lanes = slice(j * ch, (j + 1) * ch)
        xc1[:, at : at + 8, lanes] = (xc1_in[:, at : at + 8, lanes].astype(F32) + value).astype(BF)
        value = value.astype(BF)
        acc = jnp.zeros((rows * 8, ch), F32)
        for i in range(3):
            x = value[i : i + rows].reshape(rows * 8, ch)
            acc = acc + jnp.dot(x, weight[i, j * ch : (j + 1) * ch], preferred_element_type=F32)
        pre1[:, at : at + 8] = acc1[:, at : at + 8] + acc.reshape(rows, 8, ch)
    f1[...] = jnp.maximum(pre1[...], 0.0).reshape(rows * cols, ch).astype(BF)

    fetch.wait()
    block = row * rows // BLK * col_count + column
    oy, ox = offs[block, 0], offs[block, 1]
    c0, gy0, gx0 = ox + 16 - RAD - 1, row * rows + oy - RAD, column * cols + ox - RAD
    span = PITCH + 16
    base = pl.multiple_of((c0 // 8) * 8, 8)
    turn = span - c0 % 8

    def gather(r, carry):
        row = pltpu.roll(ext2[r, pl.ds(base, span), :], turn, 0)
        for j in range(3):
            xc2[r, :, j * ch : (j + 1) * ch] = row[j : j + PITCH].astype(BF)
        return carry


    shift = bias[...]
    step = 8

    def conv_two(n, carry):
        acc = jnp.zeros((step * PITCH, ch), F32)
        for i in range(3):
            x = xc2[pl.ds(n * step + i, step)].reshape(step * PITCH, 3 * ch)
            acc = acc + jnp.dot(x, weight[i], preferred_element_type=F32)
        acc = (acc + shift).reshape(step, PITCH, ch)
        y = lax.broadcasted_iota(jnp.int32, acc.shape, 0) + n * step + gy0
        x = lax.broadcasted_iota(jnp.int32, acc.shape, 1) + gx0
        ok = (y >= 0) & (y < height) & (x >= 0) & (x < width)
        acc = jnp.maximum(jnp.where(ok, acc, 0.0), 0.0).reshape(step * PITCH, ch)
        pre2[pl.ds(n * step * PITCH, step * PITCH)] = acc
        f2[pl.ds(n * step * PITCH, step * PITCH)] = acc.astype(BF)
        return carry

    done = 0
    for n in range(WROWS // step):
        for r in range(done, (n + 1) * step + 2):
            gather(r, 0)
        done = (n + 1) * step + 2
        conv_two(n, 0)

    gwin[...] = jnp.zeros(gwin.shape, F32)
    lanes = GROUP * cols
    bsum = jnp.zeros((1, ch), F32)
    for g in range(rows // GROUP):
        at = slice(g * GROUP * PITCH, (g * GROUP + GROWS) * PITCH)
        px = slice(g * lanes, (g + 1) * lanes)
        gwin[at] += jnp.dot(bt[g], f1[px], preferred_element_type=F32)
        delta = jnp.dot(b[g], f2[at], preferred_element_type=F32) * inv_root
        mine = pre1[g * GROUP : (g + 1) * GROUP].reshape(lanes, ch)
        delta = jnp.where(mine > 0, delta, 0.0).astype(BF)
        d1[px] = delta
        bsum = bsum + jnp.sum(delta.astype(F32), axis=0, keepdims=True)
    delta = jnp.where(pre2[...] > 0, gwin[...] * inv_root, 0.0)
    bsum = bsum + jnp.sum(delta, axis=0, keepdims=True)
    d2t[...] = delta.astype(BF).T
    d1t[...] = d1[...].T
    half_grad(1 - lax.axis_index("core"), d2t, d1t, xc2, xc1, send)
    tail[...] = bias_tile(bsum[:, 0:128], bsum[:, 128:])
    send[9 * ch : 9 * ch + 8] = tail[...].astype(BF)
    send[9 * ch + 8 :] = jnp.zeros((send.shape[0] - 9 * ch - 8, 128), BF)


def bias_tile(low, high):
    row = lax.broadcasted_iota(jnp.int32, (8, 128), 0)
    out = jnp.zeros((8, 128), F32)
    for n, value in enumerate((low, high)):
        top = value.astype(BF).astype(F32)
        out = jnp.where(row == n, top, jnp.where(row == n + 2, value - top, out))
    return out


def bias_again(value):
    return bias_tile(value[0:1] + value[2:3], value[1:2] + value[3:4])


def main(offs, center, xc1, acc1, got, weight, bias, bt, b, row_count, col_count, flat):
    rows, cols, ch = acc1.shape
    wpx, n2 = WROWS * PITCH, WROWS + 2
    return pl.pallas_call(
        functools.partial(main_kernel, row_count, col_count),
        out_shape=(
            jax.ShapeDtypeStruct((flat, 128), BF),
            jax.ShapeDtypeStruct((8, 128), F32),
            jax.ShapeDtypeStruct((rows * cols, ch), BF),
            jax.ShapeDtypeStruct((wpx, ch), BF),
            jax.ShapeDtypeStruct((n2, PITCH, 3 * ch), BF),
            jax.ShapeDtypeStruct(xc1.shape, BF),
            jax.ShapeDtypeStruct((ch, wpx), BF),
            jax.ShapeDtypeStruct((ch, rows * cols), BF),
        ),
        in_specs=[pl.BlockSpec(memory_space=pl.ANY)] + vmem(9),
        out_specs=tuple(vmem(8)),
        scratch_shapes=[
            pltpu.VMEM((n2, cols + 48, ch), F32),
            pltpu.VMEM((wpx, ch), F32),
            pltpu.VMEM((rows, cols, ch), F32),
            pltpu.VMEM((wpx, ch), F32),
            pltpu.VMEM((rows * cols, ch), BF),
            pltpu.SMEM(offs.shape, jnp.int32),
            pltpu.SemaphoreType.DMA(()),
        ],
        compiler_params=params(20),
        cost_estimate=pl.CostEstimate(flops=5_000_000_000, bytes_accessed=8_000_000, transcendentals=0),
        name="main",
    )(offs, center, xc1, acc1, got[1], got[0], weight, bias, bt, b)


def keep_kernel(tail, xc2, xc1, d2t, d1t, keep):
    ch = d2t.shape[0]
    half_grad(lax.axis_index("core"), d2t, d1t, xc2, xc1, keep)
    keep[9 * ch : 9 * ch + 8] = tail[...]
    keep[9 * ch + 8 :] = jnp.zeros((keep.shape[0] - 9 * ch - 8, 128), F32)


def keep_half(tail, xc2, xc1, d2t, d1t, flat):
    return pl.pallas_call(
        keep_kernel,
        out_shape=jax.ShapeDtypeStruct((flat, 128), F32),
        in_specs=vmem(5),
        out_specs=vmem(1)[0],
        compiler_params=params(),
        cost_estimate=pl.CostEstimate(flops=1_000_000_000, bytes_accessed=1_000_000, transcendentals=0),
        name="keep",
    )(tail, xc2, xc1, d2t, d1t)


def corr_kernel(f1, f2, before, out, token, lines):
    lanes = GROUP * BLK
    inv_root = f1.shape[1] ** (-0.5)
    lane = lax.broadcasted_iota(jnp.int32, (PITCH, lanes), 1)
    gap = lax.broadcasted_iota(jnp.int32, (PITCH, lanes), 0) - lane % BLK
    own = lane // BLK
    token[...] = jnp.zeros(token.shape, F32)
    lines[WIN * WIN - 1 :] = jnp.zeros((128 - WIN * WIN + 1, lanes), F32)
    for g in range(f1.shape[0] // lanes):
        at = slice(g * GROUP * PITCH, (g * GROUP + GROWS) * PITCH)
        scores = lax.dot_general(
            f2[at], f1[g * lanes : (g + 1) * lanes], (((1,), (1,)), ((), ())),
            preferred_element_type=F32,
        )
        for a in range(WIN):
            pick = scores[a * PITCH : (a + 1) * PITCH]
            for yy in range(1, GROUP):
                pick = jnp.where(own == yy, scores[(a + yy) * PITCH : (a + yy + 1) * PITCH], pick)
            for d in range(WIN):
                line = jnp.sum(jnp.where(gap == d, pick, 0.0), axis=0, keepdims=True) * inv_root
                lines[a * WIN + d : a * WIN + d + 1] = line
        out[g * lanes : (g + 1) * lanes] = lines[...].T[:, : WIN * WIN].astype(BF)


def correlate(f1, f2, before):
    return pl.pallas_call(
        corr_kernel,
        out_shape=(jax.ShapeDtypeStruct((f1.shape[0], WIN * WIN), BF), jax.ShapeDtypeStruct((8, 128), F32)),
        in_specs=vmem(2) + [pl.BlockSpec(memory_space=pl.ANY)],
        out_specs=tuple(vmem(2)),
        scratch_shapes=[pltpu.VMEM((128, GROUP * BLK), F32)],
        compiler_params=params(),
        cost_estimate=pl.CostEstimate(flops=300_000_000, bytes_accessed=1_000_000, transcendentals=0),
        name="corr",
    )(f1, f2, before)


def sum_kernel(rows, parts, after, out):
    size = parts.shape[1]
    for s in range(0, size, 8):
        value = parts[0, s : s + 8].astype(F32)
        for n in range(1, parts.shape[0]):
            value = value + parts[n, s : s + 8].astype(F32)
        if s == rows % size:
            value = jnp.where(place(GROUP_AXES) == rows // size, bias_again(value), value)
        value = value.astype(BF)
        for k in range(out.shape[0]):
            out[k, s : s + 8] = value


def sum_and_copy(parts, copies, rows, after):
    return pl.pallas_call(
        functools.partial(sum_kernel, rows),
        out_shape=jax.ShapeDtypeStruct((copies,) + parts.shape[1:], BF),
        in_specs=vmem(2),
        out_specs=vmem(1)[0],
        compiler_params=params(),
        name="sum",
    )(parts, after)


def merge_kernel(rows, kept, got, out):
    out[...] = (kept[...] + got[...].astype(F32)).astype(BF)
    tail = kept[rows : rows + 8] + got[rows : rows + 8].astype(F32)
    out[rows : rows + 8] = bias_again(tail).astype(BF)


def merge(kept, got, rows):
    return pl.pallas_call(
        functools.partial(merge_kernel, rows),
        out_shape=jax.ShapeDtypeStruct(got.shape, BF),
        in_specs=vmem(2),
        out_specs=vmem(1)[0],
        compiler_params=params(),
        name="merge",
    )(kept, got)


def unpack_half(which, part, held, grad, sems):
    ch = held.shape[1]
    first, rest = which * 6 * ch, 3 * ch + which * (3 * ch // 2) - 6 * 128
    copies = []
    for k in range(9):
        held[k * 128 : (k + 1) * 128] = part[k * ch : (k + 1) * ch].T.astype(F32)
        row = pl.multiple_of((first if k < 6 else rest) + k * 128, 128)
        copies.append(
            pltpu.make_async_copy(held.at[k * 128 : (k + 1) * 128], grad.at[pl.ds(row, 128)], sems.at[k])
        )
        copies[-1].start()
    return copies


def own_kernel(own, grad, held, sems):
    for copy in unpack_half(lax.axis_index("core"), own, held, grad, sems):
        copy.wait()


def other_kernel(own, other, grad_in, grad, bias, held, line, sems):
    core = lax.axis_index("core")
    ch = held.shape[1]
    rows = slice(9 * ch, 9 * ch + 8)
    first = jnp.where(core == 0, own[rows].astype(F32), other[rows].astype(F32))
    line[:, 0:128] = first[0:1] + first[2:3]
    line[:, 128:] = first[1:2] + first[3:4]
    copy = pltpu.make_async_copy(line, bias, sems.at[9])
    copy.start()
    for other_copy in unpack_half(1 - core, other, held, grad, sems):
        other_copy.wait()
    copy.wait()


def unpack(own, other, ch):
    grad = jax.ShapeDtypeStruct((9 * ch, ch), F32)
    held = pltpu.VMEM((9 * ch // 2, ch), F32)
    outside = [pl.BlockSpec(memory_space=pl.ANY)]
    part = pl.pallas_call(
        own_kernel,
        out_shape=grad,
        in_specs=vmem(1),
        out_specs=outside[0],
        scratch_shapes=[held, pltpu.SemaphoreType.DMA((9,))],
        compiler_params=params(),
        cost_estimate=pl.CostEstimate(flops=10_000_000, bytes_accessed=3_000_000, transcendentals=0),
        name="unpack_own",
    )(own)
    return pl.pallas_call(
        other_kernel,
        out_shape=(grad, jax.ShapeDtypeStruct((1, ch), F32)),
        in_specs=vmem(2) + outside,
        out_specs=tuple(outside * 2),
        scratch_shapes=[held, pltpu.VMEM((1, ch), F32), pltpu.SemaphoreType.DMA((10,))],
        input_output_aliases={2: 0},
        compiler_params=params(),
        name="unpack_other",
    )(own, other, part)


def shards(row_count, col_count, space, group, frames, offsets, weight, bias, cotangent):
    rows, cols, ch = frames.shape[2:]
    offs = offsets.reshape(-1, 2)
    *sent, kept = row_pieces(frames[0])
    got = swap(sent, "row", row_count)
    bt, b = band(cotangent[0])
    second, first, center, one = col_pieces(offs, kept, got)
    got = swap((first, second), space, col_count)
    taps, bias = weight.reshape(3, 3 * ch, ch), bias.reshape(1, ch)
    xc1, acc1 = convolve_one(one, taps, bias)
    count = int(np.prod([lax.axis_size(a) for a in group]))
    depth = lax.axis_size("zh")
    half = 9 * ch
    size = (half + 8 + 8 * count - 1) // (8 * count) * 8
    sent, tail, f1, f2, *rest = main(
        offs, center, xc1, acc1, got, taps, bias, bt, b, row_count, col_count, size * count
    )
    cores = [(0, 1), (1, 0)]
    got = lax.ppermute(sent, "core", cores)
    kept = keep_half(tail, *rest, size * count)
    parts = merge(kept, got, half)
    parts = lax.all_to_all(parts.reshape(count, size, 128), group, 0, 0, tiled=True)
    parts = sum_and_copy(parts, depth, half, tail)
    corr, token = correlate(f1, f2, parts)
    parts = lax.all_to_all(parts, "zh", 0, 0, tiled=True)
    parts = sum_and_copy(parts, count, half, token)
    parts = lax.all_to_all(parts, group, 0, 0, tiled=True)
    parts = parts.reshape(count * size, 128)
    grad_w, grad_b = unpack(parts, lax.ppermute(parts, "core", cores), ch)
    corr = jnp.transpose(corr.reshape(1, rows, cols, WIN * WIN), (0, 3, 1, 2))
    return corr, grad_w.reshape(3, 3, ch, ch), grad_b.reshape(ch)


def solution(mesh):
    row_count, col_count, pair_count = (mesh.shape[a] for a in ("row", "col", "pair"))
    high = 2 if col_count == 16 else 1
    near = 2 if col_count // high >= 4 else 1
    fine = Mesh(
        mesh.devices.reshape(row_count, high, col_count // high // near, near, pair_count // 2, 2),
        ("row", "high", "zh", "zl", "low", "core"),
    )
    col, pair = SPACE, ("low", "core")
    return jax.shard_map(
        functools.partial(shards, row_count, col_count, col, GROUP_AXES),
        mesh=fine,
        in_specs=(
            P(pair, None, "row", col, None),
            P(pair, None, None, None),
            P(),
            P(),
            P(pair, None, "row", col),
        ),
        out_specs=(P(pair, None, "row", col), P(), P()),
        check_vma=False,
    )
```

```python
import functools

import jax
import jax.numpy as jnp
import numpy as np
from jax import lax
from jax.experimental import pallas as pl
from jax.experimental.pallas import tpu as pltpu
from jax.sharding import Mesh
from jax.sharding import PartitionSpec as P

BLK = 32
RAD = 4
MAXOFF = 8
WIN = 2 * RAD + 1
HALO = MAXOFF + RAD + 1
PITCH = 40
WROWS = 24
GROUP = 4
GROWS = GROUP + WIN - 1
BF = jnp.bfloat16
F32 = jnp.float32


def vmem(n):
    return [pl.BlockSpec(memory_space=pltpu.VMEM)] * n


def params(mib=16):
    return pltpu.CompilerParams(vmem_limit_bytes=mib * 1024 * 1024)


def smem(n):
    return [pl.BlockSpec(memory_space=pltpu.SMEM)] * n


def even(index):
    return lax.rem(index, 2) == 0


def place(axes):
    index = 0
    for axis in axes:
        index = index * lax.axis_size(axis) + lax.axis_index(axis)
    return index


SPACE = ("high", "zh", "zl")
GROUP_AXES = ("row", "high", "zl", "low")


def rows_kernel(frames, first, second, kept):
    rows = frames.shape[1]
    below = even(lax.axis_index("row"))
    for ref, low in ((first, below), (second, jnp.logical_not(below))):
        ref[0:HALO] = frames[1, pl.ds(jnp.where(low, rows - HALO, 0), HALO)]
        ref[HALO] = frames[0, jnp.where(low, rows - 1, 0)]
    kept[...] = frames[...]


def row_pieces(frames):
    cols, ch = frames.shape[2:]
    piece = jax.ShapeDtypeStruct((HALO + 1, cols, ch), BF)
    return pl.pallas_call(
        rows_kernel,
        out_shape=(piece, piece, jax.ShapeDtypeStruct(frames.shape, BF)),
        in_specs=vmem(1),
        out_specs=tuple(vmem(3)),
        compiler_params=params(),
        name="row_pieces",
    )(frames)


def cols_kernel(offs, frames, got_first, got_second, second, first, center, one, ext):
    rows, cols, ch = frames.shape[1:]
    row, column = lax.axis_index("row"), place(SPACE)
    below = even(row)
    count = int(np.prod([lax.axis_size(a) for a in SPACE]))
    base = row * rows // BLK * count
    ext[HALO : HALO + rows] = frames[1]
    one[1 : rows + 1] = frames[0]
    for ref, low in ((got_first, below), (got_second, jnp.logical_not(below))):
        ext[pl.ds(jnp.where(low, HALO + rows, 0), HALO)] = ref[0:HALO]
        one[jnp.where(low, rows + 1, 0)] = ref[HALO]

    def down(index):
        values = offs[...].astype(F32)
        here = lax.broadcasted_iota(jnp.int32, values.shape, 0) == index
        here = here & (lax.broadcasted_iota(jnp.int32, values.shape, 1) == 0)
        return jnp.sum(jnp.where(here, values, 0.0)).astype(jnp.int32)

    center[...] = ext[pl.ds(down(base + column) + MAXOFF, WROWS + 2)]
    right = even(column)
    col = lax.broadcasted_iota(jnp.int32, (rows + 2, 16, ch), 1)
    for ref, side in ((first, right), (second, jnp.logical_not(right))):
        other = jnp.clip(jnp.where(side, column + 1, column - 1), 0, count - 1)
        start = down(base + other) + MAXOFF
        at = pl.multiple_of(jnp.where(side, cols - 16, 0), 16)
        ref[...] = ext[pl.ds(start, WROWS + 2), pl.ds(at, 16)]
        border = one[:, pl.ds(at, 16)].astype(F32)
        border = jnp.where(side, border[:, 15:16], border[:, 0:1])
        spare = jnp.where(side, 0, 15)
        ref[0 : rows + 2] = jnp.where(col == spare, border, ref[0 : rows + 2].astype(F32)).astype(BF)


def col_pieces(offs, frames, got):
    rows, cols, ch = frames.shape[1:]
    piece = jax.ShapeDtypeStruct((WROWS + 2, 16, ch), BF)
    return pl.pallas_call(
        cols_kernel,
        out_shape=(
            piece,
            piece,
            jax.ShapeDtypeStruct((WROWS + 2, cols, ch), BF),
            jax.ShapeDtypeStruct((rows + 2, cols, ch), BF),
        ),
        in_specs=vmem(4),
        out_specs=tuple(vmem(4)),
        scratch_shapes=[
            pltpu.VMEM((rows + 2 * HALO, cols, ch), BF),
        ],
        compiler_params=params(),
        name="col_pieces",
    )(offs, frames, *got)


def swap(pieces, axes, count):
    got = []
    for piece, start in ((pieces[1], 1), (pieces[0], 0)):
        pairs = []
        for i in range(start, count - 1, 2):
            pairs += [(i, i + 1), (i + 1, i)]
        got.append(lax.ppermute(piece, axes, pairs))
    return got[::-1]


def band_kernel(cot, bt, b, lines):
    count, rows, cols = cot.shape
    lanes = GROUP * BLK

    def iota(shape, axis):
        return lax.broadcasted_iota(jnp.int32, shape, axis)

    copy = (iota((cols, lanes), 1) % cols == iota((cols, lanes), 0)).astype(F32).astype(BF)
    wide = jnp.dot(cot[...].reshape(count * rows, cols), copy, preferred_element_type=F32)
    shape = (WIN * 16, count * rows)
    q, d = iota(shape, 0), iota(shape, 1) // rows
    pickd = ((q // 16 * WIN + q % 16 == d) & (q % 16 < WIN)).astype(F32).astype(BF)
    line = iota((count * rows, lanes), 0) % rows
    want = iota((count * rows, lanes), 1) // cols
    gap = iota((PITCH, lanes), 0) - iota((PITCH, lanes), 1) % BLK
    own = iota((16, lanes), 1) // BLK
    for g in range(bt.shape[0]):
        mine = jnp.where(line == want + g * GROUP, wide, 0.0).astype(BF)
        lines[...] = jnp.dot(pickd, mine, preferred_element_type=F32)
        for r in range(GROWS):
            pick = jnp.zeros((16, lanes), F32)
            for yy in range(GROUP):
                a = r - yy
                if 0 <= a < WIN:
                    pick = jnp.where(own == yy, lines[a * 16 : (a + 1) * 16], pick)
            block = jnp.zeros((PITCH, lanes), F32)
            for k in range(WIN):
                block = jnp.where(gap == k, pick[k : k + 1], block)
            bt[g, r * PITCH : (r + 1) * PITCH] = block.astype(BF)
        b[g] = bt[g].astype(F32).T.astype(BF)


def band(cot):
    groups = cot.shape[1] // GROUP
    return pl.pallas_call(
        band_kernel,
        out_shape=(
            jax.ShapeDtypeStruct((groups, GROWS * PITCH, GROUP * BLK), BF),
            jax.ShapeDtypeStruct((groups, GROUP * BLK, GROWS * PITCH), BF),
        ),
        in_specs=vmem(1),
        out_specs=tuple(vmem(2)),
        scratch_shapes=[pltpu.VMEM((WIN * 16, GROUP * BLK), F32)],
        compiler_params=params(),
        cost_estimate=pl.CostEstimate(flops=2_000_000_000, bytes_accessed=1_000_000, transcendentals=0),
        name="band",
    )(cot)


def one_kernel(one, weight, bias, xc1, acc1, ext):
    rows, cols, ch = one.shape[0] - 2, one.shape[1], one.shape[2]
    ext[:, 0:8] = jnp.zeros((rows + 2, 8, ch), F32)
    ext[:, 8 + cols :] = jnp.zeros((rows + 2, 8, ch), F32)
    ext[:, 8 : 8 + cols] = one[...].astype(F32)
    for j in range(3):
        xc1[:, :, j * ch : (j + 1) * ch] = ext[:, 7 + j : 7 + j + cols].astype(BF)
    step = 8

    def conv(n, carry):
        acc = jnp.zeros((step * cols, ch), F32) + bias[...]
        for i in range(3):
            x = xc1[pl.ds(n * step + i, step)].reshape(step * cols, 3 * ch)
            acc = acc + jnp.dot(x, weight[i], preferred_element_type=F32)
        acc1[pl.ds(n * step, step)] = acc.reshape(step, cols, ch)
        return carry

    lax.fori_loop(0, rows // step, conv, 0)


def convolve_one(one, weight, bias):
    rows, cols, ch = one.shape[0] - 2, one.shape[1], one.shape[2]
    return pl.pallas_call(
        one_kernel,
        out_shape=(
            jax.ShapeDtypeStruct((rows + 2, cols, 3 * ch), BF),
            jax.ShapeDtypeStruct((rows, cols, ch), F32),
        ),
        in_specs=vmem(3),
        out_specs=tuple(vmem(2)),
        scratch_shapes=[pltpu.VMEM((rows + 2, cols + 16, ch), F32)],
        compiler_params=params(),
        cost_estimate=pl.CostEstimate(flops=1_500_000_000, bytes_accessed=1_000_000, transcendentals=0),
        name="one",
    )(one, weight, bias)


def half_grad(which, d2t, d1t, xc2, xc1, out):
    ch, rows, cols = d2t.shape[0], xc1.shape[0] - 2, xc1.shape[1]
    for i, lanes, base in (
        (2 * which, pl.ds(0, 3 * ch), 0),
        (1, pl.ds(pl.multiple_of(which * (3 * ch // 2), 128), 3 * ch // 2), 6),
    ):
        width = lanes.size
        x2 = xc2[pl.ds(i, WROWS), :, lanes].reshape(WROWS * PITCH, width)
        x1 = xc1[pl.ds(i, rows), :, lanes].reshape(rows * cols, width)
        acc = jnp.dot(d2t[...], x2, preferred_element_type=F32)
        acc = acc + jnp.dot(d1t[...], x1, preferred_element_type=F32)
        for k in range(width // 128):
            out[(base + k) * ch : (base + k + 1) * ch] = acc[:, k * 128 : (k + 1) * 128].astype(out.dtype)


def main_kernel(
    row_count, col_count,
    offs_in, center, xc1_in, acc1, got_second, got_first, weight, bias, bt, b,
    send, tail, f1, f2, xc2, xc1, d2t, d1t,
    ext2, pre2, pre1, gwin, d1, offs, sem,
):
    rows, cols, ch = acc1.shape
    fetch = pltpu.make_async_copy(offs_in, offs, sem)
    fetch.start()
    height, width = row_count * rows, col_count * cols
    inv_root = ch ** (-0.5)
    row, column = lax.axis_index("row"), place(SPACE)
    right = even(column)
    ext2[:, 16 : 16 + cols] = center[...].astype(F32)
    v_first, v_second = got_first[...].astype(F32), got_second[...].astype(F32)
    for value, side in ((v_first, right), (v_second, jnp.logical_not(right))):
        ext2[:, pl.ds(pl.multiple_of(jnp.where(side, 16 + cols, 0), 16), 16)] = value
    ext2[:, 32 + cols :] = jnp.zeros((WROWS + 2, ext2.shape[1] - 32 - cols, ch), F32)
    xc1[...] = xc1_in[...]
    pre1[...] = acc1[...]
    col = lax.broadcasted_iota(jnp.int32, (rows + 2, 8, ch), 1)
    n1 = rows + 2
    for j, spot, at, value in (
        (0, 0, 0, jnp.where(right, v_second[0:n1, 0:8], v_first[0:n1, 0:8])),
        (2, 7, cols - 8, jnp.where(right, v_first[0:n1, 8:16], v_second[0:n1, 8:16])),
    ):
        value = jnp.where(col == spot, value, 0.0)
        lanes = slice(j * ch, (j + 1) * ch)
        xc1[:, at : at + 8, lanes] = (xc1_in[:, at : at + 8, lanes].astype(F32) + value).astype(BF)
        value = value.astype(BF)
        acc = jnp.zeros((rows * 8, ch), F32)
        for i in range(3):
            x = value[i : i + rows].reshape(rows * 8, ch)
            acc = acc + jnp.dot(x, weight[i, j * ch : (j + 1) * ch], preferred_element_type=F32)
        pre1[:, at : at + 8] = acc1[:, at : at + 8] + acc.reshape(rows, 8, ch)
    f1[...] = jnp.maximum(pre1[...], 0.0).reshape(rows * cols, ch).astype(BF)

    fetch.wait()
    block = row * rows // BLK * col_count + column
    oy, ox = offs[block, 0], offs[block, 1]
    c0, gy0, gx0 = ox + 16 - RAD - 1, row * rows + oy - RAD, column * cols + ox - RAD
    span = PITCH + 16
    base = pl.multiple_of((c0 // 8) * 8, 8)
    turn = span - c0 % 8

    def gather(r, carry):
        row = pltpu.roll(ext2[r, pl.ds(base, span), :], turn, 0)
        for j in range(3):
            xc2[r, :, j * ch : (j + 1) * ch] = row[j : j + PITCH].astype(BF)
        return carry


    shift = bias[...]
    step = 12

    def conv_two(n, carry):
        acc = jnp.zeros((step * PITCH, ch), F32)
        for i in range(3):
            x = xc2[pl.ds(n * step + i, step)].reshape(step * PITCH, 3 * ch)
            acc = acc + jnp.dot(x, weight[i], preferred_element_type=F32)
        acc = (acc + shift).reshape(step, PITCH, ch)
        y = lax.broadcasted_iota(jnp.int32, acc.shape, 0) + n * step + gy0
        x = lax.broadcasted_iota(jnp.int32, acc.shape, 1) + gx0
        ok = (y >= 0) & (y < height) & (x >= 0) & (x < width)
        acc = jnp.maximum(jnp.where(ok, acc, 0.0), 0.0).reshape(step * PITCH, ch)
        pre2[pl.ds(n * step * PITCH, step * PITCH)] = acc
        f2[pl.ds(n * step * PITCH, step * PITCH)] = acc.astype(BF)
        return carry

    done = 0
    for n in range(WROWS // step):
        for r in range(done, (n + 1) * step + 2):
            gather(r, 0)
        done = (n + 1) * step + 2
        conv_two(n, 0)

    gwin[...] = jnp.zeros(gwin.shape, F32)
    lanes = GROUP * cols
    bsum = jnp.zeros((1, ch), F32)
    for g in range(rows // GROUP):
        at = slice(g * GROUP * PITCH, (g * GROUP + GROWS) * PITCH)
        px = slice(g * lanes, (g + 1) * lanes)
        gwin[at] += jnp.dot(bt[g], f1[px], preferred_element_type=F32)
        delta = jnp.dot(b[g], f2[at], preferred_element_type=F32) * inv_root
        mine = pre1[g * GROUP : (g + 1) * GROUP].reshape(lanes, ch)
        delta = jnp.where(mine > 0, delta, 0.0).astype(BF)
        d1[px] = delta
        bsum = bsum + jnp.sum(delta.astype(F32), axis=0, keepdims=True)
    delta = jnp.where(pre2[...] > 0, gwin[...] * inv_root, 0.0)
    bsum = bsum + jnp.sum(delta, axis=0, keepdims=True)
    d2t[...] = delta.astype(BF).T
    d1t[...] = d1[...].T
    half_grad(1 - lax.axis_index("core"), d2t, d1t, xc2, xc1, send)
    tail[...] = bias_tile(bsum[:, 0:128], bsum[:, 128:])
    send[9 * ch : 9 * ch + 8] = tail[...].astype(BF)
    send[9 * ch + 8 :] = jnp.zeros((send.shape[0] - 9 * ch - 8, 128), BF)


def bias_tile(low, high):
    row = lax.broadcasted_iota(jnp.int32, (8, 128), 0)
    out = jnp.zeros((8, 128), F32)
    for n, value in enumerate((low, high)):
        top = value.astype(BF).astype(F32)
        out = jnp.where(row == n, top, jnp.where(row == n + 2, value - top, out))
    return out


def bias_again(value):
    return bias_tile(value[0:1] + value[2:3], value[1:2] + value[3:4])


def main(offs, center, xc1, acc1, got, weight, bias, bt, b, row_count, col_count, flat):
    rows, cols, ch = acc1.shape
    wpx, n2 = WROWS * PITCH, WROWS + 2
    return pl.pallas_call(
        functools.partial(main_kernel, row_count, col_count),
        out_shape=(
            jax.ShapeDtypeStruct((flat, 128), BF),
            jax.ShapeDtypeStruct((8, 128), F32),
            jax.ShapeDtypeStruct((rows * cols, ch), BF),
            jax.ShapeDtypeStruct((wpx, ch), BF),
            jax.ShapeDtypeStruct((n2, PITCH, 3 * ch), BF),
            jax.ShapeDtypeStruct(xc1.shape, BF),
            jax.ShapeDtypeStruct((ch, wpx), BF),
            jax.ShapeDtypeStruct((ch, rows * cols), BF),
        ),
        in_specs=[pl.BlockSpec(memory_space=pl.ANY)] + vmem(9),
        out_specs=tuple(vmem(8)),
        scratch_shapes=[
            pltpu.VMEM((n2, cols + 48, ch), F32),
            pltpu.VMEM((wpx, ch), F32),
            pltpu.VMEM((rows, cols, ch), F32),
            pltpu.VMEM((wpx, ch), F32),
            pltpu.VMEM((rows * cols, ch), BF),
            pltpu.SMEM(offs.shape, jnp.int32),
            pltpu.SemaphoreType.DMA(()),
        ],
        compiler_params=params(20),
        cost_estimate=pl.CostEstimate(flops=5_000_000_000, bytes_accessed=8_000_000, transcendentals=0),
        name="main",
    )(offs, center, xc1, acc1, got[1], got[0], weight, bias, bt, b)


def keep_kernel(tail, xc2, xc1, d2t, d1t, keep):
    ch = d2t.shape[0]
    half_grad(lax.axis_index("core"), d2t, d1t, xc2, xc1, keep)
    keep[9 * ch : 9 * ch + 8] = tail[...]
    keep[9 * ch + 8 :] = jnp.zeros((keep.shape[0] - 9 * ch - 8, 128), F32)


def keep_half(tail, xc2, xc1, d2t, d1t, flat):
    return pl.pallas_call(
        keep_kernel,
        out_shape=jax.ShapeDtypeStruct((flat, 128), F32),
        in_specs=vmem(5),
        out_specs=vmem(1)[0],
        compiler_params=params(),
        cost_estimate=pl.CostEstimate(flops=1_000_000_000, bytes_accessed=1_000_000, transcendentals=0),
        name="keep",
    )(tail, xc2, xc1, d2t, d1t)


def corr_kernel(f1, f2, before, out, token, lines):
    lanes = GROUP * BLK
    inv_root = f1.shape[1] ** (-0.5)
    lane = lax.broadcasted_iota(jnp.int32, (PITCH, lanes), 1)
    gap = lax.broadcasted_iota(jnp.int32, (PITCH, lanes), 0) - lane % BLK
    own = lane // BLK
    token[...] = jnp.zeros(token.shape, F32)
    lines[WIN * WIN - 1 :] = jnp.zeros((128 - WIN * WIN + 1, lanes), F32)
    for g in range(f1.shape[0] // lanes):
        at = slice(g * GROUP * PITCH, (g * GROUP + GROWS) * PITCH)
        scores = lax.dot_general(
            f2[at], f1[g * lanes : (g + 1) * lanes], (((1,), (1,)), ((), ())),
            preferred_element_type=F32,
        )
        for a in range(WIN):
            pick = scores[a * PITCH : (a + 1) * PITCH]
            for yy in range(1, GROUP):
                pick = jnp.where(own == yy, scores[(a + yy) * PITCH : (a + yy + 1) * PITCH], pick)
            for d in range(WIN):
                line = jnp.sum(jnp.where(gap == d, pick, 0.0), axis=0, keepdims=True) * inv_root
                lines[a * WIN + d : a * WIN + d + 1] = line
        out[g * lanes : (g + 1) * lanes] = lines[...].T[:, : WIN * WIN].astype(BF)


def correlate(f1, f2, before):
    return pl.pallas_call(
        corr_kernel,
        out_shape=(jax.ShapeDtypeStruct((f1.shape[0], WIN * WIN), BF), jax.ShapeDtypeStruct((8, 128), F32)),
        in_specs=vmem(2) + [pl.BlockSpec(memory_space=pl.ANY)],
        out_specs=tuple(vmem(2)),
        scratch_shapes=[pltpu.VMEM((128, GROUP * BLK), F32)],
        compiler_params=params(),
        cost_estimate=pl.CostEstimate(flops=300_000_000, bytes_accessed=1_000_000, transcendentals=0),
        name="corr",
    )(f1, f2, before)


def sum_kernel(rows, parts, after, out):
    size = parts.shape[1]
    for s in range(0, size, 8):
        value = parts[0, s : s + 8].astype(F32)
        for n in range(1, parts.shape[0]):
            value = value + parts[n, s : s + 8].astype(F32)
        if s == rows % size:
            value = jnp.where(place(GROUP_AXES) == rows // size, bias_again(value), value)
        value = value.astype(BF)
        for k in range(out.shape[0]):
            out[k, s : s + 8] = value


def sum_and_copy(parts, copies, rows, after):
    return pl.pallas_call(
        functools.partial(sum_kernel, rows),
        out_shape=jax.ShapeDtypeStruct((copies,) + parts.shape[1:], BF),
        in_specs=vmem(2),
        out_specs=vmem(1)[0],
        compiler_params=params(),
        name="sum",
    )(parts, after)


def merge_kernel(rows, kept, got, out):
    out[...] = (kept[...] + got[...].astype(F32)).astype(BF)
    tail = kept[rows : rows + 8] + got[rows : rows + 8].astype(F32)
    out[rows : rows + 8] = bias_again(tail).astype(BF)


def merge(kept, got, rows):
    return pl.pallas_call(
        functools.partial(merge_kernel, rows),
        out_shape=jax.ShapeDtypeStruct(got.shape, BF),
        in_specs=vmem(2),
        out_specs=vmem(1)[0],
        compiler_params=params(),
        name="merge",
    )(kept, got)


def unpack_half(which, part, held, grad, sems):
    ch = held.shape[1]
    first, rest = which * 6 * ch, 3 * ch + which * (3 * ch // 2) - 6 * 128
    copies = []
    for k in range(9):
        held[k * 128 : (k + 1) * 128] = part[k * ch : (k + 1) * ch].T.astype(F32)
        row = pl.multiple_of((first if k < 6 else rest) + k * 128, 128)
        copies.append(
            pltpu.make_async_copy(held.at[k * 128 : (k + 1) * 128], grad.at[pl.ds(row, 128)], sems.at[k])
        )
        copies[-1].start()
    return copies


def own_kernel(own, grad, held, sems):
    for copy in unpack_half(lax.axis_index("core"), own, held, grad, sems):
        copy.wait()


def other_kernel(own, other, grad_in, grad, bias, held, line, sems):
    core = lax.axis_index("core")
    ch = held.shape[1]
    rows = slice(9 * ch, 9 * ch + 8)
    first = jnp.where(core == 0, own[rows].astype(F32), other[rows].astype(F32))
    line[:, 0:128] = first[0:1] + first[2:3]
    line[:, 128:] = first[1:2] + first[3:4]
    copy = pltpu.make_async_copy(line, bias, sems.at[9])
    copy.start()
    for other_copy in unpack_half(1 - core, other, held, grad, sems):
        other_copy.wait()
    copy.wait()


def unpack(own, other, ch):
    grad = jax.ShapeDtypeStruct((9 * ch, ch), F32)
    held = pltpu.VMEM((9 * ch // 2, ch), F32)
    outside = [pl.BlockSpec(memory_space=pl.ANY)]
    part = pl.pallas_call(
        own_kernel,
        out_shape=grad,
        in_specs=vmem(1),
        out_specs=outside[0],
        scratch_shapes=[held, pltpu.SemaphoreType.DMA((9,))],
        compiler_params=params(),
        cost_estimate=pl.CostEstimate(flops=10_000_000, bytes_accessed=3_000_000, transcendentals=0),
        name="unpack_own",
    )(own)
    return pl.pallas_call(
        other_kernel,
        out_shape=(grad, jax.ShapeDtypeStruct((1, ch), F32)),
        in_specs=vmem(2) + outside,
        out_specs=tuple(outside * 2),
        scratch_shapes=[held, pltpu.VMEM((1, ch), F32), pltpu.SemaphoreType.DMA((10,))],
        input_output_aliases={2: 0},
        compiler_params=params(),
        name="unpack_other",
    )(own, other, part)


def shards(row_count, col_count, space, group, frames, offsets, weight, bias, cotangent):
    rows, cols, ch = frames.shape[2:]
    offs = offsets.reshape(-1, 2)
    *sent, kept = row_pieces(frames[0])
    got = swap(sent, "row", row_count)
    bt, b = band(cotangent[0])
    second, first, center, one = col_pieces(offs, kept, got)
    got = swap((first, second), space, col_count)
    taps, bias = weight.reshape(3, 3 * ch, ch), bias.reshape(1, ch)
    xc1, acc1 = convolve_one(one, taps, bias)
    count = int(np.prod([lax.axis_size(a) for a in group]))
    depth = lax.axis_size("zh")
    half = 9 * ch
    size = (half + 8 + 8 * count - 1) // (8 * count) * 8
    sent, tail, f1, f2, *rest = main(
        offs, center, xc1, acc1, got, taps, bias, bt, b, row_count, col_count, size * count
    )
    cores = [(0, 1), (1, 0)]
    got = lax.ppermute(sent, "core", cores)
    kept = keep_half(tail, *rest, size * count)
    parts = merge(kept, got, half)
    parts = lax.all_to_all(parts.reshape(count, size, 128), group, 0, 0, tiled=True)
    parts = sum_and_copy(parts, depth, half, tail)
    corr, token = correlate(f1, f2, parts)
    parts = lax.all_to_all(parts, "zh", 0, 0, tiled=True)
    parts = sum_and_copy(parts, count, half, token)
    parts = lax.all_to_all(parts, group, 0, 0, tiled=True)
    parts = parts.reshape(count * size, 128)
    grad_w, grad_b = unpack(parts, lax.ppermute(parts, "core", cores), ch)
    corr = jnp.transpose(corr.reshape(1, rows, cols, WIN * WIN), (0, 3, 1, 2))
    return corr, grad_w.reshape(3, 3, ch, ch), grad_b.reshape(ch)


def solution(mesh):
    row_count, col_count, pair_count = (mesh.shape[a] for a in ("row", "col", "pair"))
    high = 2 if col_count == 16 else 1
    near = 2 if col_count // high >= 4 else 1
    fine = Mesh(
        mesh.devices.reshape(row_count, high, col_count // high // near, near, pair_count // 2, 2),
        ("row", "high", "zh", "zl", "low", "core"),
    )
    col, pair = SPACE, ("low", "core")
    return jax.shard_map(
        functools.partial(shards, row_count, col_count, col, GROUP_AXES),
        mesh=fine,
        in_specs=(
            P(pair, None, "row", col, None),
            P(pair, None, None, None),
            P(),
            P(),
            P(pair, None, "row", col),
        ),
        out_specs=(P(pair, None, "row", col), P(), P()),
        check_vma=False,
    )
```

```python
import functools

import jax
import jax.numpy as jnp
import numpy as np
from jax import lax
from jax.experimental import pallas as pl
from jax.experimental.pallas import tpu as pltpu
from jax.sharding import Mesh
from jax.sharding import PartitionSpec as P

BLK = 32
RAD = 4
MAXOFF = 8
WIN = 2 * RAD + 1
HALO = MAXOFF + RAD + 1
PITCH = 40
WROWS = 24
GROUP = 4
GROWS = GROUP + WIN - 1
BF = jnp.bfloat16
F32 = jnp.float32


def vmem(n):
    return [pl.BlockSpec(memory_space=pltpu.VMEM)] * n


def params(mib=16):
    return pltpu.CompilerParams(vmem_limit_bytes=mib * 1024 * 1024)


def smem(n):
    return [pl.BlockSpec(memory_space=pltpu.SMEM)] * n


def even(index):
    return lax.rem(index, 2) == 0


def place(axes):
    index = 0
    for axis in axes:
        index = index * lax.axis_size(axis) + lax.axis_index(axis)
    return index


SPACE = ("high", "zh", "zl")
GROUP_AXES = ("row", "high", "zl", "low")


def rows_kernel(frames, first, second, kept):
    rows = frames.shape[1]
    below = even(lax.axis_index("row"))
    for ref, low in ((first, below), (second, jnp.logical_not(below))):
        ref[0:HALO] = frames[1, pl.ds(jnp.where(low, rows - HALO, 0), HALO)]
        ref[HALO] = frames[0, jnp.where(low, rows - 1, 0)]
    kept[...] = frames[...]


def row_pieces(frames):
    cols, ch = frames.shape[2:]
    piece = jax.ShapeDtypeStruct((HALO + 1, cols, ch), BF)
    return pl.pallas_call(
        rows_kernel,
        out_shape=(piece, piece, jax.ShapeDtypeStruct(frames.shape, BF)),
        in_specs=vmem(1),
        out_specs=tuple(vmem(3)),
        compiler_params=params(),
        name="row_pieces",
    )(frames)


def cols_kernel(offs, frames, got_first, got_second, second, first, center, one, ext):
    rows, cols, ch = frames.shape[1:]
    row, column = lax.axis_index("row"), place(SPACE)
    below = even(row)
    count = int(np.prod([lax.axis_size(a) for a in SPACE]))
    base = row * rows // BLK * count
    ext[HALO : HALO + rows] = frames[1]
    one[1 : rows + 1] = frames[0]
    for ref, low in ((got_first, below), (got_second, jnp.logical_not(below))):
        ext[pl.ds(jnp.where(low, HALO + rows, 0), HALO)] = ref[0:HALO]
        one[jnp.where(low, rows + 1, 0)] = ref[HALO]

    def down(index):
        values = offs[...].astype(F32)
        here = lax.broadcasted_iota(jnp.int32, values.shape, 0) == index
        here = here & (lax.broadcasted_iota(jnp.int32, values.shape, 1) == 0)
        return jnp.sum(jnp.where(here, values, 0.0)).astype(jnp.int32)

    center[...] = ext[pl.ds(down(base + column) + MAXOFF, WROWS + 2)]
    right = even(column)
    col = lax.broadcasted_iota(jnp.int32, (rows + 2, 16, ch), 1)
    for ref, side in ((first, right), (second, jnp.logical_not(right))):
        other = jnp.clip(jnp.where(side, column + 1, column - 1), 0, count - 1)
        start = down(base + other) + MAXOFF
        at = pl.multiple_of(jnp.where(side, cols - 16, 0), 16)
        ref[...] = ext[pl.ds(start, WROWS + 2), pl.ds(at, 16)]
        border = one[:, pl.ds(at, 16)].astype(F32)
        border = jnp.where(side, border[:, 15:16], border[:, 0:1])
        spare = jnp.where(side, 0, 15)
        ref[0 : rows + 2] = jnp.where(col == spare, border, ref[0 : rows + 2].astype(F32)).astype(BF)


def col_pieces(offs, frames, got):
    rows, cols, ch = frames.shape[1:]
    piece = jax.ShapeDtypeStruct((WROWS + 2, 16, ch), BF)
    return pl.pallas_call(
        cols_kernel,
        out_shape=(
            piece,
            piece,
            jax.ShapeDtypeStruct((WROWS + 2, cols, ch), BF),
            jax.ShapeDtypeStruct((rows + 2, cols, ch), BF),
        ),
        in_specs=vmem(4),
        out_specs=tuple(vmem(4)),
        scratch_shapes=[
            pltpu.VMEM((rows + 2 * HALO, cols, ch), BF),
        ],
        compiler_params=params(),
        name="col_pieces",
    )(offs, frames, *got)


def swap(pieces, axes, count):
    got = []
    for piece, start in ((pieces[1], 1), (pieces[0], 0)):
        pairs = []
        for i in range(start, count - 1, 2):
            pairs += [(i, i + 1), (i + 1, i)]
        got.append(lax.ppermute(piece, axes, pairs))
    return got[::-1]


def band_kernel(cot, bt, b, lines):
    count, rows, cols = cot.shape
    lanes = GROUP * BLK

    def iota(shape, axis):
        return lax.broadcasted_iota(jnp.int32, shape, axis)

    copy = (iota((cols, lanes), 1) % cols == iota((cols, lanes), 0)).astype(F32).astype(BF)
    wide = jnp.dot(cot[...].reshape(count * rows, cols), copy, preferred_element_type=F32)
    shape = (WIN * 16, count * rows)
    q, d = iota(shape, 0), iota(shape, 1) // rows
    pickd = ((q // 16 * WIN + q % 16 == d) & (q % 16 < WIN)).astype(F32).astype(BF)
    line = iota((count * rows, lanes), 0) % rows
    want = iota((count * rows, lanes), 1) // cols
    gap = iota((PITCH, lanes), 0) - iota((PITCH, lanes), 1) % BLK
    own = iota((16, lanes), 1) // BLK
    for g in range(bt.shape[0]):
        mine = jnp.where(line == want + g * GROUP, wide, 0.0).astype(BF)
        lines[...] = jnp.dot(pickd, mine, preferred_element_type=F32)
        for r in range(GROWS):
            pick = jnp.zeros((16, lanes), F32)
            for yy in range(GROUP):
                a = r - yy
                if 0 <= a < WIN:
                    pick = jnp.where(own == yy, lines[a * 16 : (a + 1) * 16], pick)
            block = jnp.zeros((PITCH, lanes), F32)
            for k in range(WIN):
                block = jnp.where(gap == k, pick[k : k + 1], block)
            bt[g, r * PITCH : (r + 1) * PITCH] = block.astype(BF)
        b[g] = bt[g].astype(F32).T.astype(BF)


def band(cot):
    groups = cot.shape[1] // GROUP
    return pl.pallas_call(
        band_kernel,
        out_shape=(
            jax.ShapeDtypeStruct((groups, GROWS * PITCH, GROUP * BLK), BF),
            jax.ShapeDtypeStruct((groups, GROUP * BLK, GROWS * PITCH), BF),
        ),
        in_specs=vmem(1),
        out_specs=tuple(vmem(2)),
        scratch_shapes=[pltpu.VMEM((WIN * 16, GROUP * BLK), F32)],
        compiler_params=params(),
        cost_estimate=pl.CostEstimate(flops=2_000_000_000, bytes_accessed=1_000_000, transcendentals=0),
        name="band",
    )(cot)


def one_kernel(one, weight, bias, xc1, acc1, ext):
    rows, cols, ch = one.shape[0] - 2, one.shape[1], one.shape[2]
    ext[:, 0:8] = jnp.zeros((rows + 2, 8, ch), F32)
    ext[:, 8 + cols :] = jnp.zeros((rows + 2, 8, ch), F32)
    ext[:, 8 : 8 + cols] = one[...].astype(F32)
    for j in range(3):
        xc1[:, :, j * ch : (j + 1) * ch] = ext[:, 7 + j : 7 + j + cols].astype(BF)
    step = 8

    def conv(n, carry):
        acc = jnp.zeros((step * cols, ch), F32) + bias[...]
        for i in range(3):
            x = xc1[pl.ds(n * step + i, step)].reshape(step * cols, 3 * ch)
            acc = acc + jnp.dot(x, weight[i], preferred_element_type=F32)
        acc1[pl.ds(n * step, step)] = acc.reshape(step, cols, ch)
        return carry

    lax.fori_loop(0, rows // step, conv, 0)


def convolve_one(one, weight, bias):
    rows, cols, ch = one.shape[0] - 2, one.shape[1], one.shape[2]
    return pl.pallas_call(
        one_kernel,
        out_shape=(
            jax.ShapeDtypeStruct((rows + 2, cols, 3 * ch), BF),
            jax.ShapeDtypeStruct((rows, cols, ch), F32),
        ),
        in_specs=vmem(3),
        out_specs=tuple(vmem(2)),
        scratch_shapes=[pltpu.VMEM((rows + 2, cols + 16, ch), F32)],
        compiler_params=params(),
        cost_estimate=pl.CostEstimate(flops=1_500_000_000, bytes_accessed=1_000_000, transcendentals=0),
        name="one",
    )(one, weight, bias)


def half_grad(which, d2t, d1t, xc2, xc1, out):
    ch, rows, cols = d2t.shape[0], xc1.shape[0] - 2, xc1.shape[1]
    for i, lanes, base in (
        (2 * which, pl.ds(0, 3 * ch), 0),
        (1, pl.ds(pl.multiple_of(which * (3 * ch // 2), 128), 3 * ch // 2), 6),
    ):
        width = lanes.size
        x2 = xc2[pl.ds(i, WROWS), :, lanes].reshape(WROWS * PITCH, width)
        x1 = xc1[pl.ds(i, rows), :, lanes].reshape(rows * cols, width)
        acc = jnp.dot(d2t[...], x2, preferred_element_type=F32)
        acc = acc + jnp.dot(d1t[...], x1, preferred_element_type=F32)
        for k in range(width // 128):
            out[(base + k) * ch : (base + k + 1) * ch] = acc[:, k * 128 : (k + 1) * 128].astype(out.dtype)


def main_kernel(
    row_count, col_count,
    offs_in, center, xc1_in, acc1, got_second, got_first, weight, bias, bt, b,
    send, tail, f1, f2, xc2, xc1, d2t, d1t,
    ext2, pre2, pre1, gwin, d1, offs, sem,
):
    rows, cols, ch = acc1.shape
    fetch = pltpu.make_async_copy(offs_in, offs, sem)
    fetch.start()
    height, width = row_count * rows, col_count * cols
    inv_root = ch ** (-0.5)
    row, column = lax.axis_index("row"), place(SPACE)
    right = even(column)
    ext2[:, 16 : 16 + cols] = center[...].astype(F32)
    v_first, v_second = got_first[...].astype(F32), got_second[...].astype(F32)
    for value, side in ((v_first, right), (v_second, jnp.logical_not(right))):
        ext2[:, pl.ds(pl.multiple_of(jnp.where(side, 16 + cols, 0), 16), 16)] = value
    ext2[:, 32 + cols :] = jnp.zeros((WROWS + 2, ext2.shape[1] - 32 - cols, ch), F32)
    xc1[...] = xc1_in[...]
    pre1[...] = acc1[...]
    col = lax.broadcasted_iota(jnp.int32, (rows + 2, 8, ch), 1)
    n1 = rows + 2
    for j, spot, at, value in (
        (0, 0, 0, jnp.where(right, v_second[0:n1, 0:8], v_first[0:n1, 0:8])),
        (2, 7, cols - 8, jnp.where(right, v_first[0:n1, 8:16], v_second[0:n1, 8:16])),
    ):
        value = jnp.where(col == spot, value, 0.0)
        lanes = slice(j * ch, (j + 1) * ch)
        xc1[:, at : at + 8, lanes] = (xc1_in[:, at : at + 8, lanes].astype(F32) + value).astype(BF)
        value = value.astype(BF)
        acc = jnp.zeros((rows * 8, ch), F32)
        for i in range(3):
            x = value[i : i + rows].reshape(rows * 8, ch)
            acc = acc + jnp.dot(x, weight[i, j * ch : (j + 1) * ch], preferred_element_type=F32)
        pre1[:, at : at + 8] = acc1[:, at : at + 8] + acc.reshape(rows, 8, ch)
    f1[...] = jnp.maximum(pre1[...], 0.0).reshape(rows * cols, ch).astype(BF)

    fetch.wait()
    block = row * rows // BLK * col_count + column
    oy, ox = offs[block, 0], offs[block, 1]
    c0, gy0, gx0 = ox + 16 - RAD - 1, row * rows + oy - RAD, column * cols + ox - RAD
    span = PITCH + 16
    base = pl.multiple_of((c0 // 8) * 8, 8)
    turn = span - c0 % 8

    def gather(r, carry):
        row = pltpu.roll(ext2[r, pl.ds(base, span), :], turn, 0)
        for j in range(3):
            xc2[r, :, j * ch : (j + 1) * ch] = row[j : j + PITCH].astype(BF)
        return carry


    shift = bias[...]
    step = 12

    def conv_two(n, carry):
        acc = jnp.zeros((step * PITCH, ch), F32)
        for i in range(3):
            x = xc2[pl.ds(n * step + i, step)].reshape(step * PITCH, 3 * ch)
            acc = acc + jnp.dot(x, weight[i], preferred_element_type=F32)
        acc = (acc + shift).reshape(step, PITCH, ch)
        y = lax.broadcasted_iota(jnp.int32, acc.shape, 0) + n * step + gy0
        x = lax.broadcasted_iota(jnp.int32, acc.shape, 1) + gx0
        ok = (y >= 0) & (y < height) & (x >= 0) & (x < width)
        acc = jnp.maximum(jnp.where(ok, acc, 0.0), 0.0).reshape(step * PITCH, ch)
        pre2[pl.ds(n * step * PITCH, step * PITCH)] = acc
        f2[pl.ds(n * step * PITCH, step * PITCH)] = acc.astype(BF)
        return carry

    done = 0
    for n in range(WROWS // step):
        for r in range(done, (n + 1) * step + 2):
            gather(r, 0)
        done = (n + 1) * step + 2
        conv_two(n, 0)

    gwin[...] = jnp.zeros(gwin.shape, F32)
    lanes = GROUP * cols
    bsum = jnp.zeros((1, ch), F32)
    for g in range(rows // GROUP):
        at = slice(g * GROUP * PITCH, (g * GROUP + GROWS) * PITCH)
        px = slice(g * lanes, (g + 1) * lanes)
        gwin[at] += jnp.dot(bt[g], f1[px], preferred_element_type=F32)
        delta = jnp.dot(b[g], f2[at], preferred_element_type=F32) * inv_root
        mine = pre1[g * GROUP : (g + 1) * GROUP].reshape(lanes, ch)
        delta = jnp.where(mine > 0, delta, 0.0).astype(BF)
        d1[px] = delta
        bsum = bsum + jnp.sum(delta.astype(F32), axis=0, keepdims=True)
    delta = jnp.where(pre2[...] > 0, gwin[...] * inv_root, 0.0)
    bsum = bsum + jnp.sum(delta, axis=0, keepdims=True)
    d2t[...] = delta.astype(BF).T
    d1t[...] = d1[...].T
    half_grad(1 - lax.axis_index("core"), d2t, d1t, xc2, xc1, send)
    tail[...] = bias_tile(bsum[:, 0:128], bsum[:, 128:])
    send[9 * ch : 9 * ch + 8] = tail[...].astype(BF)
    send[9 * ch + 8 :] = jnp.zeros((send.shape[0] - 9 * ch - 8, 128), BF)


def bias_tile(low, high):
    row = lax.broadcasted_iota(jnp.int32, (8, 128), 0)
    out = jnp.zeros((8, 128), F32)
    for n, value in enumerate((low, high)):
        top = value.astype(BF).astype(F32)
        out = jnp.where(row == n, top, jnp.where(row == n + 2, value - top, out))
    return out


def bias_again(value):
    return bias_tile(value[0:1] + value[2:3], value[1:2] + value[3:4])


def main(offs, center, xc1, acc1, got, weight, bias, bt, b, row_count, col_count, flat):
    rows, cols, ch = acc1.shape
    wpx, n2 = WROWS * PITCH, WROWS + 2
    return pl.pallas_call(
        functools.partial(main_kernel, row_count, col_count),
        out_shape=(
            jax.ShapeDtypeStruct((flat, 128), BF),
            jax.ShapeDtypeStruct((8, 128), F32),
            jax.ShapeDtypeStruct((rows * cols, ch), BF),
            jax.ShapeDtypeStruct((wpx, ch), BF),
            jax.ShapeDtypeStruct((n2, PITCH, 3 * ch), BF),
            jax.ShapeDtypeStruct(xc1.shape, BF),
            jax.ShapeDtypeStruct((ch, wpx), BF),
            jax.ShapeDtypeStruct((ch, rows * cols), BF),
        ),
        in_specs=[pl.BlockSpec(memory_space=pl.ANY)] + vmem(9),
        out_specs=tuple(vmem(8)),
        scratch_shapes=[
            pltpu.VMEM((n2, cols + 48, ch), F32),
            pltpu.VMEM((wpx, ch), F32),
            pltpu.VMEM((rows, cols, ch), F32),
            pltpu.VMEM((wpx, ch), F32),
            pltpu.VMEM((rows * cols, ch), BF),
            pltpu.SMEM(offs.shape, jnp.int32),
            pltpu.SemaphoreType.DMA(()),
        ],
        compiler_params=params(20),
        cost_estimate=pl.CostEstimate(flops=5_000_000_000, bytes_accessed=8_000_000, transcendentals=0),
        name="main",
    )(offs, center, xc1, acc1, got[1], got[0], weight, bias, bt, b)


def keep_kernel(tail, xc2, xc1, d2t, d1t, keep):
    ch = d2t.shape[0]
    half_grad(lax.axis_index("core"), d2t, d1t, xc2, xc1, keep)
    keep[9 * ch : 9 * ch + 8] = tail[...]
    keep[9 * ch + 8 :] = jnp.zeros((keep.shape[0] - 9 * ch - 8, 128), F32)


def keep_half(tail, xc2, xc1, d2t, d1t, flat):
    return pl.pallas_call(
        keep_kernel,
        out_shape=jax.ShapeDtypeStruct((flat, 128), F32),
        in_specs=vmem(5),
        out_specs=vmem(1)[0],
        compiler_params=params(),
        cost_estimate=pl.CostEstimate(flops=1_000_000_000, bytes_accessed=1_000_000, transcendentals=0),
        name="keep",
    )(tail, xc2, xc1, d2t, d1t)


def corr_kernel(f1, f2, before, out, token, lines):
    lanes = GROUP * BLK
    inv_root = f1.shape[1] ** (-0.5)
    lane = lax.broadcasted_iota(jnp.int32, (PITCH, lanes), 1)
    gap = lax.broadcasted_iota(jnp.int32, (PITCH, lanes), 0) - lane % BLK
    own = lane // BLK
    token[...] = jnp.zeros(token.shape, F32)
    lines[WIN * WIN - 1 :] = jnp.zeros((128 - WIN * WIN + 1, lanes), F32)
    for g in range(f1.shape[0] // lanes):
        at = slice(g * GROUP * PITCH, (g * GROUP + GROWS) * PITCH)
        scores = lax.dot_general(
            f2[at], f1[g * lanes : (g + 1) * lanes], (((1,), (1,)), ((), ())),
            preferred_element_type=F32,
        )
        for a in range(WIN):
            pick = scores[a * PITCH : (a + 1) * PITCH]
            for yy in range(1, GROUP):
                pick = jnp.where(own == yy, scores[(a + yy) * PITCH : (a + yy + 1) * PITCH], pick)
            for d in range(WIN):
                line = jnp.sum(jnp.where(gap == d, pick, 0.0), axis=0, keepdims=True) * inv_root
                lines[a * WIN + d : a * WIN + d + 1] = line
        out[g * lanes : (g + 1) * lanes] = lines[...].T[:, : WIN * WIN].astype(BF)


def correlate(f1, f2, before):
    return pl.pallas_call(
        corr_kernel,
        out_shape=(jax.ShapeDtypeStruct((f1.shape[0], WIN * WIN), BF), jax.ShapeDtypeStruct((8, 128), F32)),
        in_specs=vmem(2) + [pl.BlockSpec(memory_space=pl.ANY)],
        out_specs=tuple(vmem(2)),
        scratch_shapes=[pltpu.VMEM((128, GROUP * BLK), F32)],
        compiler_params=params(),
        cost_estimate=pl.CostEstimate(flops=300_000_000, bytes_accessed=1_000_000, transcendentals=0),
        name="corr",
    )(f1, f2, before)


def sum_kernel(rows, parts, after, out):
    size = parts.shape[1]
    for s in range(0, size, 8):
        value = parts[0, s : s + 8].astype(F32)
        for n in range(1, parts.shape[0]):
            value = value + parts[n, s : s + 8].astype(F32)
        if s == rows % size:
            value = jnp.where(place(GROUP_AXES) == rows // size, bias_again(value), value)
        value = value.astype(BF)
        for k in range(out.shape[0]):
            out[k, s : s + 8] = value


def sum_and_copy(parts, copies, rows, after):
    return pl.pallas_call(
        functools.partial(sum_kernel, rows),
        out_shape=jax.ShapeDtypeStruct((copies,) + parts.shape[1:], BF),
        in_specs=vmem(2),
        out_specs=vmem(1)[0],
        compiler_params=params(),
        name="sum",
    )(parts, after)


def copies_kernel(rows, own, *refs):
    *got, after, out = refs
    size = own.shape[0]
    value = own[...].astype(F32)
    if len(got) == 1:
        value = value + got[0][...].astype(F32)
    else:
        value = (value + got[1][...].astype(F32)) + (got[0][...].astype(F32) + got[2][...].astype(F32))
    at = rows % size
    tail = value[at : at + 8]
    tail = jnp.where(place(GROUP_AXES) == rows // size, bias_again(tail), tail)
    value = jnp.concatenate([value[0:at], tail, value[at + 8 :]], axis=0).astype(BF)
    for k in range(out.shape[0]):
        out[k] = value


def add_and_copy(own, got, copies, rows, after):
    return pl.pallas_call(
        functools.partial(copies_kernel, rows),
        out_shape=jax.ShapeDtypeStruct((copies,) + own.shape, BF),
        in_specs=vmem(2 + len(got)),
        out_specs=vmem(1)[0],
        compiler_params=params(),
        name="copies",
    )(own, *got, after)


def merge_kernel(rows, kept, got, out):
    out[...] = (kept[...] + got[...].astype(F32)).astype(BF)
    tail = kept[rows : rows + 8] + got[rows : rows + 8].astype(F32)
    out[rows : rows + 8] = bias_again(tail).astype(BF)


def merge(kept, got, rows):
    return pl.pallas_call(
        functools.partial(merge_kernel, rows),
        out_shape=jax.ShapeDtypeStruct(got.shape, BF),
        in_specs=vmem(2),
        out_specs=vmem(1)[0],
        compiler_params=params(),
        name="merge",
    )(kept, got)


def unpack_half(which, part, held, grad, sems):
    ch = held.shape[1]
    first, rest = which * 6 * ch, 3 * ch + which * (3 * ch // 2) - 6 * 128
    copies = []
    for k in range(9):
        held[k * 128 : (k + 1) * 128] = part[k * ch : (k + 1) * ch].T.astype(F32)
        row = pl.multiple_of((first if k < 6 else rest) + k * 128, 128)
        copies.append(
            pltpu.make_async_copy(held.at[k * 128 : (k + 1) * 128], grad.at[pl.ds(row, 128)], sems.at[k])
        )
        copies[-1].start()
    return copies


def own_kernel(own, grad, held, sems):
    for copy in unpack_half(lax.axis_index("core"), own, held, grad, sems):
        copy.wait()


def other_kernel(own, other, grad_in, grad, bias, held, line, sems):
    core = lax.axis_index("core")
    ch = held.shape[1]
    rows = slice(9 * ch, 9 * ch + 8)
    first = jnp.where(core == 0, own[rows].astype(F32), other[rows].astype(F32))
    line[:, 0:128] = first[0:1] + first[2:3]
    line[:, 128:] = first[1:2] + first[3:4]
    copy = pltpu.make_async_copy(line, bias, sems.at[9])
    copy.start()
    for other_copy in unpack_half(1 - core, other, held, grad, sems):
        other_copy.wait()
    copy.wait()


def unpack(own, other, ch):
    grad = jax.ShapeDtypeStruct((9 * ch, ch), F32)
    held = pltpu.VMEM((9 * ch // 2, ch), F32)
    outside = [pl.BlockSpec(memory_space=pl.ANY)]
    part = pl.pallas_call(
        own_kernel,
        out_shape=grad,
        in_specs=vmem(1),
        out_specs=outside[0],
        scratch_shapes=[held, pltpu.SemaphoreType.DMA((9,))],
        compiler_params=params(),
        cost_estimate=pl.CostEstimate(flops=10_000_000, bytes_accessed=3_000_000, transcendentals=0),
        name="unpack_own",
    )(own)
    return pl.pallas_call(
        other_kernel,
        out_shape=(grad, jax.ShapeDtypeStruct((1, ch), F32)),
        in_specs=vmem(2) + outside,
        out_specs=tuple(outside * 2),
        scratch_shapes=[held, pltpu.VMEM((1, ch), F32), pltpu.SemaphoreType.DMA((10,))],
        input_output_aliases={2: 0},
        compiler_params=params(),
        name="unpack_other",
    )(own, other, part)


def shards(row_count, col_count, space, group, frames, offsets, weight, bias, cotangent):
    rows, cols, ch = frames.shape[2:]
    offs = offsets.reshape(-1, 2)
    *sent, kept = row_pieces(frames[0])
    got = swap(sent, "row", row_count)
    bt, b = band(cotangent[0])
    second, first, center, one = col_pieces(offs, kept, got)
    got = swap((first, second), space, col_count)
    taps, bias = weight.reshape(3, 3 * ch, ch), bias.reshape(1, ch)
    xc1, acc1 = convolve_one(one, taps, bias)
    count = int(np.prod([lax.axis_size(a) for a in group]))
    depth = lax.axis_size("zh")
    half = 9 * ch
    size = (half + 8 + 8 * count - 1) // (8 * count) * 8
    sent, tail, f1, f2, *rest = main(
        offs, center, xc1, acc1, got, taps, bias, bt, b, row_count, col_count, size * count
    )
    cores = [(0, 1), (1, 0)]
    got = lax.ppermute(sent, "core", cores)
    kept = keep_half(tail, *rest, size * count)
    parts = merge(kept, got, half)
    parts = lax.all_to_all(parts.reshape(count, size, 128), group, 0, 0, tiled=True)
    parts = sum_and_copy(parts, 1, half, tail).reshape(size, 128)
    corr, token = correlate(f1, f2, parts)
    hops = {2: (1,), 4: (2, 1, 3)}[depth]
    got = {h: lax.ppermute(parts, "zh", [(i, (i + h) % depth) for i in range(depth)]) for h in hops}
    parts = add_and_copy(parts, [got[h] for h in sorted(hops)], count, half, token)
    parts = lax.all_to_all(parts, group, 0, 0, tiled=True)
    parts = parts.reshape(count * size, 128)
    grad_w, grad_b = unpack(parts, lax.ppermute(parts, "core", cores), ch)
    corr = jnp.transpose(corr.reshape(1, rows, cols, WIN * WIN), (0, 3, 1, 2))
    return corr, grad_w.reshape(3, 3, ch, ch), grad_b.reshape(ch)


def solution(mesh):
    row_count, col_count, pair_count = (mesh.shape[a] for a in ("row", "col", "pair"))
    high = 2 if col_count == 16 else 1
    near = 2 if col_count // high >= 4 else 1
    fine = Mesh(
        mesh.devices.reshape(row_count, high, col_count // high // near, near, pair_count // 2, 2),
        ("row", "high", "zh", "zl", "low", "core"),
    )
    col, pair = SPACE, ("low", "core")
    return jax.shard_map(
        functools.partial(shards, row_count, col_count, col, GROUP_AXES),
        mesh=fine,
        in_specs=(
            P(pair, None, "row", col, None),
            P(pair, None, None, None),
            P(),
            P(),
            P(pair, None, "row", col),
        ),
        out_specs=(P(pair, None, "row", col), P(), P()),
        check_vma=False,
    )
```

```python
import functools

import jax
import jax.numpy as jnp
import numpy as np
from jax import lax
from jax.experimental import pallas as pl
from jax.experimental.pallas import tpu as pltpu
from jax.sharding import Mesh
from jax.sharding import PartitionSpec as P

BLK = 32
RAD = 4
MAXOFF = 8
WIN = 2 * RAD + 1
HALO = MAXOFF + RAD + 1
PITCH = 40
WROWS = 24
GROUP = 4
GROWS = GROUP + WIN - 1
BF = jnp.bfloat16
F32 = jnp.float32


def vmem(n):
    return [pl.BlockSpec(memory_space=pltpu.VMEM)] * n


def params(mib=16):
    return pltpu.CompilerParams(vmem_limit_bytes=mib * 1024 * 1024)


def smem(n):
    return [pl.BlockSpec(memory_space=pltpu.SMEM)] * n


def even(index):
    return lax.rem(index, 2) == 0


def place(axes):
    index = 0
    for axis in axes:
        index = index * lax.axis_size(axis) + lax.axis_index(axis)
    return index


SPACE = ("high", "zh", "zl")
GROUP_AXES = ("row", "high", "zl", "low")


def rows_kernel(frames, first, second, kept):
    rows = frames.shape[1]
    below = even(lax.axis_index("row"))
    for ref, low in ((first, below), (second, jnp.logical_not(below))):
        ref[0:HALO] = frames[1, pl.ds(jnp.where(low, rows - HALO, 0), HALO)]
        ref[HALO] = frames[0, jnp.where(low, rows - 1, 0)]
    kept[...] = frames[...]


def row_pieces(frames):
    cols, ch = frames.shape[2:]
    piece = jax.ShapeDtypeStruct((HALO + 1, cols, ch), BF)
    return pl.pallas_call(
        rows_kernel,
        out_shape=(piece, piece, jax.ShapeDtypeStruct(frames.shape, BF)),
        in_specs=vmem(1),
        out_specs=tuple(vmem(3)),
        compiler_params=params(),
        name="row_pieces",
    )(frames)


def cols_kernel(offs, frames, got_first, got_second, second, first, center, one, ext):
    rows, cols, ch = frames.shape[1:]
    row, column = lax.axis_index("row"), place(SPACE)
    below = even(row)
    count = int(np.prod([lax.axis_size(a) for a in SPACE]))
    base = row * rows // BLK * count
    ext[HALO : HALO + rows] = frames[1]
    one[1 : rows + 1] = frames[0]
    for ref, low in ((got_first, below), (got_second, jnp.logical_not(below))):
        ext[pl.ds(jnp.where(low, HALO + rows, 0), HALO)] = ref[0:HALO]
        one[jnp.where(low, rows + 1, 0)] = ref[HALO]

    def down(index):
        values = offs[...].astype(F32)
        here = lax.broadcasted_iota(jnp.int32, values.shape, 0) == index
        here = here & (lax.broadcasted_iota(jnp.int32, values.shape, 1) == 0)
        return jnp.sum(jnp.where(here, values, 0.0)).astype(jnp.int32)

    center[...] = ext[pl.ds(down(base + column) + MAXOFF, WROWS + 2)]
    right = even(column)
    col = lax.broadcasted_iota(jnp.int32, (rows + 2, 16, ch), 1)
    for ref, side in ((first, right), (second, jnp.logical_not(right))):
        other = jnp.clip(jnp.where(side, column + 1, column - 1), 0, count - 1)
        start = down(base + other) + MAXOFF
        at = pl.multiple_of(jnp.where(side, cols - 16, 0), 16)
        ref[...] = ext[pl.ds(start, WROWS + 2), pl.ds(at, 16)]
        border = one[:, pl.ds(at, 16)].astype(F32)
        border = jnp.where(side, border[:, 15:16], border[:, 0:1])
        spare = jnp.where(side, 0, 15)
        ref[0 : rows + 2] = jnp.where(col == spare, border, ref[0 : rows + 2].astype(F32)).astype(BF)


def col_pieces(offs, frames, got):
    rows, cols, ch = frames.shape[1:]
    piece = jax.ShapeDtypeStruct((WROWS + 2, 16, ch), BF)
    return pl.pallas_call(
        cols_kernel,
        out_shape=(
            piece,
            piece,
            jax.ShapeDtypeStruct((WROWS + 2, cols, ch), BF),
            jax.ShapeDtypeStruct((rows + 2, cols, ch), BF),
        ),
        in_specs=vmem(4),
        out_specs=tuple(vmem(4)),
        scratch_shapes=[
            pltpu.VMEM((rows + 2 * HALO, cols, ch), BF),
        ],
        compiler_params=params(),
        name="col_pieces",
    )(offs, frames, *got)


def swap(pieces, axes, count):
    got = []
    for piece, start in ((pieces[1], 1), (pieces[0], 0)):
        pairs = []
        for i in range(start, count - 1, 2):
            pairs += [(i, i + 1), (i + 1, i)]
        got.append(lax.ppermute(piece, axes, pairs))
    return got[::-1]


def band_kernel(cot, bt, b, lines):
    count, rows, cols = cot.shape
    lanes = GROUP * BLK

    def iota(shape, axis):
        return lax.broadcasted_iota(jnp.int32, shape, axis)

    copy = (iota((cols, lanes), 1) % cols == iota((cols, lanes), 0)).astype(F32).astype(BF)
    wide = jnp.dot(cot[...].reshape(count * rows, cols), copy, preferred_element_type=F32)
    shape = (WIN * 16, count * rows)
    q, d = iota(shape, 0), iota(shape, 1) // rows
    pickd = ((q // 16 * WIN + q % 16 == d) & (q % 16 < WIN)).astype(F32).astype(BF)
    line = iota((count * rows, lanes), 0) % rows
    want = iota((count * rows, lanes), 1) // cols
    gap = iota((PITCH, lanes), 0) - iota((PITCH, lanes), 1) % BLK
    own = iota((16, lanes), 1) // BLK
    for g in range(bt.shape[0]):
        mine = jnp.where(line == want + g * GROUP, wide, 0.0).astype(BF)
        lines[...] = jnp.dot(pickd, mine, preferred_element_type=F32)
        for r in range(GROWS):
            pick = jnp.zeros((16, lanes), F32)
            for yy in range(GROUP):
                a = r - yy
                if 0 <= a < WIN:
                    pick = jnp.where(own == yy, lines[a * 16 : (a + 1) * 16], pick)
            block = jnp.zeros((PITCH, lanes), F32)
            for k in range(WIN):
                block = jnp.where(gap == k, pick[k : k + 1], block)
            bt[g, r * PITCH : (r + 1) * PITCH] = block.astype(BF)
        b[g] = bt[g].astype(F32).T.astype(BF)


def band(cot):
    groups = cot.shape[1] // GROUP
    return pl.pallas_call(
        band_kernel,
        out_shape=(
            jax.ShapeDtypeStruct((groups, GROWS * PITCH, GROUP * BLK), BF),
            jax.ShapeDtypeStruct((groups, GROUP * BLK, GROWS * PITCH), BF),
        ),
        in_specs=vmem(1),
        out_specs=tuple(vmem(2)),
        scratch_shapes=[pltpu.VMEM((WIN * 16, GROUP * BLK), F32)],
        compiler_params=params(),
        cost_estimate=pl.CostEstimate(flops=2_000_000_000, bytes_accessed=1_000_000, transcendentals=0),
        name="band",
    )(cot)


def one_kernel(one, weight, bias, xc1, acc1, ext):
    rows, cols, ch = one.shape[0] - 2, one.shape[1], one.shape[2]
    ext[:, 0:8] = jnp.zeros((rows + 2, 8, ch), F32)
    ext[:, 8 + cols :] = jnp.zeros((rows + 2, 8, ch), F32)
    ext[:, 8 : 8 + cols] = one[...].astype(F32)
    for j in range(3):
        xc1[:, :, j * ch : (j + 1) * ch] = ext[:, 7 + j : 7 + j + cols].astype(BF)
    step = 8

    def conv(n, carry):
        acc = jnp.zeros((step * cols, ch), F32) + bias[...]
        for i in range(3):
            x = xc1[pl.ds(n * step + i, step)].reshape(step * cols, 3 * ch)
            acc = acc + jnp.dot(x, weight[i], preferred_element_type=F32)
        acc1[pl.ds(n * step, step)] = acc.reshape(step, cols, ch)
        return carry

    lax.fori_loop(0, rows // step, conv, 0)


def convolve_one(one, weight, bias):
    rows, cols, ch = one.shape[0] - 2, one.shape[1], one.shape[2]
    return pl.pallas_call(
        one_kernel,
        out_shape=(
            jax.ShapeDtypeStruct((rows + 2, cols, 3 * ch), BF),
            jax.ShapeDtypeStruct((rows, cols, ch), F32),
        ),
        in_specs=vmem(3),
        out_specs=tuple(vmem(2)),
        scratch_shapes=[pltpu.VMEM((rows + 2, cols + 16, ch), F32)],
        compiler_params=params(),
        cost_estimate=pl.CostEstimate(flops=1_500_000_000, bytes_accessed=1_000_000, transcendentals=0),
        name="one",
    )(one, weight, bias)


def half_grad(which, d2t, d1t, xc2, xc1, out):
    ch, rows, cols = d2t.shape[0], xc1.shape[0] - 2, xc1.shape[1]
    for i, lanes, base in (
        (2 * which, pl.ds(0, 3 * ch), 0),
        (1, pl.ds(pl.multiple_of(which * (3 * ch // 2), 128), 3 * ch // 2), 6),
    ):
        width = lanes.size
        x2 = xc2[pl.ds(i, WROWS), :, lanes].reshape(WROWS * PITCH, width)
        x1 = xc1[pl.ds(i, rows), :, lanes].reshape(rows * cols, width)
        acc = jnp.dot(d2t[...], x2, preferred_element_type=F32)
        acc = acc + jnp.dot(d1t[...], x1, preferred_element_type=F32)
        for k in range(width // 128):
            out[(base + k) * ch : (base + k + 1) * ch] = acc[:, k * 128 : (k + 1) * 128].astype(out.dtype)


def main_kernel(
    row_count, col_count,
    offs_in, center, xc1_in, acc1, got_second, got_first, weight, bias, bt, b,
    send, tail, f1, f2, xc2, xc1, d2t, d1t,
    ext2, pre2, pre1, gwin, d1, offs, sem,
):
    rows, cols, ch = acc1.shape
    fetch = pltpu.make_async_copy(offs_in, offs, sem)
    fetch.start()
    height, width = row_count * rows, col_count * cols
    inv_root = ch ** (-0.5)
    row, column = lax.axis_index("row"), place(SPACE)
    right = even(column)
    ext2[:, 16 : 16 + cols] = center[...].astype(F32)
    v_first, v_second = got_first[...].astype(F32), got_second[...].astype(F32)
    for value, side in ((v_first, right), (v_second, jnp.logical_not(right))):
        ext2[:, pl.ds(pl.multiple_of(jnp.where(side, 16 + cols, 0), 16), 16)] = value
    ext2[:, 32 + cols :] = jnp.zeros((WROWS + 2, ext2.shape[1] - 32 - cols, ch), F32)
    xc1[...] = xc1_in[...]
    pre1[...] = acc1[...]
    col = lax.broadcasted_iota(jnp.int32, (rows + 2, 8, ch), 1)
    n1 = rows + 2
    for j, spot, at, value in (
        (0, 0, 0, jnp.where(right, v_second[0:n1, 0:8], v_first[0:n1, 0:8])),
        (2, 7, cols - 8, jnp.where(right, v_first[0:n1, 8:16], v_second[0:n1, 8:16])),
    ):
        value = jnp.where(col == spot, value, 0.0)
        lanes = slice(j * ch, (j + 1) * ch)
        xc1[:, at : at + 8, lanes] = (xc1_in[:, at : at + 8, lanes].astype(F32) + value).astype(BF)
        value = value.astype(BF)
        acc = jnp.zeros((rows * 8, ch), F32)
        for i in range(3):
            x = value[i : i + rows].reshape(rows * 8, ch)
            acc = acc + jnp.dot(x, weight[i, j * ch : (j + 1) * ch], preferred_element_type=F32)
        pre1[:, at : at + 8] = acc1[:, at : at + 8] + acc.reshape(rows, 8, ch)
    f1[...] = jnp.maximum(pre1[...], 0.0).reshape(rows * cols, ch).astype(BF)

    fetch.wait()
    block = row * rows // BLK * col_count + column
    oy, ox = offs[block, 0], offs[block, 1]
    c0, gy0, gx0 = ox + 16 - RAD - 1, row * rows + oy - RAD, column * cols + ox - RAD
    span = PITCH + 16
    base = pl.multiple_of((c0 // 8) * 8, 8)
    turn = span - c0 % 8

    def gather(r, carry):
        row = pltpu.roll(ext2[r, pl.ds(base, span), :], turn, 0)
        for j in range(3):
            xc2[r, :, j * ch : (j + 1) * ch] = row[j : j + PITCH].astype(BF)
        return carry


    shift = bias[...]
    step = 12

    def conv_two(n, carry):
        acc = jnp.zeros((step * PITCH, ch), F32)
        for i in range(3):
            x = xc2[pl.ds(n * step + i, step)].reshape(step * PITCH, 3 * ch)
            acc = acc + jnp.dot(x, weight[i], preferred_element_type=F32)
        acc = (acc + shift).reshape(step, PITCH, ch)
        y = lax.broadcasted_iota(jnp.int32, acc.shape, 0) + n * step + gy0
        x = lax.broadcasted_iota(jnp.int32, acc.shape, 1) + gx0
        ok = (y >= 0) & (y < height) & (x >= 0) & (x < width)
        acc = jnp.maximum(jnp.where(ok, acc, 0.0), 0.0).reshape(step * PITCH, ch)
        pre2[pl.ds(n * step * PITCH, step * PITCH)] = acc
        f2[pl.ds(n * step * PITCH, step * PITCH)] = acc.astype(BF)
        return carry

    done = 0
    for n in range(WROWS // step):
        for r in range(done, (n + 1) * step + 2):
            gather(r, 0)
        done = (n + 1) * step + 2
        conv_two(n, 0)

    gwin[...] = jnp.zeros(gwin.shape, F32)
    lanes = GROUP * cols
    bsum = jnp.zeros((1, ch), F32)
    for g in range(rows // GROUP):
        at = slice(g * GROUP * PITCH, (g * GROUP + GROWS) * PITCH)
        px = slice(g * lanes, (g + 1) * lanes)
        gwin[at] += jnp.dot(bt[g], f1[px], preferred_element_type=F32)
        delta = jnp.dot(b[g], f2[at], preferred_element_type=F32) * inv_root
        mine = pre1[g * GROUP : (g + 1) * GROUP].reshape(lanes, ch)
        delta = jnp.where(mine > 0, delta, 0.0).astype(BF)
        d1[px] = delta
        bsum = bsum + jnp.sum(delta.astype(F32), axis=0, keepdims=True)
    delta = jnp.where(pre2[...] > 0, gwin[...] * inv_root, 0.0)
    bsum = bsum + jnp.sum(delta, axis=0, keepdims=True)
    d2t[...] = delta.astype(BF).T
    d1t[...] = d1[...].T
    half_grad(1 - lax.axis_index("core"), d2t, d1t, xc2, xc1, send)
    tail[...] = bias_tile(bsum[:, 0:128], bsum[:, 128:])
    send[9 * ch : 9 * ch + 8] = tail[...].astype(BF)
    send[9 * ch + 8 :] = jnp.zeros((send.shape[0] - 9 * ch - 8, 128), BF)


def bias_tile(low, high):
    row = lax.broadcasted_iota(jnp.int32, (8, 128), 0)
    out = jnp.zeros((8, 128), F32)
    for n, value in enumerate((low, high)):
        top = value.astype(BF).astype(F32)
        out = jnp.where(row == n, top, jnp.where(row == n + 2, value - top, out))
    return out


def bias_again(value):
    return bias_tile(value[0:1] + value[2:3], value[1:2] + value[3:4])


def main(offs, center, xc1, acc1, got, weight, bias, bt, b, row_count, col_count, flat):
    rows, cols, ch = acc1.shape
    wpx, n2 = WROWS * PITCH, WROWS + 2
    return pl.pallas_call(
        functools.partial(main_kernel, row_count, col_count),
        out_shape=(
            jax.ShapeDtypeStruct((flat, 128), BF),
            jax.ShapeDtypeStruct((8, 128), F32),
            jax.ShapeDtypeStruct((rows * cols, ch), BF),
            jax.ShapeDtypeStruct((wpx, ch), BF),
            jax.ShapeDtypeStruct((n2, PITCH, 3 * ch), BF),
            jax.ShapeDtypeStruct(xc1.shape, BF),
            jax.ShapeDtypeStruct((ch, wpx), BF),
            jax.ShapeDtypeStruct((ch, rows * cols), BF),
        ),
        in_specs=[pl.BlockSpec(memory_space=pl.ANY)] + vmem(9),
        out_specs=tuple(vmem(8)),
        scratch_shapes=[
            pltpu.VMEM((n2, cols + 48, ch), F32),
            pltpu.VMEM((wpx, ch), F32),
            pltpu.VMEM((rows, cols, ch), F32),
            pltpu.VMEM((wpx, ch), F32),
            pltpu.VMEM((rows * cols, ch), BF),
            pltpu.SMEM(offs.shape, jnp.int32),
            pltpu.SemaphoreType.DMA(()),
        ],
        compiler_params=params(20),
        cost_estimate=pl.CostEstimate(flops=5_000_000_000, bytes_accessed=8_000_000, transcendentals=0),
        name="main",
    )(offs, center, xc1, acc1, got[1], got[0], weight, bias, bt, b)


def keep_kernel(tail, xc2, xc1, d2t, d1t, keep):
    ch = d2t.shape[0]
    half_grad(lax.axis_index("core"), d2t, d1t, xc2, xc1, keep)
    keep[9 * ch : 9 * ch + 8] = tail[...]
    keep[9 * ch + 8 :] = jnp.zeros((keep.shape[0] - 9 * ch - 8, 128), F32)


def keep_half(tail, xc2, xc1, d2t, d1t, flat):
    return pl.pallas_call(
        keep_kernel,
        out_shape=jax.ShapeDtypeStruct((flat, 128), F32),
        in_specs=vmem(5),
        out_specs=vmem(1)[0],
        compiler_params=params(),
        cost_estimate=pl.CostEstimate(flops=1_000_000_000, bytes_accessed=1_000_000, transcendentals=0),
        name="keep",
    )(tail, xc2, xc1, d2t, d1t)


def corr_kernel(f1, f2, before, out, token, lines):
    lanes = GROUP * BLK
    inv_root = f1.shape[1] ** (-0.5)
    lane = lax.broadcasted_iota(jnp.int32, (PITCH, lanes), 1)
    gap = lax.broadcasted_iota(jnp.int32, (PITCH, lanes), 0) - lane % BLK
    own = lane // BLK
    token[...] = jnp.zeros(token.shape, F32)
    lines[WIN * WIN - 1 :] = jnp.zeros((128 - WIN * WIN + 1, lanes), F32)
    for g in range(f1.shape[0] // lanes):
        at = slice(g * GROUP * PITCH, (g * GROUP + GROWS) * PITCH)
        scores = lax.dot_general(
            f2[at], f1[g * lanes : (g + 1) * lanes], (((1,), (1,)), ((), ())),
            preferred_element_type=F32,
        )
        for a in range(WIN):
            pick = scores[a * PITCH : (a + 1) * PITCH]
            for yy in range(1, GROUP):
                pick = jnp.where(own == yy, scores[(a + yy) * PITCH : (a + yy + 1) * PITCH], pick)
            for d in range(WIN):
                line = jnp.sum(jnp.where(gap == d, pick, 0.0), axis=0, keepdims=True) * inv_root
                lines[a * WIN + d : a * WIN + d + 1] = line
        out[g * lanes : (g + 1) * lanes] = lines[...].T[:, : WIN * WIN].astype(BF)


def correlate(f1, f2, before):
    return pl.pallas_call(
        corr_kernel,
        out_shape=(jax.ShapeDtypeStruct((f1.shape[0], WIN * WIN), BF), jax.ShapeDtypeStruct((8, 128), F32)),
        in_specs=vmem(2) + [pl.BlockSpec(memory_space=pl.ANY)],
        out_specs=tuple(vmem(2)),
        scratch_shapes=[pltpu.VMEM((128, GROUP * BLK), F32)],
        compiler_params=params(),
        cost_estimate=pl.CostEstimate(flops=300_000_000, bytes_accessed=1_000_000, transcendentals=0),
        name="corr",
    )(f1, f2, before)


def sum_kernel(rows, parts, after, out):
    size = parts.shape[1]
    for s in range(0, size, 8):
        value = parts[0, s : s + 8].astype(F32)
        for n in range(1, parts.shape[0]):
            value = value + parts[n, s : s + 8].astype(F32)
        if s == rows % size:
            value = jnp.where(place(GROUP_AXES) == rows // size, bias_again(value), value)
        value = value.astype(BF)
        for k in range(out.shape[0]):
            out[k, s : s + 8] = value


def sum_and_copy(parts, copies, rows, after):
    return pl.pallas_call(
        functools.partial(sum_kernel, rows),
        out_shape=jax.ShapeDtypeStruct((copies,) + parts.shape[1:], BF),
        in_specs=vmem(2),
        out_specs=vmem(1)[0],
        compiler_params=params(),
        name="sum",
    )(parts, after)


def copies_kernel(rows, own, *refs):
    *got, after, out = refs
    size = own.shape[0]
    value = own[...].astype(F32)
    if len(got) == 1:
        value = value + got[0][...].astype(F32)
    else:
        value = (value + got[2][...].astype(F32)) + (got[0][...].astype(F32) + got[1][...].astype(F32))
    at = rows % size
    tail = value[at : at + 8]
    tail = jnp.where(place(GROUP_AXES) == rows // size, bias_again(tail), tail)
    value = jnp.concatenate([value[0:at], tail, value[at + 8 :]], axis=0).astype(BF)
    for k in range(out.shape[0]):
        out[k] = value


def add_and_copy(own, got, copies, rows, after):
    return pl.pallas_call(
        functools.partial(copies_kernel, rows),
        out_shape=jax.ShapeDtypeStruct((copies,) + own.shape, BF),
        in_specs=vmem(2 + len(got)),
        out_specs=vmem(1)[0],
        compiler_params=params(),
        name="copies",
    )(own, *got, after)


def merge_kernel(rows, kept, got, out):
    out[...] = (kept[...] + got[...].astype(F32)).astype(BF)
    tail = kept[rows : rows + 8] + got[rows : rows + 8].astype(F32)
    out[rows : rows + 8] = bias_again(tail).astype(BF)


def merge(kept, got, rows):
    return pl.pallas_call(
        functools.partial(merge_kernel, rows),
        out_shape=jax.ShapeDtypeStruct(got.shape, BF),
        in_specs=vmem(2),
        out_specs=vmem(1)[0],
        compiler_params=params(),
        name="merge",
    )(kept, got)


def unpack_half(which, part, held, grad, sems):
    ch = held.shape[1]
    first, rest = which * 6 * ch, 3 * ch + which * (3 * ch // 2) - 6 * 128
    copies = []
    for k in range(9):
        held[k * 128 : (k + 1) * 128] = part[k * ch : (k + 1) * ch].T.astype(F32)
        row = pl.multiple_of((first if k < 6 else rest) + k * 128, 128)
        copies.append(
            pltpu.make_async_copy(held.at[k * 128 : (k + 1) * 128], grad.at[pl.ds(row, 128)], sems.at[k])
        )
        copies[-1].start()
    return copies


def own_kernel(own, grad, held, sems):
    for copy in unpack_half(lax.axis_index("core"), own, held, grad, sems):
        copy.wait()


def other_kernel(own, other, grad_in, grad, bias, held, line, sems):
    core = lax.axis_index("core")
    ch = held.shape[1]
    rows = slice(9 * ch, 9 * ch + 8)
    first = jnp.where(core == 0, own[rows].astype(F32), other[rows].astype(F32))
    line[:, 0:128] = first[0:1] + first[2:3]
    line[:, 128:] = first[1:2] + first[3:4]
    copy = pltpu.make_async_copy(line, bias, sems.at[9])
    copy.start()
    for other_copy in unpack_half(1 - core, other, held, grad, sems):
        other_copy.wait()
    copy.wait()


def unpack(own, other, ch):
    grad = jax.ShapeDtypeStruct((9 * ch, ch), F32)
    held = pltpu.VMEM((9 * ch // 2, ch), F32)
    outside = [pl.BlockSpec(memory_space=pl.ANY)]
    part = pl.pallas_call(
        own_kernel,
        out_shape=grad,
        in_specs=vmem(1),
        out_specs=outside[0],
        scratch_shapes=[held, pltpu.SemaphoreType.DMA((9,))],
        compiler_params=params(),
        cost_estimate=pl.CostEstimate(flops=10_000_000, bytes_accessed=3_000_000, transcendentals=0),
        name="unpack_own",
    )(own)
    return pl.pallas_call(
        other_kernel,
        out_shape=(grad, jax.ShapeDtypeStruct((1, ch), F32)),
        in_specs=vmem(2) + outside,
        out_specs=tuple(outside * 2),
        scratch_shapes=[held, pltpu.VMEM((1, ch), F32), pltpu.SemaphoreType.DMA((10,))],
        input_output_aliases={2: 0},
        compiler_params=params(),
        name="unpack_other",
    )(own, other, part)


def shards(row_count, col_count, space, group, frames, offsets, weight, bias, cotangent):
    rows, cols, ch = frames.shape[2:]
    offs = offsets.reshape(-1, 2)
    *sent, kept = row_pieces(frames[0])
    got = swap(sent, "row", row_count)
    bt, b = band(cotangent[0])
    second, first, center, one = col_pieces(offs, kept, got)
    got = swap((first, second), space, col_count)
    taps, bias = weight.reshape(3, 3 * ch, ch), bias.reshape(1, ch)
    xc1, acc1 = convolve_one(one, taps, bias)
    count = int(np.prod([lax.axis_size(a) for a in group]))
    depth = lax.axis_size("zh")
    half = 9 * ch
    size = (half + 8 + 8 * count - 1) // (8 * count) * 8
    sent, tail, f1, f2, *rest = main(
        offs, center, xc1, acc1, got, taps, bias, bt, b, row_count, col_count, size * count
    )
    cores = [(0, 1), (1, 0)]
    got = lax.ppermute(sent, "core", cores)
    kept = keep_half(tail, *rest, size * count)
    parts = merge(kept, got, half)
    parts = lax.all_to_all(parts.reshape(count, size, 128), group, 0, 0, tiled=True)
    parts = sum_and_copy(parts, 1, half, tail).reshape(size, 128)
    corr, token = correlate(f1, f2, parts)
    hops = {2: (1,), 4: (2, 3, 1)}[depth]
    got = {h: lax.ppermute(parts, "zh", [(i, (i + h) % depth) for i in range(depth)]) for h in hops}
    parts = add_and_copy(parts, [got[h] for h in hops[::-1]], count, half, token)
    parts = lax.all_to_all(parts, group, 0, 0, tiled=True)
    parts = parts.reshape(count * size, 128)
    grad_w, grad_b = unpack(parts, lax.ppermute(parts, "core", cores), ch)
    corr = jnp.transpose(corr.reshape(1, rows, cols, WIN * WIN), (0, 3, 1, 2))
    return corr, grad_w.reshape(3, 3, ch, ch), grad_b.reshape(ch)


def solution(mesh):
    row_count, col_count, pair_count = (mesh.shape[a] for a in ("row", "col", "pair"))
    high = 2 if col_count == 16 else 1
    near = 2 if col_count // high >= 4 else 1
    fine = Mesh(
        mesh.devices.reshape(row_count, high, col_count // high // near, near, pair_count // 2, 2),
        ("row", "high", "zh", "zl", "low", "core"),
    )
    col, pair = SPACE, ("low", "core")
    return jax.shard_map(
        functools.partial(shards, row_count, col_count, col, GROUP_AXES),
        mesh=fine,
        in_specs=(
            P(pair, None, "row", col, None),
            P(pair, None, None, None),
            P(),
            P(),
            P(pair, None, "row", col),
        ),
        out_specs=(P(pair, None, "row", col), P(), P()),
        check_vma=False,
    )
```
